32 devices in a mesh: row: 8 (over z, x), col: 4 (over y, core).
Axes of the slice: x: 2, y: 2, z: 4, core: 2. Of those that a mesh axis runs over, the one named last changes fastest.
Arguments:
- fine_coeffs: float32 [512, 4096], P(('row', 'col')), may hold values from -6 to 6
- fine_slot: int32 [512], P(('row', 'col')), may hold values from 0 to 511, as said below
- neighbours: int32 [64, 6], P('row'), may hold values from -1 to 63, as said below
- filter_matrix: float32 [32, 32], replicated, may hold values from -1 to 1
- kernel_ops: float32 [20, 3, 3, 1024], replicated, may hold values from -0.625 to 0.625
Outputs:
- fine_result: float32 [512, 4096], P(('row', 'col'))
The draws below stay inside these ranges and needn't reach their ends.
Inputs may be any that keep to these rules, and one draw needn't show every extreme that they name: `fine_slot`: every value appears once. Run r holds the parents r * 8 to (r + 1) * 8 - 1. A fine box on a device with col index c has its parent in the c-th block of 2 consecutive parents of the parent's run. Of the 16 fine boxes of one device, at most 4 have parents in one run, and some device has exactly 4 in some run. -1 where the grid of parents ends. neighbours[neighbours[p, d], d XOR 1] = p. For a parent of run r, the neighbours in directions 0, 2, 4 lie in run (r + 1) mod 8 and those in directions 1, 3, 5 in run (r - 1) mod 8.
All inputs are finite; a program needn't handle non-finite values.
Results may differ from the reference program's by a relative error of at most 0.0001.
Values sent between devices are 32-bit elements; how exact they have to be, the bound alone decides.
No kernel may reach another device: no remote copies, remote signals or barrier semaphores. Data moves between devices by JAX's collectives and lax.ppermute only.
A program may use at most 64 MiB of HBM per device.

```python
import jax
import jax.numpy as jnp
import numpy as np
from jax import lax

K = 16
TERMS = 20
GRID_X = 4
GRID_Y = 2
BLOCK = 32
FINE_DEV = 16
PARENTS = 64
FINE = 512
GRID_Z = 8
N_ROW = 8
N_COL = 4


def draw_fine_slot(key, part):
    base_share = FINE_DEV // N_ROW
    couples = N_ROW // 2
    key_first, key_second, key_amount, key_child, key_place = jax.random.split(jax.random.fold_in(key, 11), 5)
    first_row = jax.random.randint(key_first, (couples, N_COL), 0, N_ROW)
    second_row = (first_row + jax.random.randint(key_second, (couples, N_COL), 1, N_ROW)) % N_ROW
    amount = jax.random.randint(key_amount, (couples, N_COL), 1, base_share + 1).at[0, 0].set(base_share)
    row_iota = jnp.arange(N_ROW)
    raised = (row_iota[None, None, :] == first_row[:, :, None]).astype(jnp.int32)
    lowered = (row_iota[None, None, :] == second_row[:, :, None]).astype(jnp.int32)
    change = amount[:, :, None] * (raised - lowered)
    counts = base_share + jnp.stack([change, -change], axis=1).reshape(N_ROW, N_COL, N_ROW)
    running = jnp.transpose(jnp.cumsum(counts, axis=0), (2, 1, 0))
    item_iota = jnp.arange(FINE_DEV)
    source_row = jnp.sum((running[:, :, None, :] <= item_iota[None, None, :, None]).astype(jnp.int32), axis=3)
    shuffles = jax.vmap(lambda subkey: jax.random.permutation(subkey, FINE_DEV))(jax.random.split(key_child, N_ROW * N_COL))
    handler = jnp.arange(N_ROW * N_COL).reshape(N_ROW, N_COL, 1)
    child_id = handler * FINE_DEV + shuffles.reshape(N_ROW, N_COL, FINE_DEV)
    source_device = source_row * N_COL + jnp.arange(N_COL)[None, :, None]
    sort_key = source_device.reshape(-1) * FINE + jax.random.permutation(key_place, FINE)
    return child_id.reshape(-1)[jnp.argsort(sort_key, stable=True)].astype(jnp.int32)


def draw_neighbours(key, part):
    layer_size = GRID_X * GRID_Y
    cell_iota = jnp.arange(PARENTS)
    along_x = cell_iota % GRID_X
    along_y = cell_iota // GRID_X % GRID_Y
    along_z = cell_iota // layer_size
    owner_row = (along_x + along_y + along_z) % N_ROW
    shuffle = jax.random.permutation(jax.random.fold_in(key, 23), PARENTS)
    ranking = jnp.argsort(owner_row * PARENTS + shuffle, stable=True)
    parent_of = jnp.zeros((PARENTS,), jnp.int32).at[ranking].set(cell_iota.astype(jnp.int32))
    stepping = [(along_x < GRID_X - 1, 1), (along_x > 0, -1), (along_y < GRID_Y - 1, GRID_X), (along_y > 0, -GRID_X), (along_z < GRID_Z - 1, layer_size), (along_z > 0, -layer_size)]
    columns = [jnp.where(inside, parent_of[jnp.clip(cell_iota + stride, 0, PARENTS - 1)], -1) for inside, stride in stepping]
    return jnp.zeros((PARENTS, 6), jnp.int32).at[parent_of].set(jnp.stack(columns, axis=1).astype(jnp.int32))


def levels(own_key, dims, shards, least, high):
    factor_of = 1.0
    for axis_at, blocks in shards:
        heights = jax.random.uniform(jax.random.fold_in(jax.random.fold_in(own_key, 6), axis_at), (blocks,), jnp.float32, least / len(shards), high / len(shards))
        factor_of = factor_of * jnp.repeat(jnp.exp(heights), dims[axis_at] // blocks).reshape((-1,) + (1,) * (len(dims) - 1 - axis_at))
    return factor_of


def scatter_about(stream_key, extent, width, bound, cuts=(), kind=jnp.bfloat16):
    values = jax.random.normal(stream_key, extent, jnp.float32) * width
    if len(cuts) > 0:
        values = levels(stream_key, extent, cuts, -0.22, 0.18) * values
    return jnp.clip(values, min=-bound, max=bound).astype(kind)


def setup_inputs(seed: int = 0) -> dict:
    seeds = jax.random.split(jax.random.key(seed), 6)
    fine_coeffs = scatter_about(seeds[0], (FINE, K ** 3), 1.0, 6.0, ((0, 32),), jnp.float32)
    fine_slot = draw_fine_slot(jax.random.fold_in(seeds[5], 71), 0)
    neighbours = draw_neighbours(jax.random.fold_in(seeds[5], 71), 0)
    filter_matrix = scatter_about(seeds[3], (BLOCK, BLOCK), BLOCK ** -0.5, 1.0, (), jnp.float32)
    kernel_ops = scatter_about(seeds[4], (TERMS, 3, 3, BLOCK * BLOCK), (3 * BLOCK) ** -0.5, 0.625, (), jnp.float32)
    return dict(fine_coeffs=fine_coeffs, fine_slot=fine_slot, neighbours=neighbours, filter_matrix=filter_matrix, kernel_ops=kernel_ops)


exact_mode = lax.Precision.HIGHEST
offset_order = np.array([1, 2, 0])


def rotate_batch(blocks, matrices):
    breadth = matrices.shape[-1]
    viewed = blocks.reshape(blocks.shape[:2] + (-1, breadth))
    result = jnp.einsum('ekc,enmc->enkm', matrices, viewed, precision=exact_mode)
    return result.reshape(blocks.shape[:2] + (-1,))


def rotate_single(blocks, matrix):
    breadth = matrix.shape[-1]
    viewed = blocks.reshape(blocks.shape[:-1] + (-1, breadth))
    result = jnp.einsum('kc,...mc->...km', matrix, viewed, precision=exact_mode)
    return result.reshape(blocks.shape[:-1] + (-1,))


def rotate_many(blocks, matrices):
    breadth = matrices.shape[-1]
    viewed = blocks.reshape(blocks.shape[:1] + (-1, breadth))
    result = jnp.einsum('ekc,nmc->enkm', matrices, viewed, precision=exact_mode)
    return result.reshape((matrices.shape[0], blocks.shape[0], -1))


def octant_tables(pieces):
    octants = np.arange(8)
    return pieces[octants % 2], pieces[(octants // 2) % 2], pieces[octants // 4]


def filter_children(children, filter_matrix):
    breadth = filter_matrix.shape[0]
    pieces = jnp.transpose(filter_matrix.reshape(breadth, 2, breadth // 2), (1, 0, 2))
    along_z, along_y, along_x = octant_tables(pieces)
    sectioned = rotate_batch(children, along_z)
    sectioned = rotate_batch(sectioned, along_y)
    sectioned = rotate_batch(sectioned, along_x)
    return jnp.sum(sectioned, axis=0)


def unfilter_blocks(applied, filter_matrix):
    breadth = filter_matrix.shape[0]
    pieces = jnp.transpose(filter_matrix.reshape(breadth, 2, breadth // 2), (1, 2, 0))
    along_z, along_y, along_x = octant_tables(pieces)
    sectioned = rotate_many(applied, along_z)
    sectioned = rotate_batch(sectioned, along_y)
    return rotate_batch(sectioned, along_x)


def displaced(filtered, kernel_ops):
    amount = filtered.shape[0]
    volume = filtered.shape[1]

    def one_term(totals, factors):
        first_section = rotate_many(filtered, factors[2])
        mid_centre = rotate_many(first_section[1], factors[1][offset_order])
        mid_sides = rotate_single(first_section[np.array([2, 0])], factors[1, 1])
        last_centre = rotate_many(mid_centre[0], factors[0][offset_order])
        last_mid = rotate_single(mid_centre[1:], factors[0, 1])
        last_sides = rotate_single(mid_sides, factors[0, 1])
        return (totals[0] + last_centre, totals[1] + last_mid, totals[2] + last_sides), None

    initial = (jnp.zeros((3, amount, volume), jnp.float32), jnp.zeros((2, amount, volume), jnp.float32), jnp.zeros((2, amount, volume), jnp.float32))
    totals, unused = lax.scan(one_term, initial, kernel_ops)
    return totals


def regroup(stacked, parents, volume):
    return jnp.transpose(stacked, (1, 0, 2, 3)).reshape(stacked.shape[1], parents, volume)


def reference(fine_coeffs, fine_slot, neighbours, filter_matrix, kernel_ops):
    breadth = filter_matrix.shape[0]
    factor_set = kernel_ops.reshape(kernel_ops.shape[:3] + (breadth, breadth))
    parents = neighbours.shape[0]
    volume = fine_coeffs.shape[1]
    ordered = jnp.zeros((parents * 8, volume), jnp.float32).at[fine_slot].set(fine_coeffs)
    children = jnp.transpose(ordered.reshape(parents, 8, volume), (1, 0, 2))
    filtered = filter_children(children, filter_matrix)
    grouped = filtered.reshape(parents // 16, 16, -1)
    centre, middle, side_terms = lax.map(lambda group: displaced(group, factor_set), grouped)
    big_volume = filtered.shape[1]
    centre = regroup(centre, parents, big_volume)
    middle = regroup(middle, parents, big_volume)
    side_terms = regroup(side_terms, parents, big_volume)
    by_direction = [centre[1], centre[2], middle[0], middle[1], side_terms[0], side_terms[1]]
    applied = centre[0]
    for direction in range(6):
        source = neighbours[:, direction ^ 1]
        picked = by_direction[direction][jnp.clip(source, 0, parents - 1)]
        applied = applied + jnp.where((source >= 0)[:, None], picked, 0.0)
    unfiltered = lax.map(lambda group: unfilter_blocks(group, filter_matrix), applied.reshape(parents // 16, 16, -1))
    unfiltered = jnp.transpose(unfiltered, (0, 2, 1, 3)).reshape(parents * 8, volume)
    return unfiltered[fine_slot]
```

```python
import functools

import jax
import jax.numpy as jnp
import numpy as np
from jax import lax
from jax.experimental import pallas as pl
from jax.experimental.pallas import tpu as pltpu
from jax.sharding import PartitionSpec as P

F32, BF16 = jnp.float32, jnp.bfloat16


def split_host(x):
    high = lax.reduce_precision(x, 8, 7)
    return high.astype(BF16), (x - high).astype(BF16)


def split_kernel(x):
    high = x.astype(BF16)
    return high, (x - high.astype(F32)).astype(BF16)


def triple(x, axis):
    high, low = split_host(x)
    return jnp.concatenate([high, high, low], axis=axis)


def apply_weights(factor_set, groups):
    terms, breadth = factor_set.shape[0], factor_set.shape[-1]
    lo_count = 128 // breadth
    hi_count = breadth // lo_count
    first = jnp.concatenate([triple(factor_set[:, 0, k].reshape(terms * breadth, breadth), 1) for k in (1, 2, 0)], axis=1)
    turned = jnp.tile(jnp.transpose(factor_set[:, 2], (0, 1, 3, 2)), (1, 1, 1, lo_count))
    second_high, second_low = split_host(turned)
    per = terms // groups
    third = factor_set[:, 1][:, np.array([1, 2, 0])].reshape(groups, per, 3, breadth, hi_count, lo_count)
    third = jnp.transpose(third, (0, 5, 3, 2, 1, 4)).reshape(groups, lo_count * breadth, 3, per * hi_count)
    third = triple(third, 3).reshape(groups, lo_count * breadth, -1)
    return first, second_high, second_low, third


def apply_kernel(where, own, *refs, parts, groups):
    sides = refs[: 2 * parts]
    first, second_high, second_low, third, out = refs[2 * parts : 2 * parts + 5]
    vols, xbuf, ubuf, lbuf, tbuf, rbuf, obuf, sems = refs[2 * parts + 5 :]
    count, breadth, width = own.shape
    lo_count = 128 // breadth
    hi_count = breadth // lo_count
    rows = first.shape[0]
    per = rows // breadth
    kgroup = per * hi_count
    group = pl.program_id(0)

    def copies(action):
        for n in range(count):
            for side in range(2):
                for axis in range(3):
                    slot = (n * 2 + side) * 3 + axis
                    at = where[n, side * 3 + axis]
                    target = vols.at[slot]
                    start = 0
                    for part in range(parts):
                        source = sides[side * parts + part]
                        size = source.shape[0]

                        @pl.when((at >= start) & (at < start + size))
                        def _(source=source, start=start):
                            action(pltpu.make_async_copy(source.at[at - start], target, sems.at[slot]))

                        start += size

    @pl.when(group == 0)
    def _():
        for n in range(count):
            for side in range(2):
                for axis in range(3):
                    slot = (n * 2 + side) * 3 + axis

                    @pl.when(where[n, side * 3 + axis] < 0)
                    def _(slot=slot):
                        vols[slot] = jnp.zeros((breadth, width), F32)

        copies(lambda c: c.start())
        tbuf[...] = jnp.zeros(tbuf.shape, BF16)
        obuf[...] = jnp.zeros(obuf.shape, F32)
        copies(lambda c: c.wait())

    for n in range(count):
        def fill(row, block):
            high, low = split_kernel(block)
            xbuf[row : row + breadth] = high
            xbuf[row + breadth : row + 2 * breadth] = low
            xbuf[row + 2 * breadth : row + 3 * breadth] = high

        def place(g, result):
            for h in range(hi_count):
                ubuf[g, n, h] = result[:, h * 128 : (h + 1) * 128]

        fill(0, own[n])
        fill(3 * breadth, vols[(n * 2 + 0) * 3])
        fill(6 * breadth, vols[(n * 2 + 1) * 3])
        place(0, jnp.dot(first[...], xbuf[...], preferred_element_type=F32))
        for g, (side, axis) in enumerate([(0, 2), (1, 2), (0, 1), (1, 1)]):
            fill(0, vols[(n * 2 + side) * 3 + axis])
            place(g + 1, jnp.dot(first[:, : 3 * breadth], xbuf[: 3 * breadth], preferred_element_type=F32))

    flat = ubuf.reshape(5 * count * hi_count * rows, 128)
    block_mask = (
        lax.broadcasted_iota(jnp.int32, (128, 128), 0) // breadth
        == lax.broadcasted_iota(jnp.int32, (128, 128), 1) // breadth
    )
    zero_block = jnp.zeros((128, 128), BF16)

    def pair_body(pair, carry):
        for k in range(3):
            for half in range(2):
                term = pair * 2 + half
                high = jnp.concatenate([second_high[term, k]] * lo_count, axis=0)
                low = jnp.concatenate([second_low[term, k]] * lo_count, axis=0)
                high = jnp.where(block_mask, high, zero_block)
                low = jnp.where(block_mask, low, zero_block)
                tbuf[half, k, :128, :128] = high
                tbuf[half, k, 128:, :128] = high
                tbuf[half, k, :128, 128:] = low
        for n in range(count):
            for half in range(2):
                term = pair * 2 + half
                for g in range(5):
                    base = (g * count + n) * hi_count * rows + term * breadth
                    for a in range(0, breadth, 2):
                        pieces = [flat[pl.ds(base + a + d, hi_count, stride=rows), :] for d in range(2)]
                        high, low = split_kernel(jnp.concatenate(pieces, axis=0))
                        at = a * hi_count
                        lbuf[half, g, at : at + 2 * hi_count, :128] = high
                        lbuf[half, g, at : at + 2 * hi_count, 128:] = low

            def mixed(half, g, k):
                return jnp.dot(lbuf[half, g], tbuf[half, k], preferred_element_type=F32)

            def folded(wide):
                return wide[:, :128] + wide[:, 128:]

            results = []
            for half in range(2):
                centre = folded(mixed(half, 0, 1) + mixed(half, 1, 2) + mixed(half, 2, 0))
                results.append((centre, folded(mixed(half, 3, 1)), folded(mixed(half, 4, 1))))
            for q in range(3):
                for a in range(breadth):
                    both = jnp.concatenate([results[half][q][a * hi_count : (a + 1) * hi_count] for half in range(2)], axis=0)
                    high, low = split_kernel(both)
                    tile = (n * breadth + a) // 2
                    lane = (a % 2) * 128
                    step = 2 * hi_count
                    row = pl.multiple_of(q * 3 * kgroup + pair * step, step)
                    rbuf[tile, pl.ds(row, step), lane : lane + 128] = high
                    rbuf[tile, pl.ds(row + kgroup, step), lane : lane + 128] = low
                    rbuf[tile, pl.ds(row + 2 * kgroup, step), lane : lane + 128] = high
        return carry

    lax.fori_loop(0, per // 2, pair_body, 0)

    lane_block = lax.broadcasted_iota(jnp.int32, (breadth, 256), 1) % 128 // breadth

    def tile_body(tile, carry):
        wide = jnp.dot(third[0], rbuf[tile], preferred_element_type=F32)
        total = wide[:breadth]
        for low in range(1, lo_count):
            total = jnp.where(lane_block == low, wide[low * breadth : (low + 1) * breadth], total)
        for d in range(2):
            row = pl.multiple_of((tile * 2 + d) * breadth, breadth)
            obuf[pl.ds(row, breadth), :] = obuf[pl.ds(row, breadth), :] + total[:, d * 128 : (d + 1) * 128]
        return carry

    lax.fori_loop(0, count * breadth // 2, tile_body, 0)

    @pl.when(group == groups - 1)
    def _():
        lane_of = lax.broadcasted_iota(jnp.int32, (8, 128), 1) // breadth
        for n in range(count):
            for a in range(0, breadth, 8):
                for high in range(hi_count):
                    total = None
                    for low in range(lo_count):
                        b = high * lo_count + low
                        piece = obuf[pl.ds((n * breadth + a) * breadth + b, 8, stride=breadth), :]
                        shift = 64
                        while shift >= breadth:
                            piece = piece + pltpu.roll(piece, shift, 1)
                            shift //= 2
                        total = piece if total is None else jnp.where(lane_of == low, piece, total)
                    out[n, a : a + 8, high * 128 : (high + 1) * 128] = total


def apply_call(where, own, below, above, weights, groups):
    first, second_high, second_low, third = weights
    count, breadth, width = own.shape
    lo_count = 128 // breadth
    hi_count = breadth // lo_count
    rows = first.shape[0] // groups
    per = rows // breadth
    parts = len(below)
    tiles = count * breadth // 2
    anywhere = pl.BlockSpec(memory_space=pl.ANY)
    return pl.pallas_call(
        functools.partial(apply_kernel, parts=parts, groups=groups),
        out_shape=jax.ShapeDtypeStruct(own.shape, F32),
        grid_spec=pltpu.PrefetchScalarGridSpec(
            num_scalar_prefetch=1,
            grid=(groups,),
            in_specs=[pl.BlockSpec(own.shape, lambda g, w: (0, 0, 0))]
            + [anywhere] * (2 * parts)
            + [
                pl.BlockSpec((rows, first.shape[1]), lambda g, w: (g, 0)),
                pl.BlockSpec((per,) + second_high.shape[1:], lambda g, w: (g, 0, 0, 0)),
                pl.BlockSpec((per,) + second_low.shape[1:], lambda g, w: (g, 0, 0, 0)),
                pl.BlockSpec((1,) + third.shape[1:], lambda g, w: (g, 0, 0)),
            ],
            out_specs=pl.BlockSpec(own.shape, lambda g, w: (0, 0, 0)),
            scratch_shapes=[
                pltpu.VMEM((count * 6, breadth, width), F32),
                pltpu.VMEM((9 * breadth, width), BF16),
                pltpu.VMEM((5, count, hi_count, rows, 128), F32),
                pltpu.VMEM((2, 5, breadth * hi_count, 256), BF16),
                pltpu.VMEM((2, 3, 256, 256), BF16),
                pltpu.VMEM((tiles, third.shape[2], 256), BF16),
                pltpu.VMEM((count * breadth * breadth, 128), F32),
                pltpu.SemaphoreType.DMA((count * 6,)),
            ],
        ),
        compiler_params=pltpu.CompilerParams(dimension_semantics=("arbitrary",), vmem_limit_bytes=60 << 20),
        name="apply",
    )(where, own, *below, *above, first, second_high, second_low, third)


def iota(shape, axis):
    return lax.broadcasted_iota(jnp.int32, shape, axis)


def to_row(column):
    size = column.shape[0]
    diagonal = iota((size, size), 0) == iota((size, size), 1)
    return jnp.sum(jnp.where(diagonal, column, 0.0), axis=0, keepdims=True)


def to_column(row):
    size = row.shape[1]
    diagonal = iota((size, size), 0) == iota((size, size), 1)
    return jnp.sum(jnp.where(diagonal, row, 0.0), axis=1, keepdims=True)


def run_of(slots, runs, run_size):
    run = jnp.zeros(slots.shape, F32)
    for r in range(1, runs):
        run = run + jnp.where(slots >= r * run_size, 1.0, 0.0)
    return run


def place_row(slot_row, runs, run_size, capacity):
    held = slot_row.shape[1]
    run_row = run_of(slot_row, runs, run_size)
    same = to_column(run_row) == run_row
    earlier = iota((held, held), 0) < iota((held, held), 1)
    before = jnp.sum(jnp.where(same & earlier, 1.0, 0.0), axis=0, keepdims=True)
    return run_row * capacity + before


def pack_kernel(slot_row, fine, out, stack, *, runs, run_size, capacity):
    held, volume = fine.shape
    places = runs * capacity
    slots = slot_row[...]
    place = place_row(slots, runs, run_size, capacity)
    hit = iota((places, held), 0).astype(F32) == place
    ids = jnp.sum(jnp.where(hit, slots.astype(F32) + 1.0, 0.0), axis=1, keepdims=True)
    out[:, volume:] = jnp.broadcast_to(ids, (places, 128))
    one = jnp.where(hit, 1.0, 0.0).astype(BF16)
    rest = fine[...]
    for part in range(3):
        head = rest.astype(BF16)
        stack[part * held : (part + 1) * held] = head
        rest = rest - head.astype(F32)
    out[:, :volume] = jnp.dot(jnp.concatenate([one] * 3, axis=1), stack[...], preferred_element_type=F32)


def unpack_kernel(slot_row, back, out, stack, *, runs, run_size, capacity):
    held, volume = out.shape
    places = runs * capacity
    place = to_column(place_row(slot_row[...], runs, run_size, capacity))
    hit = iota((held, places), 1).astype(F32) == place
    one = jnp.where(hit, 1.0, 0.0).astype(BF16)
    rest = back[...]
    for part in range(3):
        head = rest.astype(BF16)
        stack[part * places : (part + 1) * places] = head
        rest = rest - head.astype(F32)
    out[...] = jnp.dot(jnp.concatenate([one] * 3, axis=1), stack[...], preferred_element_type=F32)


def child_code(ids, held):
    at = ids - 1.0
    return jnp.where(at < 0.0, -1.0, at - held * jnp.floor(at / held))


def row_code(index, count):
    inner = index & 7
    code = (inner >> 1) * 8 + (inner & 1) * 4 + (index >> 3)
    return jnp.where(inner < 2 * count, code.astype(F32), -2.0)


def filter_kernel(got, across_z, across_y, rows, out, stack, lines, cross, weave, *, count):
    places = got.shape[0]
    width = out.shape[1]
    volume = got.shape[1] - 128
    face = width // 4
    span = volume // face
    held = 8 * count
    code = to_row(child_code(got[:, volume : volume + 1], held))
    hit = row_code(iota((32, places), 0), count) == code
    one = jnp.where(hit, 1.0, 0.0).astype(BF16)
    high, low = split_kernel(got[:, :volume])
    stack[:places] = high
    stack[places:] = low
    boxes = jnp.dot(jnp.concatenate([one, one], axis=1), stack[...], preferred_element_type=F32)
    for g in range(4):
        for i in range(0, span, 2):
            both = jnp.concatenate([boxes[g * 8 : g * 8 + 8, (i + d) * face : (i + d + 1) * face] for d in range(2)], axis=0)
            high, low = split_kernel(both)
            lines[0, i * 8 : i * 8 + 16, g * face : (g + 1) * face] = high
            lines[1, i * 8 : i * 8 + 16, g * face : (g + 1) * face] = low
    half = across_z.shape[0] // 2
    for g in range(4):
        zs = across_z[(g & 1) * half : (g & 1) * half + half]
        for j in range(half):
            row = (g >> 1) * half + j
            high, low = split_kernel(zs * across_y[row : row + 1])
            at = (g * half + j) * half
            cross[0, at : at + half] = high
            cross[1, at : at + half] = low
    total = jnp.dot(lines[0], cross[0], preferred_element_type=F32)
    total = total + jnp.dot(lines[1], cross[0], preferred_element_type=F32)
    total = total + jnp.dot(lines[0], cross[1], preferred_element_type=F32)
    high, low = split_kernel(total)
    size = total.shape[0]
    weave[:size] = high
    weave[size : 2 * size] = low
    weave[2 * size :] = high
    out[...] = jnp.dot(rows[...], weave[...], preferred_element_type=F32)


def unfilter_kernel(applied, ids, across_c, across_b, rows, out, weave, cross, stack, *, count):
    places = out.shape[0]
    size, width = applied.shape
    breadth = across_c.shape[0]
    face = width // 4
    held = 8 * count
    high, low = split_kernel(applied[...])
    weave[:size] = high
    weave[size : 2 * size] = low
    weave[2 * size :] = high
    lines = jnp.dot(rows[...], weave[...], preferred_element_type=F32)
    for b in range(breadth):
        high, low = split_kernel(across_c[...] * across_b[b : b + 1])
        cross[0, b * breadth : (b + 1) * breadth] = high
        cross[1, b * breadth : (b + 1) * breadth] = low
    high, low = split_kernel(lines)
    total = jnp.dot(high, cross[0], preferred_element_type=F32)
    total = total + jnp.dot(low, cross[0], preferred_element_type=F32)
    total = total + jnp.dot(high, cross[1], preferred_element_type=F32)
    for g in range(0, 4, 2):
        for i in range(total.shape[0] // 8):
            both = jnp.concatenate([total[i * 8 : i * 8 + 8, (g + d) * face : (g + d + 1) * face] for d in range(2)], axis=0)
            high, low = split_kernel(both)
            stack[g * 8 : g * 8 + 16, i * face : (i + 1) * face] = high
            stack[32 + g * 8 : 32 + g * 8 + 16, i * face : (i + 1) * face] = low
    code = child_code(ids[:, :1], held)
    hit = row_code(iota((places, 32), 1), count) == code
    one = jnp.where(hit, 1.0, 0.0).astype(BF16)
    out[...] = jnp.dot(jnp.concatenate([one, one], axis=1), stack[...], preferred_element_type=F32)


def shifted(array, axis, by):
    peers = lax.axis_size(axis)
    return lax.ppermute(array, axis, [(i, (i + by) % peers) for i in range(peers)])


def swapped(array, axis, bit):
    peers = lax.axis_size(axis)
    return lax.ppermute(array, axis, [(i, i ^ bit) for i in range(peers)])


def vmem_call(kernel, out_shape, scratch, name, **settings):
    return pl.pallas_call(
        functools.partial(kernel, **settings),
        out_shape=jax.ShapeDtypeStruct(out_shape, F32),
        scratch_shapes=[pltpu.VMEM(shape, dtype) for shape, dtype in scratch],
        compiler_params=pltpu.CompilerParams(vmem_limit_bytes=60 << 20),
        name=name,
    )


def local(fine_coeffs, fine_slot, neighbours, filter_matrix, kernel_ops):
    breadth = filter_matrix.shape[0]
    half = breadth // 2
    factor_set = kernel_ops.reshape(kernel_ops.shape[:3] + (breadth, breadth))
    runs = lax.axis_size("row")
    cols = lax.axis_size("col")
    held, volume = fine_coeffs.shape
    par_row = neighbours.shape[0]
    count = held // 8
    capacity = 2 * (held // runs)
    places = runs * capacity
    width = breadth * breadth
    routing = dict(runs=runs, run_size=8 * par_row, capacity=capacity)
    groups = 2

    slot_row = fine_slot.reshape(1, held)
    sent = vmem_call(pack_kernel, (places, volume + 128), [((3 * held, volume), BF16)], "pack", **routing)(slot_row, fine_coeffs)
    got = lax.all_to_all(sent, "row", split_axis=0, concat_axis=0, tiled=True)

    turned = filter_matrix.T
    across_z = jnp.tile(turned, (1, breadth))
    across_y = jnp.repeat(turned, breadth, axis=1)
    tall = filter_matrix.reshape(breadth, 2, half)
    same = np.eye(count, dtype=np.float32)
    mix = jnp.einsum("nm,aoi->naimo", same, tall, precision=lax.Precision.HIGHEST).reshape(count * breadth, half, 2 * count)
    mix = jnp.pad(mix, ((0, 0), (0, 0), (0, 8 - 2 * count))).reshape(count * breadth, half * 8)
    filtered = vmem_call(
        filter_kernel,
        (count * breadth, width),
        [
            ((2 * places, volume), BF16),
            ((2, half * 8, width), BF16),
            ((2, width, width), BF16),
            ((3 * half * 8, width), BF16),
        ],
        "filter",
        count=count,
    )(got, across_z, across_y, triple(mix, 1)).reshape(count, breadth, width)

    col_index = lax.axis_index("col")
    bits = [1 << k for k in reversed(range(cols.bit_length() - 1))]
    below = [shifted(filtered, "row", 1)]
    above = [shifted(filtered, "row", -1)]
    for bit in bits:
        below = below + [swapped(part, "col", bit) for part in below]
        above = above + [swapped(part, "col", bit) for part in above]
    mine = lax.dynamic_slice_in_dim(neighbours, col_index * count, count, 0)
    within = mine % par_row
    relation = (within // count) ^ col_index
    part = jnp.zeros_like(relation)
    for order, bit in enumerate(bits):
        part = part + ((relation // bit) % 2) * (1 << order)
    at = jnp.where(mine >= 0, part * count + within % count, -1)
    where = jnp.concatenate([at[:, 1::2], at[:, 0::2]], axis=1)
    weights = apply_weights(factor_set, groups)
    applied = apply_call(where, filtered, below, above, weights, groups).reshape(count * breadth, width)

    across_c = jnp.broadcast_to(filter_matrix.reshape(breadth, 1, 2, 1, half), (breadth, 2, 2, half, half)).reshape(breadth, width)
    across_b = jnp.broadcast_to(filter_matrix.reshape(breadth, 2, 1, half, 1), (breadth, 2, 2, half, half)).reshape(breadth, width)
    results = vmem_call(
        unfilter_kernel,
        (places, volume),
        [
            ((3 * count * breadth, width), BF16),
            ((2, width, width), BF16),
            ((64, volume), BF16),
        ],
        "unfilter",
        count=count,
    )(applied, got[:, volume:], across_c, across_b, triple(mix.T, 1))
    back = lax.all_to_all(results, "row", split_axis=0, concat_axis=0, tiled=True)
    return vmem_call(unpack_kernel, (held, volume), [((3 * places, volume), BF16)], "unpack", **routing)(slot_row, back)


def solution(mesh):
    in_specs = (P(("row", "col"), None), P(("row", "col")), P("row", None), P(), P())
    out_specs = P(("row", "col"), None)
    return jax.shard_map(local, mesh=mesh, in_specs=in_specs, out_specs=out_specs, check_vma=False)
```

```python
import functools

import jax
import jax.numpy as jnp
import numpy as np
from jax import lax
from jax.experimental import pallas as pl
from jax.experimental.pallas import tpu as pltpu
from jax.sharding import PartitionSpec as P

F32, BF16 = jnp.float32, jnp.bfloat16
LANES = 128
PAD = 8


def iota(shape, axis):
    return lax.broadcasted_iota(jnp.int32, shape, axis)


def split(x):
    high = x.astype(BF16)
    return high, (x - high.astype(F32)).astype(BF16)


def product(a, b):
    return jnp.dot(a, b, preferred_element_type=F32)


def exact_expand(x, hot):
    one = jnp.where(hot, 1.0, 0.0).astype(BF16)
    total = None
    for part in range(3):
        head = x.astype(BF16)
        piece = product(head, one)
        total = piece if total is None else total + piece
        x = x - head.astype(F32)
    return total


def prepare_kernel(ops, first, second_high, second_low, merge, spread, *, groups):
    breadth = ops.shape[1]
    terms = ops.shape[0] // (9 * breadth)
    lo_count = LANES // breadth
    hi_count = breadth // lo_count
    per = terms // groups

    def factor(term, axis, k):
        at = ((term * 3 + axis) * 3 + k) * breadth
        return ops[at : at + breadth]

    blank = jnp.zeros((breadth, LANES - 3 * breadth), F32)
    for term in range(terms):
        for k in range(3):
            value = factor(term, 0, k)
            high = value.astype(BF16).astype(F32)
            line = jnp.concatenate([high, high, value - high, blank], axis=1)
            first[term * breadth : (term + 1) * breadth, k * LANES : (k + 1) * LANES] = line.astype(BF16)
        at = (term * 9 + 6) * breadth
        turned = ops[at : at + 3 * breadth].T
        for k in range(3):
            high, low = split(jnp.concatenate([turned[:, k * breadth : (k + 1) * breadth]] * lo_count, axis=1))
            second_high[term, k] = high
            second_low[term, k] = low
    for g in range(groups):
        for inner in range(lo_count):
            strip = [
                jnp.concatenate(
                    [factor(g * per + t, 1, k)[:, inner * hi_count : (inner + 1) * hi_count] for t in range(per)], axis=1
                )
                for k in range(3)
            ]
            high, low = split(jnp.concatenate([strip[1], strip[0]], axis=1))
            merge[g, inner * breadth : (inner + 1) * breadth] = high
            merge[g, LANES + inner * breadth : LANES + (inner + 1) * breadth] = low
            for s, k in enumerate((1, 2)):
                high = strip[k].astype(BF16).astype(F32)
                line = jnp.concatenate([high, high, strip[k] - high], axis=1)
                spread[g, s, inner * breadth : (inner + 1) * breadth] = line.astype(BF16)


def fill(xbuf, slot, block):
    breadth = block.shape[0]
    high, low = split(block)
    base = slot * LANES
    xbuf[base : base + breadth] = high
    xbuf[base + breadth : base + 2 * breadth] = low
    xbuf[base + 2 * breadth : base + 3 * breadth] = high


def place(ubuf, g, n, result):
    rows = result.shape[0]
    for h in range(result.shape[1] // LANES):
        ubuf[g, n, h, :rows] = result[:, h * LANES : (h + 1) * LANES]


def second_stage(ubuf, lbuf, tbuf, second_high, second_low, per, breadth, offsets, recipes, emit):
    volumes, count, hi_count, stride = ubuf.shape[:4]
    lo_count = LANES // breadth
    flat = ubuf.reshape(volumes * count * hi_count * stride, LANES)
    block_mask = iota((LANES, LANES), 0) // breadth == iota((LANES, LANES), 1) // breadth
    zero_block = jnp.zeros((LANES, LANES), BF16)

    def pair_body(pair, carry):
        for spot, k in enumerate(offsets):
            for half in range(2):
                term = pair * 2 + half
                high = jnp.concatenate([second_high[term, k]] * lo_count, axis=0)
                low = jnp.concatenate([second_low[term, k]] * lo_count, axis=0)
                high = jnp.where(block_mask, high, zero_block)
                low = jnp.where(block_mask, low, zero_block)
                tbuf[half, spot, :LANES, :LANES] = high
                tbuf[half, spot, LANES:, :LANES] = high
                tbuf[half, spot, :LANES, LANES:] = low
        for n in range(count):
            for half in range(2):
                term = pair * 2 + half
                for g in range(volumes):
                    base = (g * count + n) * hi_count * stride + term * breadth
                    for a in range(0, breadth, 2):
                        pieces = [flat[pl.ds(base + a + d, hi_count, stride=stride), :] for d in range(2)]
                        high, low = split(jnp.concatenate(pieces, axis=0))
                        at = a * hi_count
                        lbuf[half, g, at : at + 2 * hi_count, :LANES] = high
                        lbuf[half, g, at : at + 2 * hi_count, LANES:] = low
            results = []
            for half in range(2):
                line = []
                for recipe in recipes:
                    wide = None
                    for g, spot in recipe:
                        piece = product(lbuf[half, g], tbuf[half, spot])
                        wide = piece if wide is None else wide + piece
                    line.append(wide[:, :LANES] + wide[:, LANES:])
                results.append(line)
            for q in range(len(recipes)):
                for a in range(breadth):
                    both = jnp.concatenate(
                        [results[half][q][a * hi_count : (a + 1) * hi_count] for half in range(2)], axis=0
                    )
                    high, low = split(both)
                    emit(q, pair, (n * breadth + a) // 2, (a % 2) * LANES, high, low)
        return carry

    lax.fori_loop(0, per // 2, pair_body, 0)


def pick_diagonal(wide, breadth):
    lane_block = iota((breadth, wide.shape[1]), 1) % LANES // breadth
    total = wide[:breadth]
    for low in range(1, LANES // breadth):
        total = jnp.where(lane_block == low, wide[low * breadth : (low + 1) * breadth], total)
    return total


def turn_block(obuf, base, breadth, store):
    lo_count = LANES // breadth
    lane_of = iota((8, LANES), 1) // breadth
    for a in range(0, breadth, 8):
        for high in range(breadth // lo_count):
            total = None
            for low in range(lo_count):
                b = high * lo_count + low
                piece = obuf[pl.ds(base + a * breadth + b, 8, stride=breadth), :]
                shift = LANES // 2
                while shift >= breadth:
                    piece = piece + pltpu.roll(piece, shift, 1)
                    shift //= 2
                total = piece if total is None else jnp.where(lane_of == low, piece, total)
            store(a, high * LANES, total)


def merge_kernel(where, own, *refs, parts):
    sources = refs[:parts]
    first, second_high, second_low, third, out = refs[parts : parts + 5]
    vols, xbuf, ubuf, lbuf, tbuf, rbuf, obuf, sems = refs[parts + 5 :]
    count, breadth, width = own.shape
    per = first.shape[0] // breadth
    kgroup = per * breadth * breadth // LANES

    def copies(action):
        for n in range(count):
            for axis in range(3):
                slot = n * 3 + axis
                at = where[n, axis]
                start = 0
                for source in sources:
                    size = source.shape[0]

                    @pl.when((at >= start) & (at < start + size))
                    def _(source=source, start=start, slot=slot, at=at):
                        action(pltpu.make_async_copy(source.at[at - start], vols.at[slot], sems.at[slot]))

                    start += size

    copies(lambda c: c.start())
    for n in range(count):
        for axis in range(3):

            @pl.when(where[n, axis] < 0)
            def _(slot=n * 3 + axis):
                vols[slot] = jnp.zeros((breadth, width), F32)

    tbuf[...] = jnp.zeros(tbuf.shape, BF16)
    xbuf[...] = jnp.zeros(xbuf.shape, BF16)
    copies(lambda c: c.wait())
    for n in range(count):
        fill(xbuf, 0, vols[n * 3])
        fill(xbuf, 1, own[n])
        place(ubuf, 0, n, product(first[:, : 2 * LANES], xbuf[...]))
        for g, axis in ((1, 2), (2, 1)):
            fill(xbuf, 0, vols[n * 3 + axis])
            place(ubuf, g, n, product(first[:, LANES : 2 * LANES], xbuf[:LANES]))

    def emit(q, pair, tile, lane, high, low):
        step = high.shape[0]
        row = pl.multiple_of(q * kgroup + pair * step, step)
        rbuf[tile, pl.ds(row, step), lane : lane + LANES] = high
        rbuf[tile, pl.ds(row + 2 * kgroup, step), lane : lane + LANES] = low

    second_stage(ubuf, lbuf, tbuf, second_high, second_low, per, breadth, (1, 0), (((0, 0), (1, 1)), ((2, 0),)), emit)

    def tile_body(tile, carry):
        wide = product(third[0], rbuf[tile, : 2 * kgroup])
        wide = wide[:LANES] + wide[LANES:] + product(third[0, :LANES], rbuf[tile, 2 * kgroup :])
        total = pick_diagonal(wide, breadth)
        for d in range(2):
            row = pl.multiple_of((tile * 2 + d) * breadth, breadth)
            obuf[pl.ds(row, breadth), :] = total[:, d * LANES : (d + 1) * LANES]
        return carry

    lax.fori_loop(0, count * breadth // 2, tile_body, 0)
    for n in range(count):

        def store(a, lane, value, n=n):
            out[n, a : a + 8, lane : lane + LANES] = value

        turn_block(obuf, n * breadth * breadth, breadth, store)


def spread_kernel(where, own, *refs, resumed):
    if resumed:
        old_keep, old_send = refs[:2]
        refs = refs[2:]
    first, second_high, second_low, third, keep, send = refs[:6]
    xbuf, ubuf, lbuf, tbuf, rbuf, obuf, block = refs[6:]
    count, breadth, width = own.shape
    per = first.shape[0] // breadth
    kgroup = per * breadth * breadth // LANES
    half_slots = keep.shape[0]
    if resumed:
        keep[...] = old_keep[...]
        send[...] = old_send[...]
    else:
        keep[...] = jnp.zeros(keep.shape, F32)
        send[...] = jnp.zeros(send.shape, F32)
    tbuf[...] = jnp.zeros(tbuf.shape, BF16)
    xbuf[...] = jnp.zeros(xbuf.shape, BF16)
    for n in range(count):
        fill(xbuf, 0, own[n])
        for g in range(2):
            place(ubuf, g, n, product(first[:, (1 + g) * LANES : (2 + g) * LANES], xbuf[...]))

    def emit(q, pair, tile, lane, high, low):
        step = high.shape[0]
        row = pl.multiple_of(q * 3 * kgroup + pair * step, step)
        rbuf[tile, pl.ds(row, step), lane : lane + LANES] = high
        rbuf[tile, pl.ds(row + kgroup, step), lane : lane + LANES] = low
        rbuf[tile, pl.ds(row + 2 * kgroup, step), lane : lane + LANES] = high

    recipes = (((1, 0),), ((0, 0),), ((0, 1),))
    second_stage(ubuf, lbuf, tbuf, second_high, second_low, per, breadth, (1, 2), recipes, emit)

    def tile_body(tile, carry):
        for q in range(3):
            wide = product(third[0, 1 if q == 1 else 0], rbuf[tile, q * 3 * kgroup : (q + 1) * 3 * kgroup])
            total = pick_diagonal(wide, breadth)
            for d in range(2):
                row = pl.multiple_of((tile * 2 + d) * breadth, breadth)
                obuf[q, pl.ds(row, breadth), :] = total[:, d * LANES : (d + 1) * LANES]
        return carry

    lax.fori_loop(0, count * breadth // 2, tile_body, 0)
    for n in range(count):
        for q in range(3):

            def store(a, lane, value):
                block[a : a + 8, lane : lane + LANES] = value

            turn_block(obuf.at[q], n * breadth * breadth, breadth, store)
            slot = where[n, q]

            @pl.when((slot >= 0) & (slot < half_slots))
            def _(slot=slot):
                keep[slot] = keep[slot] + block[...]

            @pl.when(slot >= half_slots)
            def _(slot=slot):
                send[slot - half_slots] = send[slot - half_slots] + block[...]


def whole_spec(array):
    return pl.BlockSpec(array.shape, lambda i, w, rank=len(array.shape): (0,) * rank)


def group_spec(array, g, size):
    rank = len(array.shape)
    return pl.BlockSpec((size,) + array.shape[1:], lambda i, w: (g,) + (0,) * (rank - 1))


def stage_scratch(volumes, recipes, thick, count, breadth, width, per):
    hi_count = breadth * breadth // LANES
    return [
        pltpu.VMEM((volumes, count, hi_count, per * breadth + PAD, LANES), F32),
        pltpu.VMEM((2, volumes, breadth * hi_count, 2 * LANES), BF16),
        pltpu.VMEM((2, 2, 2 * LANES, 2 * LANES), BF16),
        pltpu.VMEM((count * breadth // 2, recipes * thick * per * hi_count, 2 * LANES), BF16),
    ]


def cost(count, breadth, per, units):
    return pl.CostEstimate(flops=units * per * 2 * count * breadth**4 * 200, transcendentals=0, bytes_accessed=1 << 22)


def stage_call(kernel, name, where, own, extra, extra_specs, weights, third, g, groups, out_shapes, scratch, units):
    first, second_high, second_low = weights
    breadth = own.shape[1]
    terms = second_high.shape[0]
    per = terms // groups
    return pl.pallas_call(
        kernel,
        out_shape=out_shapes,
        grid_spec=pltpu.PrefetchScalarGridSpec(
            num_scalar_prefetch=1,
            grid=(1,),
            in_specs=[whole_spec(own)]
            + extra_specs
            + [
                group_spec(first, g, per * breadth),
                group_spec(second_high, g, per),
                group_spec(second_low, g, per),
                group_spec(third, g, 1),
            ],
            out_specs=[whole_spec(shape) for shape in out_shapes],
            scratch_shapes=scratch,
        ),
        compiler_params=pltpu.CompilerParams(dimension_semantics=("arbitrary",), vmem_limit_bytes=60 << 20),
        cost_estimate=cost(own.shape[0], breadth, per, units),
        name=name,
    )(where, own, *extra, first, second_high, second_low, third)


def merge_call(where, own, parts, weights, third, g, groups):
    count, breadth, width = own.shape
    per = weights[1].shape[0] // groups
    scratch = stage_scratch(3, 2, 2, count, breadth, width, per)
    scratch = (
        [pltpu.VMEM((count * 3, breadth, width), F32), pltpu.VMEM((2 * LANES, width), BF16)]
        + scratch
        + [pltpu.VMEM((count * breadth * breadth, LANES), F32), pltpu.SemaphoreType.DMA((count * 3,))]
    )
    return stage_call(
        functools.partial(merge_kernel, parts=len(parts)),
        "merge",
        where,
        own,
        list(parts),
        [pl.BlockSpec(memory_space=pl.ANY)] * len(parts),
        weights,
        third,
        g,
        groups,
        [jax.ShapeDtypeStruct(own.shape, F32)],
        scratch,
        9,
    )[0]


def spread_call(where, own, old, slots, weights, third, g, groups):
    count, breadth, width = own.shape
    per = weights[1].shape[0] // groups
    scratch = stage_scratch(2, 3, 3, count, breadth, width, per)
    scratch = (
        [pltpu.VMEM((LANES, width), BF16)]
        + scratch
        + [pltpu.VMEM((3, count * breadth * breadth, LANES), F32), pltpu.VMEM((breadth, width), F32)]
    )
    shape = jax.ShapeDtypeStruct((slots // 2, breadth, width), F32)
    return stage_call(
        functools.partial(spread_kernel, resumed=len(old) > 0),
        "spread",
        where,
        own,
        list(old),
        [whole_spec(shape)] * len(old),
        weights,
        third,
        g,
        groups,
        [shape, shape],
        scratch,
        8,
    )


def to_row(column):
    size = column.shape[0]
    diagonal = iota((size, size), 0) == iota((size, size), 1)
    return jnp.sum(jnp.where(diagonal, column, 0.0), axis=0, keepdims=True)


def to_column(row):
    size = row.shape[1]
    diagonal = iota((size, size), 0) == iota((size, size), 1)
    return jnp.sum(jnp.where(diagonal, row, 0.0), axis=1, keepdims=True)


def place_row(slot_row, runs, run_size, capacity):
    held = slot_row.shape[1]
    run_row = jnp.zeros(slot_row.shape, F32)
    for r in range(1, runs):
        run_row = run_row + jnp.where(slot_row >= r * run_size, 1.0, 0.0)
    same = to_column(run_row) == run_row
    earlier = iota((held, held), 0) < iota((held, held), 1)
    before = jnp.sum(jnp.where(same & earlier, 1.0, 0.0), axis=0, keepdims=True)
    return run_row * capacity + before


def pack_kernel(slot_row, fine, out, stack, *, runs, run_size):
    held, volume = fine.shape
    capacity = out.shape[1]
    places = runs * capacity
    slots = slot_row[...]
    place = place_row(slots, runs, run_size, capacity)
    hit = iota((places, held), 0).astype(F32) == place
    ids = jnp.sum(jnp.where(hit, slots.astype(F32) + 1.0, 0.0), axis=1, keepdims=True)
    ids = jnp.broadcast_to(ids, (places, LANES))
    one = jnp.where(hit, 1.0, 0.0).astype(BF16)
    rest = fine[...]
    for part in range(3):
        head = rest.astype(BF16)
        stack[part * held : (part + 1) * held] = head
        rest = rest - head.astype(F32)
    packed = product(jnp.concatenate([one] * 3, axis=1), stack[...])
    for r in range(runs):
        out[r, :, :volume] = packed[r * capacity : (r + 1) * capacity]
        out[r, :, volume:] = ids[r * capacity : (r + 1) * capacity]


def unpack_kernel(slot_row, back, out, stack, *, run_size):
    held, volume = out.shape
    runs, capacity = back.shape[:2]
    places = runs * capacity
    place = to_column(place_row(slot_row[...], runs, run_size, capacity))
    hit = iota((held, places), 1).astype(F32) == place
    one = jnp.where(hit, 1.0, 0.0).astype(BF16)
    rest = jnp.concatenate([back[r] for r in range(runs)], axis=0)
    for part in range(3):
        head = rest.astype(BF16)
        stack[part * places : (part + 1) * places] = head
        rest = rest - head.astype(F32)
    out[...] = product(jnp.concatenate([one] * 3, axis=1), stack[...])


def child_code(ids, held):
    at = ids - 1.0
    return jnp.where(at < 0.0, -1.0, at - held * jnp.floor(at / held))


def row_code(index, count):
    inner = index & 7
    code = (inner >> 1) * 8 + (inner & 1) * 4 + (index >> 3)
    return jnp.where(inner < 2 * count, code.astype(F32), -2.0)


def child_rows(filter_matrix, count):
    breadth = filter_matrix.shape[0]
    half = breadth // 2
    lane = iota((breadth, half * 8), 1)
    inner = lane & 7
    hot = iota((breadth, half * 8), 0) == (inner & 1) * half + (lane >> 3)
    spread = exact_expand(filter_matrix, hot)
    return jnp.concatenate([jnp.where(inner >> 1 == n, spread, 0.0) for n in range(count)], axis=0)


def triple_lanes(x):
    high, low = split(x)
    return jnp.concatenate([high, high, low], axis=1)


def filter_kernel(got, filter_ref, out, stack, lines, cross, weave, *, count):
    runs, capacity, volume = got.shape
    volume = volume - LANES
    places = runs * capacity
    breadth = filter_ref.shape[0]
    half = breadth // 2
    width = out.shape[2]
    face = width // 4
    span = volume // face
    lo_count = LANES // breadth
    hi_count = breadth // lo_count
    matrix = filter_ref[...]
    turned = matrix.T
    lane = iota((breadth, width), 1)
    outer = lane // breadth
    across_z = exact_expand(turned, iota((breadth, width), 0) == lane % breadth)
    across_y = exact_expand(turned, iota((breadth, width), 0) == (outer % lo_count) * hi_count + outer // lo_count)
    for g in range(4):
        zs = across_z[(g & 1) * half : (g & 1) * half + half]
        for j in range(half):
            row = (g >> 1) * half + j
            high, low = split(zs * across_y[row : row + 1])
            at = (g * half + j) * half
            cross[0, at : at + half] = high
            cross[1, at : at + half] = low
    joined = jnp.concatenate([got[r] for r in range(runs)], axis=0)
    code = to_row(child_code(joined[:, volume : volume + 1], 8 * count))
    hit = row_code(iota((32, places), 0), count) == code
    one = jnp.where(hit, 1.0, 0.0).astype(BF16)
    high, low = split(joined[:, :volume])
    stack[:places] = high
    stack[places:] = low
    boxes = product(jnp.concatenate([one, one], axis=1), stack[...])
    for g in range(4):
        for i in range(0, span, 2):
            both = jnp.concatenate(
                [boxes[g * 8 : g * 8 + 8, (i + d) * face : (i + d + 1) * face] for d in range(2)], axis=0
            )
            high, low = split(both)
            lines[0, i * 8 : i * 8 + 16, g * face : (g + 1) * face] = high
            lines[1, i * 8 : i * 8 + 16, g * face : (g + 1) * face] = low
    total = product(lines[0], cross[0]) + product(lines[1], cross[0]) + product(lines[0], cross[1])
    high, low = split(total)
    size = total.shape[0]
    weave[:size] = high
    weave[size : 2 * size] = low
    weave[2 * size :] = high
    result = product(triple_lanes(child_rows(matrix, count)), weave[...])
    for n in range(count):
        out[n] = result[n * breadth : (n + 1) * breadth]


def unfilter_kernel(got, filter_ref, *refs, count, pieces):
    applied = refs[:pieces]
    out, weave, cross, stack = refs[pieces:]
    runs, capacity, volume = out.shape
    places = runs * capacity
    breadth = filter_ref.shape[0]
    half = breadth // 2
    width = applied[0].shape[2]
    face = width // 4
    size = count * breadth
    matrix = filter_ref[...]
    lane = iota((breadth, width), 1)
    octant = lane // face
    across_c = exact_expand(matrix, iota((breadth, width), 0) == octant % 2 * half + lane % half)
    across_b = exact_expand(matrix, iota((breadth, width), 0) == octant // 2 * half + lane // half % half)
    for b in range(breadth):
        high, low = split(across_c * across_b[b : b + 1])
        cross[0, b * breadth : (b + 1) * breadth] = high
        cross[1, b * breadth : (b + 1) * breadth] = low
    for n in range(count):
        total = applied[0][n]
        for piece in applied[1:]:
            total = total + piece[n]
        high, low = split(total)
        at = n * breadth
        weave[at : at + breadth] = high
        weave[size + at : size + at + breadth] = low
        weave[2 * size + at : 2 * size + at + breadth] = high
    lines = product(triple_lanes(child_rows(matrix, count).T), weave[...])
    high, low = split(lines)
    total = product(high, cross[0]) + product(low, cross[0]) + product(high, cross[1])
    for g in range(0, 4, 2):
        for i in range(total.shape[0] // 8):
            both = jnp.concatenate(
                [total[i * 8 : i * 8 + 8, (g + d) * face : (g + d + 1) * face] for d in range(2)], axis=0
            )
            high, low = split(both)
            stack[g * 8 : g * 8 + 16, i * face : (i + 1) * face] = high
            stack[32 + g * 8 : 32 + g * 8 + 16, i * face : (i + 1) * face] = low
    ids = jnp.concatenate([got[r] for r in range(runs)], axis=0)
    code = child_code(ids[:, :1], 8 * count)
    hit = row_code(iota((places, 32), 1), count) == code
    one = jnp.where(hit, 1.0, 0.0).astype(BF16)
    packed = product(jnp.concatenate([one, one], axis=1), stack[...])
    for r in range(runs):
        out[r] = packed[r * capacity : (r + 1) * capacity]


def vmem_call(kernel, out_shape, scratch, name, in_specs=None, **settings):
    extra = {} if in_specs is None else dict(grid=(1,), in_specs=in_specs)
    if in_specs is not None:
        rank = len(out_shape)
        extra["out_specs"] = pl.BlockSpec(out_shape, lambda i: (0,) * rank)
    return pl.pallas_call(
        functools.partial(kernel, **settings),
        out_shape=jax.ShapeDtypeStruct(out_shape, F32),
        scratch_shapes=[pltpu.VMEM(shape, dtype) for shape, dtype in scratch],
        compiler_params=pltpu.CompilerParams(vmem_limit_bytes=60 << 20),
        name=name,
        **extra,
    )


def moved(array, row_step, bit):
    rows = lax.axis_size("row")
    cols = lax.axis_size("col")
    pairs = [
        (r * cols + c, (r + row_step) % rows * cols + (c ^ bit)) for r in range(rows) for c in range(cols)
    ]
    return lax.ppermute(array, ("row", "col"), pairs)


def local(fine_coeffs, fine_slot, neighbours, filter_matrix, kernel_ops):
    breadth = filter_matrix.shape[0]
    terms = kernel_ops.shape[0]
    runs = lax.axis_size("row")
    cols = lax.axis_size("col")
    held, volume = fine_coeffs.shape
    par_row = neighbours.shape[0]
    count = held // 8
    capacity = 2 * (held // runs)
    places = runs * capacity
    width = breadth * breadth
    hi_count = width // LANES
    groups = 2
    per = terms // groups
    uppers = range(0, cols, 2)

    slot_row = fine_slot.reshape(1, held)
    routing = dict(run_size=8 * par_row)
    sent = vmem_call(
        pack_kernel, (runs, capacity, volume + LANES), [((3 * held, volume), BF16)], "pack", runs=runs, **routing
    )(slot_row, fine_coeffs)
    got = lax.all_to_all(sent, "row", split_axis=0, concat_axis=0, tiled=True)

    first, second_high, second_low, merge_third, spread_third = pl.pallas_call(
        functools.partial(prepare_kernel, groups=groups),
        out_shape=[
            jax.ShapeDtypeStruct((terms * breadth, 3 * LANES), BF16),
            jax.ShapeDtypeStruct((terms, 3, breadth, LANES), BF16),
            jax.ShapeDtypeStruct((terms, 3, breadth, LANES), BF16),
            jax.ShapeDtypeStruct((groups, 2 * LANES, 2 * per * hi_count), BF16),
            jax.ShapeDtypeStruct((groups, 2, LANES, 3 * per * hi_count), BF16),
        ],
        compiler_params=pltpu.CompilerParams(vmem_limit_bytes=60 << 20),
        name="prepare",
    )(kernel_ops.reshape(terms * 9 * breadth, breadth))
    weights = (first, second_high, second_low)

    col_index = lax.axis_index("col")
    mine = lax.dynamic_slice_in_dim(neighbours, col_index * count, count, 0)[:, ::2]
    within = mine % par_row
    relation = (within // count) ^ col_index
    spot = (relation % 2) * (len(uppers) * count) + relation // 2 * count + within % count
    where = jnp.where(mine >= 0, spot, -1)

    filtered = vmem_call(
        filter_kernel,
        (count, breadth, width),
        [
            ((2 * places, volume), BF16),
            ((2, breadth * 4, width), BF16),
            ((2, width, width), BF16),
            ((12 * breadth, width), BF16),
        ],
        "filter",
        count=count,
    )(got, filter_matrix)

    parts = [moved(filtered, -1, u) for u in uppers]
    spread = spread_call(where, filtered, (), par_row, weights, spread_third, 0, groups)
    parts, spread = lax.optimization_barrier((parts, spread))
    parts = parts + [moved(part, 0, 1) for part in parts]
    keep, send = spread_call(where, filtered, spread, par_row, weights, spread_third, 1, groups)
    parts, keep, send = lax.optimization_barrier((parts, keep, send))

    came = moved(send, 0, 1)
    early = merge_call(where, filtered, parts, weights, merge_third, 0, groups)
    came, early = lax.optimization_barrier((came, early))
    terms_out = [moved(keep[u // 2 * count : (u // 2 + 1) * count] + came[u // 2 * count : (u // 2 + 1) * count], 1, u) for u in uppers]
    late = merge_call(where, filtered, parts, weights, merge_third, 1, groups)

    pieces = [early, late] + terms_out
    tail = volume // LANES
    results = vmem_call(
        unfilter_kernel,
        (runs, capacity, volume),
        [
            ((3 * count * breadth, width), BF16),
            ((2, width, width), BF16),
            ((64, volume), BF16),
        ],
        "unfilter",
        in_specs=[
            pl.BlockSpec((runs, capacity, LANES), lambda i: (0, 0, tail)),
            pl.BlockSpec((breadth, breadth), lambda i: (0, 0)),
        ]
        + [pl.BlockSpec((count, breadth, width), lambda i: (0, 0, 0))] * len(pieces),
        count=count,
        pieces=len(pieces),
    )(got, filter_matrix, *pieces)
    back = lax.all_to_all(results, "row", split_axis=0, concat_axis=0, tiled=True)
    return vmem_call(unpack_kernel, (held, volume), [((3 * places, volume), BF16)], "unpack", **routing)(slot_row, back)


def solution(mesh):
    in_specs = (P(("row", "col"), None), P(("row", "col")), P("row", None), P(), P())
    out_specs = P(("row", "col"), None)
    return jax.shard_map(local, mesh=mesh, in_specs=in_specs, out_specs=out_specs, check_vma=False)
```

```python
import functools

import jax
import jax.numpy as jnp
import numpy as np
from jax import lax
from jax.experimental import pallas as pl
from jax.experimental.pallas import tpu as pltpu
from jax.sharding import PartitionSpec as P

F32, BF16 = jnp.float32, jnp.bfloat16
LANES = 128
PAD = 8


def iota(shape, axis):
    return lax.broadcasted_iota(jnp.int32, shape, axis)


def split(x):
    high = x.astype(BF16)
    return high, (x - high.astype(F32)).astype(BF16)


def product(a, b):
    return jnp.dot(a, b, preferred_element_type=F32)


def exact_expand(x, hot):
    one = jnp.where(hot, 1.0, 0.0).astype(BF16)
    total = None
    for part in range(3):
        head = x.astype(BF16)
        piece = product(head, one)
        total = piece if total is None else total + piece
        x = x - head.astype(F32)
    return total


def prepare_kernel(ops, first, second_high, second_low, merge, spread, *, groups):
    breadth = ops.shape[1]
    terms = ops.shape[0] // (9 * breadth)
    lo_count = LANES // breadth
    hi_count = breadth // lo_count
    per = terms // groups

    def factor(term, axis, k):
        at = ((term * 3 + axis) * 3 + k) * breadth
        return ops[at : at + breadth]

    blank = jnp.zeros((breadth, LANES - 3 * breadth), F32)
    for term in range(terms):
        for k in range(3):
            value = factor(term, 0, k)
            high = value.astype(BF16).astype(F32)
            line = jnp.concatenate([high, high, value - high, blank], axis=1)
            first[term * breadth : (term + 1) * breadth, k * LANES : (k + 1) * LANES] = line.astype(BF16)
        at = (term * 9 + 6) * breadth
        turned = ops[at : at + 3 * breadth].T
        for k in range(3):
            high, low = split(jnp.concatenate([turned[:, k * breadth : (k + 1) * breadth]] * lo_count, axis=1))
            second_high[term, k] = high
            second_low[term, k] = low
    for g in range(groups):
        for inner in range(lo_count):
            strip = [
                jnp.concatenate(
                    [factor(g * per + t, 1, k)[:, inner * hi_count : (inner + 1) * hi_count] for t in range(per)], axis=1
                )
                for k in range(3)
            ]
            high, low = split(jnp.concatenate([strip[1], strip[0]], axis=1))
            merge[g, inner * breadth : (inner + 1) * breadth] = high
            merge[g, LANES + inner * breadth : LANES + (inner + 1) * breadth] = low
            for s, k in enumerate((1, 2)):
                high = strip[k].astype(BF16).astype(F32)
                line = jnp.concatenate([high, high, strip[k] - high], axis=1)
                spread[g, s, inner * breadth : (inner + 1) * breadth] = line.astype(BF16)


def fill(xbuf, slot, block):
    breadth = block.shape[0]
    high, low = split(block)
    base = slot * LANES
    xbuf[base : base + breadth] = high
    xbuf[base + breadth : base + 2 * breadth] = low
    xbuf[base + 2 * breadth : base + 3 * breadth] = high


def place(ubuf, g, n, result):
    rows = result.shape[0]
    for h in range(result.shape[1] // LANES):
        ubuf[g, n, h, :rows] = result[:, h * LANES : (h + 1) * LANES]


def second_stage(ubuf, lbuf, tbuf, second_high, second_low, per, breadth, offsets, recipes, emit):
    volumes, count, hi_count, stride = ubuf.shape[:4]
    lo_count = LANES // breadth
    flat = ubuf.reshape(volumes * count * hi_count * stride, LANES)
    block_mask = iota((LANES, LANES), 0) // breadth == iota((LANES, LANES), 1) // breadth
    zero_block = jnp.zeros((LANES, LANES), BF16)

    def pair_body(pair, carry):
        for spot, k in enumerate(offsets):
            for half in range(2):
                term = pair * 2 + half
                high = jnp.concatenate([second_high[term, k]] * lo_count, axis=0)
                low = jnp.concatenate([second_low[term, k]] * lo_count, axis=0)
                high = jnp.where(block_mask, high, zero_block)
                low = jnp.where(block_mask, low, zero_block)
                tbuf[half, spot, :LANES, :LANES] = high
                tbuf[half, spot, LANES:, :LANES] = high
                tbuf[half, spot, :LANES, LANES:] = low
        for n in range(count):
            for half in range(2):
                term = pair * 2 + half
                for g in range(volumes):
                    base = (g * count + n) * hi_count * stride + term * breadth
                    for a in range(0, breadth, 2):
                        pieces = [flat[pl.ds(base + a + d, hi_count, stride=stride), :] for d in range(2)]
                        high, low = split(jnp.concatenate(pieces, axis=0))
                        at = a * hi_count
                        lbuf[half, g, at : at + 2 * hi_count, :LANES] = high
                        lbuf[half, g, at : at + 2 * hi_count, LANES:] = low
            results = []
            for half in range(2):
                line = []
                for recipe in recipes:
                    wide = None
                    for g, spot in recipe:
                        piece = product(lbuf[half, g], tbuf[half, spot])
                        wide = piece if wide is None else wide + piece
                    line.append(wide[:, :LANES] + wide[:, LANES:])
                results.append(line)
            for q in range(len(recipes)):
                for a in range(breadth):
                    both = jnp.concatenate(
                        [results[half][q][a * hi_count : (a + 1) * hi_count] for half in range(2)], axis=0
                    )
                    high, low = split(both)
                    emit(q, pair, (n * breadth + a) // 2, (a % 2) * LANES, high, low)
        return carry

    lax.fori_loop(0, per // 2, pair_body, 0)


def pick_diagonal(wide, breadth):
    lane_block = iota((breadth, wide.shape[1]), 1) % LANES // breadth
    total = wide[:breadth]
    for low in range(1, LANES // breadth):
        total = jnp.where(lane_block == low, wide[low * breadth : (low + 1) * breadth], total)
    return total


def turn_block(obuf, base, breadth, store):
    lo_count = LANES // breadth
    lane_of = iota((8, LANES), 1) // breadth
    for a in range(0, breadth, 8):
        for high in range(breadth // lo_count):
            level = [
                obuf[pl.ds(base + a * breadth + high * lo_count + low, 8, stride=breadth), :] for low in range(lo_count)
            ]
            step = 1
            while step < lo_count:
                own_side = (lane_of // step) % 2 == 0
                level = [
                    jnp.where(own_side, p, q) + pltpu.roll(jnp.where(own_side, q, p), step * breadth, 1)
                    for p, q in zip(level[::2], level[1::2])
                ]
                step *= 2
            store(a, high * LANES, level[0])


def merge_kernel(where, own, *refs, parts):
    sources = refs[:parts]
    first, second_high, second_low, third, out = refs[parts : parts + 5]
    vols, xbuf, ubuf, lbuf, tbuf, rbuf, obuf, sems = refs[parts + 5 :]
    count, breadth, width = own.shape
    per = first.shape[0] // breadth
    kgroup = per * breadth * breadth // LANES

    def copies(action):
        for n in range(count):
            for axis in range(3):
                slot = n * 3 + axis
                at = where[n, axis]
                start = 0
                for source in sources:
                    size = source.shape[0]

                    @pl.when((at >= start) & (at < start + size))
                    def _(source=source, start=start, slot=slot, at=at):
                        action(pltpu.make_async_copy(source.at[at - start], vols.at[slot], sems.at[slot]))

                    start += size

    group = pl.program_id(0)

    @pl.when(group == 0)
    def _():
        copies(lambda c: c.start())
        for n in range(count):
            for axis in range(3):

                @pl.when(where[n, axis] < 0)
                def _(slot=n * 3 + axis):
                    vols[slot] = jnp.zeros((breadth, width), F32)

        tbuf[...] = jnp.zeros(tbuf.shape, BF16)
        xbuf[...] = jnp.zeros(xbuf.shape, BF16)
        obuf[...] = jnp.zeros(obuf.shape, F32)
        copies(lambda c: c.wait())

    for n in range(count):
        fill(xbuf, 0, vols[n * 3])
        fill(xbuf, 1, own[n])
        place(ubuf, 0, n, product(first[:, : 2 * LANES], xbuf[...]))
        for g, axis in ((1, 2), (2, 1)):
            fill(xbuf, 0, vols[n * 3 + axis])
            place(ubuf, g, n, product(first[:, LANES : 2 * LANES], xbuf[:LANES]))

    def emit(q, pair, tile, lane, high, low):
        step = high.shape[0]
        row = pl.multiple_of(q * kgroup + pair * step, step)
        rbuf[tile, pl.ds(row, step), lane : lane + LANES] = high
        rbuf[tile, pl.ds(row + 2 * kgroup, step), lane : lane + LANES] = low

    second_stage(ubuf, lbuf, tbuf, second_high, second_low, per, breadth, (1, 0), (((0, 0), (1, 1)), ((2, 0),)), emit)

    def tile_body(tile, carry):
        wide = product(third[0], rbuf[tile, : 2 * kgroup])
        wide = wide[:LANES] + wide[LANES:] + product(third[0, :LANES], rbuf[tile, 2 * kgroup :])
        total = pick_diagonal(wide, breadth)
        for d in range(2):
            row = pl.multiple_of((tile * 2 + d) * breadth, breadth)
            obuf[pl.ds(row, breadth), :] = obuf[pl.ds(row, breadth), :] + total[:, d * LANES : (d + 1) * LANES]
        return carry

    lax.fori_loop(0, count * breadth // 2, tile_body, 0, unroll=True)

    @pl.when(group == pl.num_programs(0) - 1)
    def _():
        for n in range(count):

            def store(a, lane, value, n=n):
                out[n, a : a + 8, lane : lane + LANES] = value

            turn_block(obuf, n * breadth * breadth, breadth, store)


def spread_kernel(where, own, first, second_high, second_low, third, keep, send, *refs):
    xbuf, ubuf, lbuf, tbuf, rbuf, obuf, block = refs
    count, breadth, width = own.shape
    per = first.shape[0] // breadth
    kgroup = per * breadth * breadth // LANES
    half_slots = keep.shape[0]
    group = pl.program_id(0)

    @pl.when(group == 0)
    def _():
        keep[...] = jnp.zeros(keep.shape, F32)
        send[...] = jnp.zeros(send.shape, F32)
        tbuf[...] = jnp.zeros(tbuf.shape, BF16)
        xbuf[...] = jnp.zeros(xbuf.shape, BF16)
        obuf[...] = jnp.zeros(obuf.shape, F32)

    for n in range(count):
        fill(xbuf, 0, own[n])
        for g in range(2):
            place(ubuf, g, n, product(first[:, (1 + g) * LANES : (2 + g) * LANES], xbuf[...]))

    def emit(q, pair, tile, lane, high, low):
        step = high.shape[0]
        row = pl.multiple_of(q * 3 * kgroup + pair * step, step)
        rbuf[tile, pl.ds(row, step), lane : lane + LANES] = high
        rbuf[tile, pl.ds(row + kgroup, step), lane : lane + LANES] = low
        rbuf[tile, pl.ds(row + 2 * kgroup, step), lane : lane + LANES] = high

    recipes = (((1, 0),), ((0, 0),), ((0, 1),))
    second_stage(ubuf, lbuf, tbuf, second_high, second_low, per, breadth, (1, 2), recipes, emit)

    def tile_body(tile, carry):
        for q in range(3):
            wide = product(third[0, 1 if q == 1 else 0], rbuf[tile, q * 3 * kgroup : (q + 1) * 3 * kgroup])
            total = pick_diagonal(wide, breadth)
            for d in range(2):
                row = pl.multiple_of((tile * 2 + d) * breadth, breadth)
                obuf[q, pl.ds(row, breadth), :] = (
                    obuf[q, pl.ds(row, breadth), :] + total[:, d * LANES : (d + 1) * LANES]
                )
        return carry

    lax.fori_loop(0, count * breadth // 2, tile_body, 0, unroll=True)

    @pl.when(group == pl.num_programs(0) - 1)
    def _():
        for n in range(count):
            for q in range(3):

                def store(a, lane, value):
                    block[a : a + 8, lane : lane + LANES] = value

                turn_block(obuf.at[q], n * breadth * breadth, breadth, store)
                slot = where[n, q]

                @pl.when((slot >= 0) & (slot < half_slots))
                def _(slot=slot):
                    keep[slot] = keep[slot] + block[...]

                @pl.when(slot >= half_slots)
                def _(slot=slot):
                    send[slot - half_slots] = send[slot - half_slots] + block[...]


def whole_spec(array):
    return pl.BlockSpec(array.shape, lambda i, w, rank=len(array.shape): (0,) * rank)


def group_spec(array, size):
    rank = len(array.shape)
    return pl.BlockSpec((size,) + array.shape[1:], lambda i, w: (i,) + (0,) * (rank - 1))


def stage_scratch(volumes, recipes, thick, count, breadth, width, per):
    hi_count = breadth * breadth // LANES
    return [
        pltpu.VMEM((volumes, count, hi_count, per * breadth + PAD, LANES), F32),
        pltpu.VMEM((2, volumes, breadth * hi_count, 2 * LANES), BF16),
        pltpu.VMEM((2, 2, 2 * LANES, 2 * LANES), BF16),
        pltpu.VMEM((count * breadth // 2, recipes * thick * per * hi_count, 2 * LANES), BF16),
    ]


def cost(count, breadth, per, units):
    return pl.CostEstimate(flops=units * per * 2 * count * breadth**4 * 200, transcendentals=0, bytes_accessed=1 << 22)


def stage_call(kernel, name, where, own, extra, extra_specs, weights, third, groups, out_shapes, scratch, units):
    first, second_high, second_low = weights
    breadth = own.shape[1]
    terms = second_high.shape[0]
    per = terms // groups
    return pl.pallas_call(
        kernel,
        out_shape=out_shapes,
        grid_spec=pltpu.PrefetchScalarGridSpec(
            num_scalar_prefetch=1,
            grid=(groups,),
            in_specs=[whole_spec(own)]
            + extra_specs
            + [
                group_spec(first, per * breadth),
                group_spec(second_high, per),
                group_spec(second_low, per),
                group_spec(third, 1),
            ],
            out_specs=[whole_spec(shape) for shape in out_shapes],
            scratch_shapes=scratch,
        ),
        compiler_params=pltpu.CompilerParams(dimension_semantics=("arbitrary",), vmem_limit_bytes=60 << 20),
        cost_estimate=cost(own.shape[0], breadth, terms, units),
        name=name,
    )(where, own, *extra, first, second_high, second_low, third)


def merge_call(where, own, parts, weights, third, groups):
    count, breadth, width = own.shape
    per = weights[1].shape[0] // groups
    scratch = stage_scratch(3, 2, 2, count, breadth, width, per)
    scratch = (
        [pltpu.VMEM((count * 3, breadth, width), F32), pltpu.VMEM((2 * LANES, width), BF16)]
        + scratch
        + [pltpu.VMEM((count * breadth * breadth, LANES), F32), pltpu.SemaphoreType.DMA((count * 3,))]
    )
    return stage_call(
        functools.partial(merge_kernel, parts=len(parts)),
        "merge",
        where,
        own,
        list(parts),
        [pl.BlockSpec(memory_space=pl.ANY)] * len(parts),
        weights,
        third,
        groups,
        [jax.ShapeDtypeStruct(own.shape, F32)],
        scratch,
        9,
    )[0]


def spread_call(where, own, slots, weights, third, groups):
    count, breadth, width = own.shape
    per = weights[1].shape[0] // groups
    scratch = stage_scratch(2, 3, 3, count, breadth, width, per)
    scratch = (
        [pltpu.VMEM((LANES, width), BF16)]
        + scratch
        + [pltpu.VMEM((3, count * breadth * breadth, LANES), F32), pltpu.VMEM((breadth, width), F32)]
    )
    shape = jax.ShapeDtypeStruct((slots // 2, breadth, width), F32)
    return stage_call(
        spread_kernel,
        "spread",
        where,
        own,
        [],
        [],
        weights,
        third,
        groups,
        [shape, shape],
        scratch,
        8,
    )


def to_row(column):
    size = column.shape[0]
    diagonal = iota((size, size), 0) == iota((size, size), 1)
    return jnp.sum(jnp.where(diagonal, column, 0.0), axis=0, keepdims=True)


def to_column(row):
    size = row.shape[1]
    diagonal = iota((size, size), 0) == iota((size, size), 1)
    return jnp.sum(jnp.where(diagonal, row, 0.0), axis=1, keepdims=True)


def place_row(slot_row, runs, run_size, capacity):
    held = slot_row.shape[1]
    run_row = jnp.zeros(slot_row.shape, F32)
    for r in range(1, runs):
        run_row = run_row + jnp.where(slot_row >= r * run_size, 1.0, 0.0)
    same = to_column(run_row) == run_row
    earlier = iota((held, held), 0) < iota((held, held), 1)
    before = jnp.sum(jnp.where(same & earlier, 1.0, 0.0), axis=0, keepdims=True)
    return run_row * capacity + before


def pack_kernel(slot_row, fine, out, stack, *, runs, run_size):
    held, volume = fine.shape
    capacity = out.shape[1]
    places = runs * capacity
    slots = slot_row[...]
    place = place_row(slots, runs, run_size, capacity)
    hit = iota((places, held), 0).astype(F32) == place
    ids = jnp.sum(jnp.where(hit, slots.astype(F32) + 1.0, 0.0), axis=1, keepdims=True)
    ids = jnp.broadcast_to(ids, (places, LANES))
    one = jnp.where(hit, 1.0, 0.0).astype(BF16)
    rest = fine[...]
    for part in range(3):
        head = rest.astype(BF16)
        stack[part * held : (part + 1) * held] = head
        rest = rest - head.astype(F32)
    packed = product(jnp.concatenate([one] * 3, axis=1), stack[...])
    for r in range(runs):
        out[r, :, :volume] = packed[r * capacity : (r + 1) * capacity]
        out[r, :, volume:] = ids[r * capacity : (r + 1) * capacity]


def unpack_kernel(slot_row, back, out, stack, *, run_size):
    held, volume = out.shape
    runs, capacity = back.shape[:2]
    places = runs * capacity
    place = to_column(place_row(slot_row[...], runs, run_size, capacity))
    hit = iota((held, places), 1).astype(F32) == place
    one = jnp.where(hit, 1.0, 0.0).astype(BF16)
    rest = jnp.concatenate([back[r] for r in range(runs)], axis=0)
    for part in range(3):
        head = rest.astype(BF16)
        stack[part * places : (part + 1) * places] = head
        rest = rest - head.astype(F32)
    out[...] = product(jnp.concatenate([one] * 3, axis=1), stack[...])


def child_code(ids, held):
    at = ids - 1.0
    return jnp.where(at < 0.0, -1.0, at - held * jnp.floor(at / held))


def row_code(index, count):
    inner = index & 7
    code = (inner >> 1) * 8 + (inner & 1) * 4 + (index >> 3)
    return jnp.where(inner < 2 * count, code.astype(F32), -2.0)


def child_rows(filter_matrix, count):
    breadth = filter_matrix.shape[0]
    half = breadth // 2
    lane = iota((breadth, half * 8), 1)
    inner = lane & 7
    hot = iota((breadth, half * 8), 0) == (inner & 1) * half + (lane >> 3)
    spread = exact_expand(filter_matrix, hot)
    return jnp.concatenate([jnp.where(inner >> 1 == n, spread, 0.0) for n in range(count)], axis=0)


def triple_lanes(x):
    high, low = split(x)
    return jnp.concatenate([high, high, low], axis=1)


def filter_kernel(got, filter_ref, out, stack, lines, cross, weave, *, count):
    runs, capacity, volume = got.shape
    volume = volume - LANES
    places = runs * capacity
    breadth = filter_ref.shape[0]
    half = breadth // 2
    width = out.shape[2]
    face = width // 4
    span = volume // face
    lo_count = LANES // breadth
    hi_count = breadth // lo_count
    matrix = filter_ref[...]
    turned = matrix.T
    lane = iota((breadth, width), 1)
    outer = lane // breadth
    across_z = exact_expand(turned, iota((breadth, width), 0) == lane % breadth)
    across_y = exact_expand(turned, iota((breadth, width), 0) == (outer % lo_count) * hi_count + outer // lo_count)
    for g in range(4):
        zs = across_z[(g & 1) * half : (g & 1) * half + half]
        for j in range(half):
            row = (g >> 1) * half + j
            high, low = split(zs * across_y[row : row + 1])
            at = (g * half + j) * half
            cross[0, at : at + half] = high
            cross[1, at : at + half] = low
    joined = jnp.concatenate([got[r] for r in range(runs)], axis=0)
    code = to_row(child_code(joined[:, volume : volume + 1], 8 * count))
    hit = row_code(iota((32, places), 0), count) == code
    one = jnp.where(hit, 1.0, 0.0).astype(BF16)
    high, low = split(joined[:, :volume])
    stack[:places] = high
    stack[places:] = low
    boxes = product(jnp.concatenate([one, one], axis=1), stack[...])
    for g in range(4):
        for i in range(0, span, 2):
            both = jnp.concatenate(
                [boxes[g * 8 : g * 8 + 8, (i + d) * face : (i + d + 1) * face] for d in range(2)], axis=0
            )
            high, low = split(both)
            lines[0, i * 8 : i * 8 + 16, g * face : (g + 1) * face] = high
            lines[1, i * 8 : i * 8 + 16, g * face : (g + 1) * face] = low
    total = product(lines[0], cross[0]) + product(lines[1], cross[0]) + product(lines[0], cross[1])
    high, low = split(total)
    size = total.shape[0]
    weave[:size] = high
    weave[size : 2 * size] = low
    weave[2 * size :] = high
    result = product(triple_lanes(child_rows(matrix, count)), weave[...])
    for n in range(count):
        out[n] = result[n * breadth : (n + 1) * breadth]


def unfilter_kernel(got, filter_ref, *refs, count, pieces):
    applied = refs[:pieces]
    out, weave, cross, stack = refs[pieces:]
    runs, capacity, volume = out.shape
    places = runs * capacity
    breadth = filter_ref.shape[0]
    half = breadth // 2
    width = applied[0].shape[2]
    face = width // 4
    size = count * breadth
    matrix = filter_ref[...]
    lane = iota((breadth, width), 1)
    octant = lane // face
    across_c = exact_expand(matrix, iota((breadth, width), 0) == octant % 2 * half + lane % half)
    across_b = exact_expand(matrix, iota((breadth, width), 0) == octant // 2 * half + lane // half % half)
    for b in range(breadth):
        high, low = split(across_c * across_b[b : b + 1])
        cross[0, b * breadth : (b + 1) * breadth] = high
        cross[1, b * breadth : (b + 1) * breadth] = low
    for n in range(count):
        total = applied[0][n]
        for piece in applied[1:]:
            total = total + piece[n]
        high, low = split(total)
        at = n * breadth
        weave[at : at + breadth] = high
        weave[size + at : size + at + breadth] = low
        weave[2 * size + at : 2 * size + at + breadth] = high
    lines = product(triple_lanes(child_rows(matrix, count).T), weave[...])
    high, low = split(lines)
    total = product(high, cross[0]) + product(low, cross[0]) + product(high, cross[1])
    for g in range(0, 4, 2):
        for i in range(total.shape[0] // 8):
            both = jnp.concatenate(
                [total[i * 8 : i * 8 + 8, (g + d) * face : (g + d + 1) * face] for d in range(2)], axis=0
            )
            high, low = split(both)
            stack[g * 8 : g * 8 + 16, i * face : (i + 1) * face] = high
            stack[32 + g * 8 : 32 + g * 8 + 16, i * face : (i + 1) * face] = low
    ids = jnp.concatenate([got[r] for r in range(runs)], axis=0)
    code = child_code(ids[:, :1], 8 * count)
    hit = row_code(iota((places, 32), 1), count) == code
    one = jnp.where(hit, 1.0, 0.0).astype(BF16)
    packed = product(jnp.concatenate([one, one], axis=1), stack[...])
    for r in range(runs):
        out[r] = packed[r * capacity : (r + 1) * capacity]


def vmem_call(kernel, out_shape, scratch, name, in_specs=None, **settings):
    extra = {} if in_specs is None else dict(grid=(1,), in_specs=in_specs)
    if in_specs is not None:
        rank = len(out_shape)
        extra["out_specs"] = pl.BlockSpec(out_shape, lambda i: (0,) * rank)
    return pl.pallas_call(
        functools.partial(kernel, **settings),
        out_shape=jax.ShapeDtypeStruct(out_shape, F32),
        scratch_shapes=[pltpu.VMEM(shape, dtype) for shape, dtype in scratch],
        compiler_params=pltpu.CompilerParams(vmem_limit_bytes=60 << 20),
        name=name,
        **extra,
    )


def moved(array, row_step, bit):
    rows = lax.axis_size("row")
    cols = lax.axis_size("col")
    pairs = [
        (r * cols + c, (r + row_step) % rows * cols + (c ^ bit)) for r in range(rows) for c in range(cols)
    ]
    return lax.ppermute(array, ("row", "col"), pairs)


def local(fine_coeffs, fine_slot, neighbours, filter_matrix, kernel_ops):
    breadth = filter_matrix.shape[0]
    terms = kernel_ops.shape[0]
    runs = lax.axis_size("row")
    cols = lax.axis_size("col")
    held, volume = fine_coeffs.shape
    par_row = neighbours.shape[0]
    count = held // 8
    capacity = 2 * (held // runs)
    places = runs * capacity
    width = breadth * breadth
    hi_count = width // LANES
    groups = 2
    per = terms // groups
    uppers = range(0, cols, 2)

    slot_row = fine_slot.reshape(1, held)
    routing = dict(run_size=8 * par_row)
    sent = vmem_call(
        pack_kernel, (runs, capacity, volume + LANES), [((3 * held, volume), BF16)], "pack", runs=runs, **routing
    )(slot_row, fine_coeffs)
    got = lax.all_to_all(sent, "row", split_axis=0, concat_axis=0, tiled=True)

    first, second_high, second_low, merge_third, spread_third = pl.pallas_call(
        functools.partial(prepare_kernel, groups=groups),
        out_shape=[
            jax.ShapeDtypeStruct((terms * breadth, 3 * LANES), BF16),
            jax.ShapeDtypeStruct((terms, 3, breadth, LANES), BF16),
            jax.ShapeDtypeStruct((terms, 3, breadth, LANES), BF16),
            jax.ShapeDtypeStruct((groups, 2 * LANES, 2 * per * hi_count), BF16),
            jax.ShapeDtypeStruct((groups, 2, LANES, 3 * per * hi_count), BF16),
        ],
        compiler_params=pltpu.CompilerParams(vmem_limit_bytes=60 << 20),
        name="prepare",
    )(kernel_ops.reshape(terms * 9 * breadth, breadth))
    weights = (first, second_high, second_low)

    col_index = lax.axis_index("col")
    mine = lax.dynamic_slice_in_dim(neighbours, col_index * count, count, 0)[:, ::2]
    within = mine % par_row
    relation = (within // count) ^ col_index
    spot = (relation % 2) * (len(uppers) * count) + relation // 2 * count + within % count
    where = jnp.where(mine >= 0, spot, -1)

    filtered = vmem_call(
        filter_kernel,
        (count, breadth, width),
        [
            ((2 * places, volume), BF16),
            ((2, breadth * 4, width), BF16),
            ((2, width, width), BF16),
            ((12 * breadth, width), BF16),
        ],
        "filter",
        count=count,
    )(got, filter_matrix)

    parts = [moved(filtered, -1, u) for u in uppers]
    keep, send = spread_call(where, filtered, par_row, weights, spread_third, groups)
    parts, keep, send = lax.optimization_barrier((parts, keep, send))
    parts = parts + [moved(part, 0, 1) for part in parts]
    came = moved(send, 0, 1)

    terms_out = []
    for u in uppers:
        at = u // 2 * count
        terms_out.append(moved(keep[at : at + count] + came[at : at + count], 1, u))
    pieces = [merge_call(where, filtered, parts, weights, merge_third, groups)] + terms_out
    tail = volume // LANES
    results = vmem_call(
        unfilter_kernel,
        (runs, capacity, volume),
        [
            ((3 * count * breadth, width), BF16),
            ((2, width, width), BF16),
            ((64, volume), BF16),
        ],
        "unfilter",
        in_specs=[
            pl.BlockSpec((runs, capacity, LANES), lambda i: (0, 0, tail)),
            pl.BlockSpec((breadth, breadth), lambda i: (0, 0)),
        ]
        + [pl.BlockSpec((count, breadth, width), lambda i: (0, 0, 0))] * len(pieces),
        count=count,
        pieces=len(pieces),
    )(got, filter_matrix, *pieces)
    back = lax.all_to_all(results, "row", split_axis=0, concat_axis=0, tiled=True)
    return vmem_call(unpack_kernel, (held, volume), [((3 * places, volume), BF16)], "unpack", **routing)(slot_row, back)


def solution(mesh):
    in_specs = (P(("row", "col"), None), P(("row", "col")), P("row", None), P(), P())
    out_specs = P(("row", "col"), None)
    return jax.shard_map(local, mesh=mesh, in_specs=in_specs, out_specs=out_specs, check_vma=False)
```

```python
import functools

import jax
import jax.numpy as jnp
import numpy as np
from jax import lax
from jax.experimental import pallas as pl
from jax.experimental.pallas import tpu as pltpu
from jax.sharding import PartitionSpec as P

F32, BF16 = jnp.float32, jnp.bfloat16
LANES = 128
PAD = 8


def iota(shape, axis):
    return lax.broadcasted_iota(jnp.int32, shape, axis)


def split(x):
    high = x.astype(BF16)
    return high, (x - high.astype(F32)).astype(BF16)


def product(a, b):
    return jnp.dot(a, b, preferred_element_type=F32)


def exact_expand(x, hot):
    one = jnp.where(hot, 1.0, 0.0).astype(BF16)
    total = None
    for part in range(3):
        head = x.astype(BF16)
        piece = product(head, one)
        total = piece if total is None else total + piece
        x = x - head.astype(F32)
    return total


def prepare_kernel(ops, first, second_high, second_low, merge, spread, *, groups):
    breadth = ops.shape[1]
    terms = ops.shape[0] // (9 * breadth)
    lo_count = LANES // breadth
    hi_count = breadth // lo_count
    per = terms // groups

    def factor(term, axis, k):
        at = ((term * 3 + axis) * 3 + k) * breadth
        return ops[at : at + breadth]

    blank = jnp.zeros((breadth, LANES - 3 * breadth), F32)
    for term in range(terms):
        for k in range(3):
            value = factor(term, 0, k)
            high = value.astype(BF16).astype(F32)
            line = jnp.concatenate([high, high, value - high, blank], axis=1)
            first[term * breadth : (term + 1) * breadth, k * LANES : (k + 1) * LANES] = line.astype(BF16)
        at = (term * 9 + 6) * breadth
        turned = ops[at : at + 3 * breadth].T
        for k in range(3):
            high, low = split(jnp.concatenate([turned[:, k * breadth : (k + 1) * breadth]] * lo_count, axis=1))
            second_high[term, k] = high
            second_low[term, k] = low
    for g in range(groups):
        for inner in range(lo_count):
            strip = [
                jnp.concatenate(
                    [factor(g * per + t, 1, k)[:, inner * hi_count : (inner + 1) * hi_count] for t in range(per)], axis=1
                )
                for k in range(3)
            ]
            high, low = split(jnp.concatenate([strip[1], strip[0]], axis=1))
            merge[g, inner * breadth : (inner + 1) * breadth] = high
            merge[g, LANES + inner * breadth : LANES + (inner + 1) * breadth] = low
            for s, k in enumerate((1, 2)):
                high = strip[k].astype(BF16).astype(F32)
                line = jnp.concatenate([high, high, strip[k] - high], axis=1)
                spread[g, s, inner * breadth : (inner + 1) * breadth] = line.astype(BF16)


def fill(xbuf, slot, block):
    breadth = block.shape[0]
    high, low = split(block)
    base = slot * LANES
    xbuf[base : base + breadth] = high
    xbuf[base + breadth : base + 2 * breadth] = low
    xbuf[base + 2 * breadth : base + 3 * breadth] = high


def place(ubuf, g, n, result):
    rows = result.shape[0]
    for h in range(result.shape[1] // LANES):
        ubuf[g, n, h, :rows] = result[:, h * LANES : (h + 1) * LANES]


def second_stage(ubuf, lbuf, tbuf, second_high, second_low, per, breadth, offsets, recipes, emit):
    volumes, count, hi_count, stride = ubuf.shape[:4]
    lo_count = LANES // breadth
    flat = ubuf.reshape(volumes * count * hi_count * stride, LANES)
    block_mask = iota((LANES, LANES), 0) // breadth == iota((LANES, LANES), 1) // breadth
    zero_block = jnp.zeros((LANES, LANES), BF16)

    def pair_body(pair, carry):
        for spot, k in enumerate(offsets):
            for half in range(2):
                term = pair * 2 + half
                high = jnp.concatenate([second_high[term, k]] * lo_count, axis=0)
                low = jnp.concatenate([second_low[term, k]] * lo_count, axis=0)
                high = jnp.where(block_mask, high, zero_block)
                low = jnp.where(block_mask, low, zero_block)
                tbuf[half, spot, :LANES, :LANES] = high
                tbuf[half, spot, LANES:, :LANES] = high
                tbuf[half, spot, :LANES, LANES:] = low
        for n in range(count):
            for half in range(2):
                term = pair * 2 + half
                for g in range(volumes):
                    base = (g * count + n) * hi_count * stride + term * breadth
                    for a in range(0, breadth, 2):
                        pieces = [flat[pl.ds(base + a + d, hi_count, stride=stride), :] for d in range(2)]
                        high, low = split(jnp.concatenate(pieces, axis=0))
                        at = a * hi_count
                        lbuf[half, g, at : at + 2 * hi_count, :LANES] = high
                        lbuf[half, g, at : at + 2 * hi_count, LANES:] = low
            results = []
            for half in range(2):
                line = []
                for recipe in recipes:
                    wide = None
                    for g, spot in recipe:
                        piece = product(lbuf[half, g], tbuf[half, spot])
                        wide = piece if wide is None else wide + piece
                    line.append(wide[:, :LANES] + wide[:, LANES:])
                results.append(line)
            for q in range(len(recipes)):
                for a in range(breadth):
                    both = jnp.concatenate(
                        [results[half][q][a * hi_count : (a + 1) * hi_count] for half in range(2)], axis=0
                    )
                    high, low = split(both)
                    emit(q, pair, (n * breadth + a) // 2, (a % 2) * LANES, high, low)
        return carry

    lax.fori_loop(0, per // 2, pair_body, 0)


def pick_diagonal(wide, breadth):
    lane_block = iota((breadth, wide.shape[1]), 1) % LANES // breadth
    total = wide[:breadth]
    for low in range(1, LANES // breadth):
        total = jnp.where(lane_block == low, wide[low * breadth : (low + 1) * breadth], total)
    return total


def turn_block(obuf, base, breadth, store):
    lo_count = LANES // breadth
    lane_of = iota((8, LANES), 1) // breadth
    for a in range(0, breadth, 8):
        for high in range(breadth // lo_count):
            level = [
                obuf[pl.ds(base + a * breadth + high * lo_count + low, 8, stride=breadth), :] for low in range(lo_count)
            ]
            step = 1
            while step < lo_count:
                own_side = (lane_of // step) % 2 == 0
                level = [
                    jnp.where(own_side, p, q) + pltpu.roll(jnp.where(own_side, q, p), step * breadth, 1)
                    for p, q in zip(level[::2], level[1::2])
                ]
                step *= 2
            store(a, high * LANES, level[0])


def merge_kernel(where, own, *refs, parts):
    sources = refs[:parts]
    first, second_high, second_low, third, out = refs[parts : parts + 5]
    vols, xbuf, ubuf, lbuf, tbuf, rbuf, obuf, sems = refs[parts + 5 :]
    count, breadth, width = own.shape
    per = first.shape[0] // breadth
    kgroup = per * breadth * breadth // LANES

    def copies(action):
        for n in range(count):
            for axis in range(3):
                slot = n * 3 + axis
                at = where[n, axis]
                start = 0
                for source in sources:
                    size = source.shape[0]

                    @pl.when((at >= start) & (at < start + size))
                    def _(source=source, start=start, slot=slot, at=at):
                        action(pltpu.make_async_copy(source.at[at - start], vols.at[slot], sems.at[slot]))

                    start += size

    group = pl.program_id(0)

    @pl.when(group == 0)
    def _():
        copies(lambda c: c.start())
        for n in range(count):
            for axis in range(3):

                @pl.when(where[n, axis] < 0)
                def _(slot=n * 3 + axis):
                    vols[slot] = jnp.zeros((breadth, width), F32)

        tbuf[...] = jnp.zeros(tbuf.shape, BF16)
        xbuf[...] = jnp.zeros(xbuf.shape, BF16)
        obuf[...] = jnp.zeros(obuf.shape, F32)
        copies(lambda c: c.wait())

    for n in range(count):
        fill(xbuf, 0, vols[n * 3])
        fill(xbuf, 1, own[n])
        place(ubuf, 0, n, product(first[:, : 2 * LANES], xbuf[...]))
        for g, axis in ((1, 2), (2, 1)):
            fill(xbuf, 0, vols[n * 3 + axis])
            place(ubuf, g, n, product(first[:, LANES : 2 * LANES], xbuf[:LANES]))

    def emit(q, pair, tile, lane, high, low):
        step = high.shape[0]
        row = pl.multiple_of(q * kgroup + pair * step, step)
        rbuf[tile, pl.ds(row, step), lane : lane + LANES] = high
        rbuf[tile, pl.ds(row + 2 * kgroup, step), lane : lane + LANES] = low

    second_stage(ubuf, lbuf, tbuf, second_high, second_low, per, breadth, (1, 0), (((0, 0), (1, 1)), ((2, 0),)), emit)

    def tile_body(tile, carry):
        wide = product(third[0], rbuf[tile, : 2 * kgroup])
        wide = wide[:LANES] + wide[LANES:] + product(third[0, :LANES], rbuf[tile, 2 * kgroup :])
        total = pick_diagonal(wide, breadth)
        for d in range(2):
            row = pl.multiple_of((tile * 2 + d) * breadth, breadth)
            obuf[pl.ds(row, breadth), :] = obuf[pl.ds(row, breadth), :] + total[:, d * LANES : (d + 1) * LANES]
        return carry

    lax.fori_loop(0, count * breadth // 2, tile_body, 0, unroll=True)

    @pl.when(group == pl.num_programs(0) - 1)
    def _():
        for n in range(count):

            def store(a, lane, value, n=n):
                out[n, a : a + 8, lane : lane + LANES] = value

            turn_block(obuf, n * breadth * breadth, breadth, store)


def spread_kernel(where, own, first, second_high, second_low, third, keep, send, *refs):
    xbuf, ubuf, lbuf, tbuf, rbuf, obuf, block = refs
    count, breadth, width = own.shape
    per = first.shape[0] // breadth
    kgroup = per * breadth * breadth // LANES
    half_slots = keep.shape[0]
    group = pl.program_id(0)

    @pl.when(group == 0)
    def _():
        keep[...] = jnp.zeros(keep.shape, F32)
        send[...] = jnp.zeros(send.shape, F32)
        tbuf[...] = jnp.zeros(tbuf.shape, BF16)
        xbuf[...] = jnp.zeros(xbuf.shape, BF16)
        obuf[...] = jnp.zeros(obuf.shape, F32)

    for n in range(count):
        fill(xbuf, 0, own[n])
        for g in range(2):
            place(ubuf, g, n, product(first[:, (1 + g) * LANES : (2 + g) * LANES], xbuf[...]))

    def emit(q, pair, tile, lane, high, low):
        step = high.shape[0]
        row = pl.multiple_of(q * 3 * kgroup + pair * step, step)
        rbuf[tile, pl.ds(row, step), lane : lane + LANES] = high
        rbuf[tile, pl.ds(row + kgroup, step), lane : lane + LANES] = low
        rbuf[tile, pl.ds(row + 2 * kgroup, step), lane : lane + LANES] = high

    recipes = (((1, 0),), ((0, 0),), ((0, 1),))
    second_stage(ubuf, lbuf, tbuf, second_high, second_low, per, breadth, (1, 2), recipes, emit)

    def tile_body(tile, carry):
        for q in range(3):
            wide = product(third[0, 1 if q == 1 else 0], rbuf[tile, q * 3 * kgroup : (q + 1) * 3 * kgroup])
            total = pick_diagonal(wide, breadth)
            for d in range(2):
                row = pl.multiple_of((tile * 2 + d) * breadth, breadth)
                obuf[q, pl.ds(row, breadth), :] = (
                    obuf[q, pl.ds(row, breadth), :] + total[:, d * LANES : (d + 1) * LANES]
                )
        return carry

    lax.fori_loop(0, count * breadth // 2, tile_body, 0, unroll=True)

    @pl.when(group == pl.num_programs(0) - 1)
    def _():
        for n in range(count):
            for q in range(3):

                def store(a, lane, value):
                    block[a : a + 8, lane : lane + LANES] = value

                turn_block(obuf.at[q], n * breadth * breadth, breadth, store)
                slot = where[n, q]

                @pl.when((slot >= 0) & (slot < half_slots))
                def _(slot=slot):
                    keep[slot] = keep[slot] + block[...]

                @pl.when(slot >= half_slots)
                def _(slot=slot):
                    send[slot - half_slots] = send[slot - half_slots] + block[...]


def whole_spec(array):
    return pl.BlockSpec(array.shape, lambda i, w, rank=len(array.shape): (0,) * rank)


def group_spec(array, size):
    rank = len(array.shape)
    return pl.BlockSpec((size,) + array.shape[1:], lambda i, w: (i,) + (0,) * (rank - 1))


def stage_scratch(volumes, recipes, thick, count, breadth, width, per):
    hi_count = breadth * breadth // LANES
    return [
        pltpu.VMEM((volumes, count, hi_count, per * breadth + PAD, LANES), F32),
        pltpu.VMEM((2, volumes, breadth * hi_count, 2 * LANES), BF16),
        pltpu.VMEM((2, 2, 2 * LANES, 2 * LANES), BF16),
        pltpu.VMEM((count * breadth // 2, recipes * thick * per * hi_count, 2 * LANES), BF16),
    ]


def cost(count, breadth, per, units):
    return pl.CostEstimate(flops=units * per * 2 * count * breadth**4 * 200, transcendentals=0, bytes_accessed=1 << 22)


def stage_call(kernel, name, where, own, extra, extra_specs, weights, third, groups, out_shapes, scratch, units):
    first, second_high, second_low = weights
    breadth = own.shape[1]
    terms = second_high.shape[0]
    per = terms // groups
    return pl.pallas_call(
        kernel,
        out_shape=out_shapes,
        grid_spec=pltpu.PrefetchScalarGridSpec(
            num_scalar_prefetch=1,
            grid=(groups,),
            in_specs=[whole_spec(own)]
            + extra_specs
            + [
                group_spec(first, per * breadth),
                group_spec(second_high, per),
                group_spec(second_low, per),
                group_spec(third, 1),
            ],
            out_specs=[whole_spec(shape) for shape in out_shapes],
            scratch_shapes=scratch,
        ),
        compiler_params=pltpu.CompilerParams(dimension_semantics=("arbitrary",), vmem_limit_bytes=30 << 20),
        cost_estimate=cost(own.shape[0], breadth, terms, units),
        name=name,
    )(where, own, *extra, first, second_high, second_low, third)


def merge_call(where, own, parts, weights, third, groups):
    count, breadth, width = own.shape
    per = weights[1].shape[0] // groups
    scratch = stage_scratch(3, 2, 2, count, breadth, width, per)
    scratch = (
        [pltpu.VMEM((count * 3, breadth, width), F32), pltpu.VMEM((2 * LANES, width), BF16)]
        + scratch
        + [pltpu.VMEM((count * breadth * breadth, LANES), F32), pltpu.SemaphoreType.DMA((count * 3,))]
    )
    return stage_call(
        functools.partial(merge_kernel, parts=len(parts)),
        "merge",
        where,
        own,
        list(parts),
        [pl.BlockSpec(memory_space=pl.ANY)] * len(parts),
        weights,
        third,
        groups,
        [jax.ShapeDtypeStruct(own.shape, F32)],
        scratch,
        9,
    )[0]


def spread_call(where, own, slots, weights, third, groups):
    count, breadth, width = own.shape
    per = weights[1].shape[0] // groups
    scratch = stage_scratch(2, 3, 3, count, breadth, width, per)
    scratch = (
        [pltpu.VMEM((LANES, width), BF16)]
        + scratch
        + [pltpu.VMEM((3, count * breadth * breadth, LANES), F32), pltpu.VMEM((breadth, width), F32)]
    )
    shape = jax.ShapeDtypeStruct((slots // 2, breadth, width), F32)
    return stage_call(
        spread_kernel,
        "spread",
        where,
        own,
        [],
        [],
        weights,
        third,
        groups,
        [shape, shape],
        scratch,
        8,
    )


def to_row(column):
    size = column.shape[0]
    diagonal = iota((size, size), 0) == iota((size, size), 1)
    return jnp.sum(jnp.where(diagonal, column, 0.0), axis=0, keepdims=True)


def to_column(row):
    size = row.shape[1]
    diagonal = iota((size, size), 0) == iota((size, size), 1)
    return jnp.sum(jnp.where(diagonal, row, 0.0), axis=1, keepdims=True)


def place_row(slot_row, runs, run_size, capacity):
    held = slot_row.shape[1]
    run_row = jnp.zeros(slot_row.shape, F32)
    for r in range(1, runs):
        run_row = run_row + jnp.where(slot_row >= r * run_size, 1.0, 0.0)
    same = to_column(run_row) == run_row
    earlier = iota((held, held), 0) < iota((held, held), 1)
    before = jnp.sum(jnp.where(same & earlier, 1.0, 0.0), axis=0, keepdims=True)
    return run_row * capacity + before


def pack_kernel(slot_row, fine, out, stack, *, runs, run_size):
    held, volume = fine.shape
    capacity = out.shape[1]
    places = runs * capacity
    slots = slot_row[...]
    place = place_row(slots, runs, run_size, capacity)
    hit = iota((places, held), 0).astype(F32) == place
    ids = jnp.sum(jnp.where(hit, slots.astype(F32) + 1.0, 0.0), axis=1, keepdims=True)
    ids = jnp.broadcast_to(ids, (places, LANES))
    one = jnp.where(hit, 1.0, 0.0).astype(BF16)
    rest = fine[...]
    for part in range(3):
        head = rest.astype(BF16)
        stack[part * held : (part + 1) * held] = head
        rest = rest - head.astype(F32)
    packed = product(jnp.concatenate([one] * 3, axis=1), stack[...])
    for r in range(runs):
        out[r, :, :volume] = packed[r * capacity : (r + 1) * capacity]
        out[r, :, volume:] = ids[r * capacity : (r + 1) * capacity]


def unpack_kernel(slot_row, back, out, stack, *, run_size):
    held, volume = out.shape
    runs, capacity = back.shape[:2]
    places = runs * capacity
    place = to_column(place_row(slot_row[...], runs, run_size, capacity))
    hit = iota((held, places), 1).astype(F32) == place
    one = jnp.where(hit, 1.0, 0.0).astype(BF16)
    rest = jnp.concatenate([back[r] for r in range(runs)], axis=0)
    for part in range(3):
        head = rest.astype(BF16)
        stack[part * places : (part + 1) * places] = head
        rest = rest - head.astype(F32)
    out[...] = product(jnp.concatenate([one] * 3, axis=1), stack[...])


def child_code(ids, held):
    at = ids - 1.0
    return jnp.where(at < 0.0, -1.0, at - held * jnp.floor(at / held))


def row_code(index, count):
    inner = index & 7
    code = (inner >> 1) * 8 + (inner & 1) * 4 + (index >> 3)
    return jnp.where(inner < 2 * count, code.astype(F32), -2.0)


def child_rows(filter_matrix, count):
    breadth = filter_matrix.shape[0]
    half = breadth // 2
    lane = iota((breadth, half * 8), 1)
    inner = lane & 7
    hot = iota((breadth, half * 8), 0) == (inner & 1) * half + (lane >> 3)
    spread = exact_expand(filter_matrix, hot)
    return jnp.concatenate([jnp.where(inner >> 1 == n, spread, 0.0) for n in range(count)], axis=0)


def triple_lanes(x):
    high, low = split(x)
    return jnp.concatenate([high, high, low], axis=1)


def filter_kernel(got, filter_ref, out, stack, lines, cross, weave, *, count):
    runs, capacity, volume = got.shape
    volume = volume - LANES
    places = runs * capacity
    breadth = filter_ref.shape[0]
    half = breadth // 2
    width = out.shape[2]
    face = width // 4
    span = volume // face
    lo_count = LANES // breadth
    hi_count = breadth // lo_count
    matrix = filter_ref[...]
    turned = matrix.T
    lane = iota((breadth, width), 1)
    outer = lane // breadth
    across_z = exact_expand(turned, iota((breadth, width), 0) == lane % breadth)
    across_y = exact_expand(turned, iota((breadth, width), 0) == (outer % lo_count) * hi_count + outer // lo_count)
    for g in range(4):
        zs = across_z[(g & 1) * half : (g & 1) * half + half]
        for j in range(half):
            row = (g >> 1) * half + j
            high, low = split(zs * across_y[row : row + 1])
            at = (g * half + j) * half
            cross[0, at : at + half] = high
            cross[1, at : at + half] = low
    joined = jnp.concatenate([got[r] for r in range(runs)], axis=0)
    code = to_row(child_code(joined[:, volume : volume + 1], 8 * count))
    hit = row_code(iota((32, places), 0), count) == code
    one = jnp.where(hit, 1.0, 0.0).astype(BF16)
    high, low = split(joined[:, :volume])
    stack[:places] = high
    stack[places:] = low
    boxes = product(jnp.concatenate([one, one], axis=1), stack[...])
    for g in range(4):
        for i in range(0, span, 2):
            both = jnp.concatenate(
                [boxes[g * 8 : g * 8 + 8, (i + d) * face : (i + d + 1) * face] for d in range(2)], axis=0
            )
            high, low = split(both)
            lines[0, i * 8 : i * 8 + 16, g * face : (g + 1) * face] = high
            lines[1, i * 8 : i * 8 + 16, g * face : (g + 1) * face] = low
    total = product(lines[0], cross[0]) + product(lines[1], cross[0]) + product(lines[0], cross[1])
    high, low = split(total)
    size = total.shape[0]
    weave[:size] = high
    weave[size : 2 * size] = low
    weave[2 * size :] = high
    result = product(triple_lanes(child_rows(matrix, count)), weave[...])
    for n in range(count):
        out[n] = result[n * breadth : (n + 1) * breadth]


def unfilter_kernel(got, filter_ref, *refs, count, pieces):
    applied = refs[:pieces]
    out, weave, cross, stack = refs[pieces:]
    runs, capacity, volume = out.shape
    places = runs * capacity
    breadth = filter_ref.shape[0]
    half = breadth // 2
    width = applied[0].shape[2]
    face = width // 4
    size = count * breadth
    matrix = filter_ref[...]
    lane = iota((breadth, width), 1)
    octant = lane // face
    across_c = exact_expand(matrix, iota((breadth, width), 0) == octant % 2 * half + lane % half)
    across_b = exact_expand(matrix, iota((breadth, width), 0) == octant // 2 * half + lane // half % half)
    for b in range(breadth):
        high, low = split(across_c * across_b[b : b + 1])
        cross[0, b * breadth : (b + 1) * breadth] = high
        cross[1, b * breadth : (b + 1) * breadth] = low
    for n in range(count):
        total = applied[0][n]
        for piece in applied[1:]:
            total = total + piece[n]
        high, low = split(total)
        at = n * breadth
        weave[at : at + breadth] = high
        weave[size + at : size + at + breadth] = low
        weave[2 * size + at : 2 * size + at + breadth] = high
    lines = product(triple_lanes(child_rows(matrix, count).T), weave[...])
    high, low = split(lines)
    total = product(high, cross[0]) + product(low, cross[0]) + product(high, cross[1])
    for g in range(0, 4, 2):
        for i in range(total.shape[0] // 8):
            both = jnp.concatenate(
                [total[i * 8 : i * 8 + 8, (g + d) * face : (g + d + 1) * face] for d in range(2)], axis=0
            )
            high, low = split(both)
            stack[g * 8 : g * 8 + 16, i * face : (i + 1) * face] = high
            stack[32 + g * 8 : 32 + g * 8 + 16, i * face : (i + 1) * face] = low
    ids = jnp.concatenate([got[r] for r in range(runs)], axis=0)
    code = child_code(ids[:, :1], 8 * count)
    hit = row_code(iota((places, 32), 1), count) == code
    one = jnp.where(hit, 1.0, 0.0).astype(BF16)
    packed = product(jnp.concatenate([one, one], axis=1), stack[...])
    for r in range(runs):
        out[r] = packed[r * capacity : (r + 1) * capacity]


def vmem_call(kernel, out_shape, scratch, name, in_specs=None, **settings):
    extra = {} if in_specs is None else dict(grid=(1,), in_specs=in_specs)
    if in_specs is not None:
        rank = len(out_shape)
        extra["out_specs"] = pl.BlockSpec(out_shape, lambda i: (0,) * rank)
    return pl.pallas_call(
        functools.partial(kernel, **settings),
        out_shape=jax.ShapeDtypeStruct(out_shape, F32),
        scratch_shapes=[pltpu.VMEM(shape, dtype) for shape, dtype in scratch],
        compiler_params=pltpu.CompilerParams(vmem_limit_bytes=30 << 20),
        name=name,
        **extra,
    )


def moved(array, row_step, bit):
    rows = lax.axis_size("row")
    cols = lax.axis_size("col")
    pairs = [
        (r * cols + c, (r + row_step) % rows * cols + (c ^ bit)) for r in range(rows) for c in range(cols)
    ]
    return lax.ppermute(array, ("row", "col"), pairs)


def local(fine_coeffs, fine_slot, neighbours, filter_matrix, kernel_ops):
    breadth = filter_matrix.shape[0]
    terms = kernel_ops.shape[0]
    runs = lax.axis_size("row")
    cols = lax.axis_size("col")
    held, volume = fine_coeffs.shape
    par_row = neighbours.shape[0]
    count = held // 8
    capacity = 2 * (held // runs)
    places = runs * capacity
    width = breadth * breadth
    hi_count = width // LANES
    groups = 2
    per = terms // groups
    uppers = range(0, cols, 2)

    slot_row = fine_slot.reshape(1, held)
    routing = dict(run_size=8 * par_row)
    sent = vmem_call(
        pack_kernel, (runs, capacity, volume + LANES), [((3 * held, volume), BF16)], "pack", runs=runs, **routing
    )(slot_row, fine_coeffs)
    got = lax.all_to_all(sent, "row", split_axis=0, concat_axis=0, tiled=True)

    first, second_high, second_low, merge_third, spread_third = pl.pallas_call(
        functools.partial(prepare_kernel, groups=groups),
        out_shape=[
            jax.ShapeDtypeStruct((terms * breadth, 3 * LANES), BF16),
            jax.ShapeDtypeStruct((terms, 3, breadth, LANES), BF16),
            jax.ShapeDtypeStruct((terms, 3, breadth, LANES), BF16),
            jax.ShapeDtypeStruct((groups, 2 * LANES, 2 * per * hi_count), BF16),
            jax.ShapeDtypeStruct((groups, 2, LANES, 3 * per * hi_count), BF16),
        ],
        compiler_params=pltpu.CompilerParams(vmem_limit_bytes=30 << 20),
        name="prepare",
    )(kernel_ops.reshape(terms * 9 * breadth, breadth))
    weights = (first, second_high, second_low)

    col_index = lax.axis_index("col")
    mine = lax.dynamic_slice_in_dim(neighbours, col_index * count, count, 0)[:, ::2]
    within = mine % par_row
    relation = (within // count) ^ col_index
    spot = (relation % 2) * (len(uppers) * count) + relation // 2 * count + within % count
    where = jnp.where(mine >= 0, spot, -1)

    filtered = vmem_call(
        filter_kernel,
        (count, breadth, width),
        [
            ((2 * places, volume), BF16),
            ((2, breadth * 4, width), BF16),
            ((2, width, width), BF16),
            ((12 * breadth, width), BF16),
        ],
        "filter",
        count=count,
    )(got, filter_matrix)

    parts = [moved(filtered, -1, u) for u in uppers]
    keep, send = spread_call(where, filtered, par_row, weights, spread_third, groups)
    parts, keep, send = lax.optimization_barrier((parts, keep, send))
    parts = parts + [moved(part, 0, 1) for part in parts]
    came = moved(send, 0, 1)

    terms_out = []
    for u in uppers:
        at = u // 2 * count
        terms_out.append(moved(keep[at : at + count] + came[at : at + count], 1, u))
    pieces = [merge_call(where, filtered, parts, weights, merge_third, groups)] + terms_out
    tail = volume // LANES
    results = vmem_call(
        unfilter_kernel,
        (runs, capacity, volume),
        [
            ((3 * count * breadth, width), BF16),
            ((2, width, width), BF16),
            ((64, volume), BF16),
        ],
        "unfilter",
        in_specs=[
            pl.BlockSpec((runs, capacity, LANES), lambda i: (0, 0, tail)),
            pl.BlockSpec((breadth, breadth), lambda i: (0, 0)),
        ]
        + [pl.BlockSpec((count, breadth, width), lambda i: (0, 0, 0))] * len(pieces),
        count=count,
        pieces=len(pieces),
    )(got, filter_matrix, *pieces)
    back = lax.all_to_all(results, "row", split_axis=0, concat_axis=0, tiled=True)
    return vmem_call(unpack_kernel, (held, volume), [((3 * places, volume), BF16)], "unpack", **routing)(slot_row, back)


def solution(mesh):
    in_specs = (P(("row", "col"), None), P(("row", "col")), P("row", None), P(), P())
    out_specs = P(("row", "col"), None)
    return jax.shard_map(local, mesh=mesh, in_specs=in_specs, out_specs=out_specs, check_vma=False)
```

```python
import functools

import jax
import jax.numpy as jnp
import numpy as np
from jax import lax
from jax.experimental import pallas as pl
from jax.experimental.pallas import tpu as pltpu
from jax.sharding import PartitionSpec as P

F32, BF16 = jnp.float32, jnp.bfloat16
LANES = 128
PAD = 8


def iota(shape, axis):
    return lax.broadcasted_iota(jnp.int32, shape, axis)


def split(x):
    high = x.astype(BF16)
    return high, (x - high.astype(F32)).astype(BF16)


def product(a, b):
    return jnp.dot(a, b, preferred_element_type=F32)


def exact_expand(x, hot):
    one = jnp.where(hot, 1.0, 0.0).astype(BF16)
    total = None
    for part in range(3):
        head = x.astype(BF16)
        piece = product(head, one)
        total = piece if total is None else total + piece
        x = x - head.astype(F32)
    return total


def prepare_kernel(ops, first, second_high, second_low, merge, spread, *, groups):
    breadth = ops.shape[1]
    terms = ops.shape[0] // (9 * breadth)
    lo_count = LANES // breadth
    hi_count = breadth // lo_count
    per = terms // groups

    def factor(term, axis, k):
        at = ((term * 3 + axis) * 3 + k) * breadth
        return ops[at : at + breadth]

    blank = jnp.zeros((breadth, LANES - 3 * breadth), F32)
    for term in range(terms):
        for k in range(3):
            value = factor(term, 0, k)
            high = value.astype(BF16).astype(F32)
            line = jnp.concatenate([high, high, value - high, blank], axis=1)
            first[term * breadth : (term + 1) * breadth, k * LANES : (k + 1) * LANES] = line.astype(BF16)
        at = (term * 9 + 6) * breadth
        turned = ops[at : at + 3 * breadth].T
        for k in range(3):
            high, low = split(jnp.concatenate([turned[:, k * breadth : (k + 1) * breadth]] * lo_count, axis=1))
            second_high[term, k] = high
            second_low[term, k] = low
    for g in range(groups):
        for inner in range(lo_count):
            strip = [
                jnp.concatenate(
                    [factor(g * per + t, 1, k)[:, inner * hi_count : (inner + 1) * hi_count] for t in range(per)], axis=1
                )
                for k in range(3)
            ]
            high, low = split(jnp.concatenate([strip[1], strip[0]], axis=1))
            merge[g, inner * breadth : (inner + 1) * breadth] = high
            merge[g, LANES + inner * breadth : LANES + (inner + 1) * breadth] = low
            for s, k in enumerate((1, 2)):
                high = strip[k].astype(BF16).astype(F32)
                line = jnp.concatenate([high, high, strip[k] - high], axis=1)
                spread[g, s, inner * breadth : (inner + 1) * breadth] = line.astype(BF16)


class Loader:
    def __init__(self, sources, targets, sems):
        self.copies = [pltpu.make_async_copy(a, b, sems.at[i]) for i, (a, b) in enumerate(zip(sources, targets))]

    def start(self):
        for copy in self.copies:
            copy.start()

    def wait(self, chosen):
        for i in chosen:
            self.copies[i].wait()


def fill(xbuf, slot, block):
    breadth = block.shape[0]
    high, low = split(block)
    base = slot * LANES
    xbuf[base : base + breadth] = high
    xbuf[base + breadth : base + 2 * breadth] = low
    xbuf[base + 2 * breadth : base + 3 * breadth] = high


def place(ubuf, g, n, result):
    rows = result.shape[0]
    for h in range(result.shape[1] // LANES):
        ubuf[g, n, h, :rows] = result[:, h * LANES : (h + 1) * LANES]


def second_stage(ubuf, lbuf, tbuf, second_high, second_low, group, per, breadth, offsets, recipes, emit):
    volumes, count, hi_count, stride = ubuf.shape[:4]
    lo_count = LANES // breadth
    flat = ubuf.reshape(volumes * count * hi_count * stride, LANES)
    block_mask = iota((LANES, LANES), 0) // breadth == iota((LANES, LANES), 1) // breadth
    zero_block = jnp.zeros((LANES, LANES), BF16)

    def pair_body(pair, carry):
        for spot, k in enumerate(offsets):
            for half in range(2):
                term = group * per + pair * 2 + half
                high = jnp.concatenate([second_high[term, k]] * lo_count, axis=0)
                low = jnp.concatenate([second_low[term, k]] * lo_count, axis=0)
                high = jnp.where(block_mask, high, zero_block)
                low = jnp.where(block_mask, low, zero_block)
                tbuf[half, spot, :LANES, :LANES] = high
                tbuf[half, spot, LANES:, :LANES] = high
                tbuf[half, spot, :LANES, LANES:] = low
        for n in range(count):
            for half in range(2):
                term = pair * 2 + half
                for g in range(volumes):
                    base = (g * count + n) * hi_count * stride + term * breadth
                    for a in range(0, breadth, 2):
                        pieces = [flat[pl.ds(base + a + d, hi_count, stride=stride), :] for d in range(2)]
                        high, low = split(jnp.concatenate(pieces, axis=0))
                        at = a * hi_count
                        lbuf[half, g, at : at + 2 * hi_count, :LANES] = high
                        lbuf[half, g, at : at + 2 * hi_count, LANES:] = low
            results = []
            for half in range(2):
                line = []
                for recipe in recipes:
                    wide = None
                    for g, spot in recipe:
                        piece = product(lbuf[half, g], tbuf[half, spot])
                        wide = piece if wide is None else wide + piece
                    line.append(wide[:, :LANES] + wide[:, LANES:])
                results.append(line)
            for q in range(len(recipes)):
                for a in range(breadth):
                    both = jnp.concatenate(
                        [results[half][q][a * hi_count : (a + 1) * hi_count] for half in range(2)], axis=0
                    )
                    high, low = split(both)
                    emit(q, pair, (n * breadth + a) // 2, (a % 2) * LANES, high, low)
        return carry

    lax.fori_loop(0, per // 2, pair_body, 0)


def pick_diagonal(wide, breadth):
    lane_block = iota((breadth, wide.shape[1]), 1) % LANES // breadth
    total = wide[:breadth]
    for low in range(1, LANES // breadth):
        total = jnp.where(lane_block == low, wide[low * breadth : (low + 1) * breadth], total)
    return total


def turn_block(obuf, base, breadth, store):
    lo_count = LANES // breadth
    lane_of = iota((8, LANES), 1) // breadth
    for a in range(0, breadth, 8):
        for high in range(breadth // lo_count):
            level = [
                obuf[pl.ds(base + a * breadth + high * lo_count + low, 8, stride=breadth), :] for low in range(lo_count)
            ]
            step = 1
            while step < lo_count:
                own_side = (lane_of // step) % 2 == 0
                level = [
                    jnp.where(own_side, p, q) + pltpu.roll(jnp.where(own_side, q, p), step * breadth, 1)
                    for p, q in zip(level[::2], level[1::2])
                ]
                step *= 2
            store(a, high * LANES, level[0])


def merge_kernel(where, own, *refs, parts):
    sources = refs[:parts]
    remote = refs[parts : parts + 4]
    out = refs[parts + 4]
    first, second_high, second_low, third, weight_sems = refs[parts + 5 : parts + 10]
    vols, xbuf, ubuf, lbuf, tbuf, rbuf, obuf, sems = refs[parts + 10 :]
    loader = Loader(remote, (first, second_high, second_low, third), weight_sems)
    count, breadth, width = own.shape
    rows = first.shape[0] // third.shape[0]
    per = rows // breadth
    kgroup = per * breadth * breadth // LANES

    def copies(action):
        for n in range(count):
            for axis in range(3):
                slot = n * 3 + axis
                at = where[n, axis]
                start = 0
                for source in sources:
                    size = source.shape[0]

                    @pl.when((at >= start) & (at < start + size))
                    def _(source=source, start=start, slot=slot, at=at):
                        action(pltpu.make_async_copy(source.at[at - start], vols.at[slot], sems.at[slot]))

                    start += size

    group = pl.program_id(0)

    @pl.when(group == 0)
    def _():
        copies(lambda c: c.start())
        loader.start()
        for n in range(count):
            for axis in range(3):

                @pl.when(where[n, axis] < 0)
                def _(slot=n * 3 + axis):
                    vols[slot] = jnp.zeros((breadth, width), F32)

        tbuf[...] = jnp.zeros(tbuf.shape, BF16)
        xbuf[...] = jnp.zeros(xbuf.shape, BF16)
        obuf[...] = jnp.zeros(obuf.shape, F32)
        copies(lambda c: c.wait())
        loader.wait((0,))

    top = pl.multiple_of(group * rows, 8)
    for n in range(count):
        fill(xbuf, 0, vols[n * 3])
        fill(xbuf, 1, own[n])
        place(ubuf, 0, n, product(first[pl.ds(top, rows), : 2 * LANES], xbuf[...]))
        for g, axis in ((1, 2), (2, 1)):
            fill(xbuf, 0, vols[n * 3 + axis])
            place(ubuf, g, n, product(first[pl.ds(top, rows), LANES : 2 * LANES], xbuf[:LANES]))

    @pl.when(group == 0)
    def _():
        loader.wait((1, 2, 3))

    def emit(q, pair, tile, lane, high, low):
        step = high.shape[0]
        row = pl.multiple_of(q * kgroup + pair * step, step)
        rbuf[tile, pl.ds(row, step), lane : lane + LANES] = high
        rbuf[tile, pl.ds(row + 2 * kgroup, step), lane : lane + LANES] = low

    second_stage(
        ubuf, lbuf, tbuf, second_high, second_low, group, per, breadth, (1, 0), (((0, 0), (1, 1)), ((2, 0),)), emit
    )

    def tile_body(tile, carry):
        wide = product(third[group], rbuf[tile, : 2 * kgroup])
        wide = wide[:LANES] + wide[LANES:] + product(third[group, :LANES], rbuf[tile, 2 * kgroup :])
        total = pick_diagonal(wide, breadth)
        for d in range(2):
            row = pl.multiple_of((tile * 2 + d) * breadth, breadth)
            obuf[pl.ds(row, breadth), :] = obuf[pl.ds(row, breadth), :] + total[:, d * LANES : (d + 1) * LANES]
        return carry

    lax.fori_loop(0, count * breadth // 2, tile_body, 0, unroll=True)

    @pl.when(group == pl.num_programs(0) - 1)
    def _():
        for n in range(count):

            def store(a, lane, value, n=n):
                out[n, a : a + 8, lane : lane + LANES] = value

            turn_block(obuf, n * breadth * breadth, breadth, store)


def spread_kernel(where, own, *refs):
    remote = refs[:4]
    keep, send, first, second_high, second_low, third, weight_sems = refs[4:11]
    xbuf, ubuf, lbuf, tbuf, rbuf, obuf, block = refs[11:]
    loader = Loader(remote, (first, second_high, second_low, third), weight_sems)
    count, breadth, width = own.shape
    rows = first.shape[0] // third.shape[0]
    per = rows // breadth
    kgroup = per * breadth * breadth // LANES
    half_slots = keep.shape[0]
    group = pl.program_id(0)

    @pl.when(group == 0)
    def _():
        loader.start()
        keep[...] = jnp.zeros(keep.shape, F32)
        send[...] = jnp.zeros(send.shape, F32)
        tbuf[...] = jnp.zeros(tbuf.shape, BF16)
        xbuf[...] = jnp.zeros(xbuf.shape, BF16)
        obuf[...] = jnp.zeros(obuf.shape, F32)
        loader.wait((0,))

    top = pl.multiple_of(group * rows, 8)
    for n in range(count):
        fill(xbuf, 0, own[n])
        for g in range(2):
            place(ubuf, g, n, product(first[pl.ds(top, rows), (1 + g) * LANES : (2 + g) * LANES], xbuf[...]))

    @pl.when(group == 0)
    def _():
        loader.wait((1, 2, 3))

    def emit(q, pair, tile, lane, high, low):
        step = high.shape[0]
        row = pl.multiple_of(q * 3 * kgroup + pair * step, step)
        rbuf[tile, pl.ds(row, step), lane : lane + LANES] = high
        rbuf[tile, pl.ds(row + kgroup, step), lane : lane + LANES] = low
        rbuf[tile, pl.ds(row + 2 * kgroup, step), lane : lane + LANES] = high

    recipes = (((1, 0),), ((0, 0),), ((0, 1),))
    second_stage(ubuf, lbuf, tbuf, second_high, second_low, group, per, breadth, (1, 2), recipes, emit)

    def tile_body(tile, carry):
        for q in range(3):
            wide = product(third[group, 1 if q == 1 else 0], rbuf[tile, q * 3 * kgroup : (q + 1) * 3 * kgroup])
            total = pick_diagonal(wide, breadth)
            for d in range(2):
                row = pl.multiple_of((tile * 2 + d) * breadth, breadth)
                obuf[q, pl.ds(row, breadth), :] = (
                    obuf[q, pl.ds(row, breadth), :] + total[:, d * LANES : (d + 1) * LANES]
                )
        return carry

    lax.fori_loop(0, count * breadth // 2, tile_body, 0, unroll=True)

    @pl.when(group == pl.num_programs(0) - 1)
    def _():
        for n in range(count):
            for q in range(3):

                def store(a, lane, value):
                    block[a : a + 8, lane : lane + LANES] = value

                turn_block(obuf.at[q], n * breadth * breadth, breadth, store)
                slot = where[n, q]

                @pl.when((slot >= 0) & (slot < half_slots))
                def _(slot=slot):
                    keep[slot] = keep[slot] + block[...]

                @pl.when(slot >= half_slots)
                def _(slot=slot):
                    send[slot - half_slots] = send[slot - half_slots] + block[...]


def whole_spec(array):
    return pl.BlockSpec(array.shape, lambda i, w, rank=len(array.shape): (0,) * rank)


def stage_scratch(volumes, recipes, thick, count, breadth, width, per):
    hi_count = breadth * breadth // LANES
    return [
        pltpu.VMEM((volumes, count, hi_count, per * breadth + PAD, LANES), F32),
        pltpu.VMEM((2, volumes, breadth * hi_count, 2 * LANES), BF16),
        pltpu.VMEM((2, 2, 2 * LANES, 2 * LANES), BF16),
        pltpu.VMEM((count * breadth // 2, recipes * thick * per * hi_count, 2 * LANES), BF16),
    ]


def cost(count, breadth, per, units):
    return pl.CostEstimate(flops=units * per * 2 * count * breadth**4 * 200, transcendentals=0, bytes_accessed=1 << 22)


def stage_call(kernel, name, where, own, extra, extra_specs, weights, third, groups, out_shapes, scratch, units):
    first, second_high, second_low = weights
    breadth = own.shape[1]
    terms = second_high.shape[0]
    per = terms // groups
    return pl.pallas_call(
        kernel,
        out_shape=out_shapes,
        grid_spec=pltpu.PrefetchScalarGridSpec(
            num_scalar_prefetch=1,
            grid=(groups,),
            in_specs=[whole_spec(own)]
            + extra_specs
            + [pl.BlockSpec(memory_space=pltpu.HBM)] * 4,
            out_specs=[whole_spec(shape) for shape in out_shapes],
            scratch_shapes=[pltpu.VMEM(array.shape, BF16) for array in (first, second_high, second_low, third)]
            + [pltpu.SemaphoreType.DMA((4,))]
            + scratch,
        ),
        compiler_params=pltpu.CompilerParams(dimension_semantics=("arbitrary",), vmem_limit_bytes=30 << 20),
        cost_estimate=cost(own.shape[0], breadth, terms, units),
        name=name,
    )(where, own, *extra, *[pltpu.with_memory_space_constraint(w, pltpu.HBM) for w in (first, second_high, second_low, third)])


def merge_call(where, own, parts, weights, third, groups):
    count, breadth, width = own.shape
    per = weights[1].shape[0] // groups
    scratch = stage_scratch(3, 2, 2, count, breadth, width, per)
    scratch = (
        [pltpu.VMEM((count * 3, breadth, width), F32), pltpu.VMEM((2 * LANES, width), BF16)]
        + scratch
        + [pltpu.VMEM((count * breadth * breadth, LANES), F32), pltpu.SemaphoreType.DMA((count * 3,))]
    )
    return stage_call(
        functools.partial(merge_kernel, parts=len(parts)),
        "merge",
        where,
        own,
        list(parts),
        [pl.BlockSpec(memory_space=pl.ANY)] * len(parts),
        weights,
        third,
        groups,
        [jax.ShapeDtypeStruct(own.shape, F32)],
        scratch,
        9,
    )[0]


def spread_call(where, own, slots, weights, third, groups):
    count, breadth, width = own.shape
    per = weights[1].shape[0] // groups
    scratch = stage_scratch(2, 3, 3, count, breadth, width, per)
    scratch = (
        [pltpu.VMEM((LANES, width), BF16)]
        + scratch
        + [pltpu.VMEM((3, count * breadth * breadth, LANES), F32), pltpu.VMEM((breadth, width), F32)]
    )
    shape = jax.ShapeDtypeStruct((slots // 2, breadth, width), F32)
    return stage_call(
        spread_kernel,
        "spread",
        where,
        own,
        [],
        [],
        weights,
        third,
        groups,
        [shape, shape],
        scratch,
        8,
    )


def to_row(column):
    size = column.shape[0]
    diagonal = iota((size, size), 0) == iota((size, size), 1)
    return jnp.sum(jnp.where(diagonal, column, 0.0), axis=0, keepdims=True)


def to_column(row):
    size = row.shape[1]
    diagonal = iota((size, size), 0) == iota((size, size), 1)
    return jnp.sum(jnp.where(diagonal, row, 0.0), axis=1, keepdims=True)


def place_row(slot_row, runs, run_size, capacity):
    held = slot_row.shape[1]
    run_row = jnp.zeros(slot_row.shape, F32)
    for r in range(1, runs):
        run_row = run_row + jnp.where(slot_row >= r * run_size, 1.0, 0.0)
    same = to_column(run_row) == run_row
    earlier = iota((held, held), 0) < iota((held, held), 1)
    before = jnp.sum(jnp.where(same & earlier, 1.0, 0.0), axis=0, keepdims=True)
    return run_row * capacity + before


def pack_kernel(slot_row, fine, out, stack, *, runs, run_size):
    held, volume = fine.shape
    capacity = out.shape[1]
    places = runs * capacity
    slots = slot_row[...]
    place = place_row(slots, runs, run_size, capacity)
    hit = iota((places, held), 0).astype(F32) == place
    ids = jnp.sum(jnp.where(hit, slots.astype(F32) + 1.0, 0.0), axis=1, keepdims=True)
    ids = jnp.broadcast_to(ids, (places, LANES))
    one = jnp.where(hit, 1.0, 0.0).astype(BF16)
    rest = fine[...]
    for part in range(3):
        head = rest.astype(BF16)
        stack[part * held : (part + 1) * held] = head
        rest = rest - head.astype(F32)
    packed = product(jnp.concatenate([one] * 3, axis=1), stack[...])
    for r in range(runs):
        out[r, :, :volume] = packed[r * capacity : (r + 1) * capacity]
        out[r, :, volume:] = ids[r * capacity : (r + 1) * capacity]


def unpack_kernel(slot_row, back, out, stack, *, run_size):
    held, volume = out.shape
    runs, capacity = back.shape[:2]
    places = runs * capacity
    place = to_column(place_row(slot_row[...], runs, run_size, capacity))
    hit = iota((held, places), 1).astype(F32) == place
    one = jnp.where(hit, 1.0, 0.0).astype(BF16)
    rest = jnp.concatenate([back[r] for r in range(runs)], axis=0)
    for part in range(3):
        head = rest.astype(BF16)
        stack[part * places : (part + 1) * places] = head
        rest = rest - head.astype(F32)
    out[...] = product(jnp.concatenate([one] * 3, axis=1), stack[...])


def child_code(ids, held):
    at = ids - 1.0
    return jnp.where(at < 0.0, -1.0, at - held * jnp.floor(at / held))


def row_code(index, count):
    inner = index & 7
    code = (inner >> 1) * 8 + (inner & 1) * 4 + (index >> 3)
    return jnp.where(inner < 2 * count, code.astype(F32), -2.0)


def child_rows(filter_matrix, count):
    breadth = filter_matrix.shape[0]
    half = breadth // 2
    lane = iota((breadth, half * 8), 1)
    inner = lane & 7
    hot = iota((breadth, half * 8), 0) == (inner & 1) * half + (lane >> 3)
    spread = exact_expand(filter_matrix, hot)
    return jnp.concatenate([jnp.where(inner >> 1 == n, spread, 0.0) for n in range(count)], axis=0)


def triple_lanes(x):
    high, low = split(x)
    return jnp.concatenate([high, high, low], axis=1)


def filter_kernel(got, filter_ref, out, stack, lines, cross, weave, *, count):
    runs, capacity, volume = got.shape
    volume = volume - LANES
    places = runs * capacity
    breadth = filter_ref.shape[0]
    half = breadth // 2
    width = out.shape[2]
    face = width // 4
    span = volume // face
    lo_count = LANES // breadth
    hi_count = breadth // lo_count
    matrix = filter_ref[...]
    turned = matrix.T
    lane = iota((breadth, width), 1)
    outer = lane // breadth
    across_z = exact_expand(turned, iota((breadth, width), 0) == lane % breadth)
    across_y = exact_expand(turned, iota((breadth, width), 0) == (outer % lo_count) * hi_count + outer // lo_count)
    for g in range(4):
        zs = across_z[(g & 1) * half : (g & 1) * half + half]
        for j in range(half):
            row = (g >> 1) * half + j
            high, low = split(zs * across_y[row : row + 1])
            at = (g * half + j) * half
            cross[0, at : at + half] = high
            cross[1, at : at + half] = low
    joined = jnp.concatenate([got[r] for r in range(runs)], axis=0)
    code = to_row(child_code(joined[:, volume : volume + 1], 8 * count))
    hit = row_code(iota((32, places), 0), count) == code
    one = jnp.where(hit, 1.0, 0.0).astype(BF16)
    high, low = split(joined[:, :volume])
    stack[:places] = high
    stack[places:] = low
    boxes = product(jnp.concatenate([one, one], axis=1), stack[...])
    for g in range(4):
        for i in range(0, span, 2):
            both = jnp.concatenate(
                [boxes[g * 8 : g * 8 + 8, (i + d) * face : (i + d + 1) * face] for d in range(2)], axis=0
            )
            high, low = split(both)
            lines[0, i * 8 : i * 8 + 16, g * face : (g + 1) * face] = high
            lines[1, i * 8 : i * 8 + 16, g * face : (g + 1) * face] = low
    total = product(lines[0], cross[0]) + product(lines[1], cross[0]) + product(lines[0], cross[1])
    high, low = split(total)
    size = total.shape[0]
    weave[:size] = high
    weave[size : 2 * size] = low
    weave[2 * size :] = high
    result = product(triple_lanes(child_rows(matrix, count)), weave[...])
    for n in range(count):
        out[n] = result[n * breadth : (n + 1) * breadth]


def unfilter_kernel(got, filter_ref, *refs, count, pieces):
    applied = refs[:pieces]
    out, weave, cross, stack = refs[pieces:]
    runs, capacity, volume = out.shape
    places = runs * capacity
    breadth = filter_ref.shape[0]
    half = breadth // 2
    width = applied[0].shape[2]
    face = width // 4
    size = count * breadth
    matrix = filter_ref[...]
    lane = iota((breadth, width), 1)
    octant = lane // face
    across_c = exact_expand(matrix, iota((breadth, width), 0) == octant % 2 * half + lane % half)
    across_b = exact_expand(matrix, iota((breadth, width), 0) == octant // 2 * half + lane // half % half)
    for b in range(breadth):
        high, low = split(across_c * across_b[b : b + 1])
        cross[0, b * breadth : (b + 1) * breadth] = high
        cross[1, b * breadth : (b + 1) * breadth] = low
    for n in range(count):
        total = applied[0][n]
        for piece in applied[1:]:
            total = total + piece[n]
        high, low = split(total)
        at = n * breadth
        weave[at : at + breadth] = high
        weave[size + at : size + at + breadth] = low
        weave[2 * size + at : 2 * size + at + breadth] = high
    lines = product(triple_lanes(child_rows(matrix, count).T), weave[...])
    high, low = split(lines)
    total = product(high, cross[0]) + product(low, cross[0]) + product(high, cross[1])
    for g in range(0, 4, 2):
        for i in range(total.shape[0] // 8):
            both = jnp.concatenate(
                [total[i * 8 : i * 8 + 8, (g + d) * face : (g + d + 1) * face] for d in range(2)], axis=0
            )
            high, low = split(both)
            stack[g * 8 : g * 8 + 16, i * face : (i + 1) * face] = high
            stack[32 + g * 8 : 32 + g * 8 + 16, i * face : (i + 1) * face] = low
    ids = jnp.concatenate([got[r] for r in range(runs)], axis=0)
    code = child_code(ids[:, :1], 8 * count)
    hit = row_code(iota((places, 32), 1), count) == code
    one = jnp.where(hit, 1.0, 0.0).astype(BF16)
    packed = product(jnp.concatenate([one, one], axis=1), stack[...])
    for r in range(runs):
        out[r] = packed[r * capacity : (r + 1) * capacity]


def vmem_call(kernel, out_shape, scratch, name, in_specs=None, room=14, **settings):
    extra = {} if in_specs is None else dict(grid=(1,), in_specs=in_specs)
    if in_specs is not None:
        rank = len(out_shape)
        extra["out_specs"] = pl.BlockSpec(out_shape, lambda i: (0,) * rank)
    return pl.pallas_call(
        functools.partial(kernel, **settings),
        out_shape=jax.ShapeDtypeStruct(out_shape, F32),
        scratch_shapes=[pltpu.VMEM(shape, dtype) for shape, dtype in scratch],
        compiler_params=pltpu.CompilerParams(vmem_limit_bytes=room << 20),
        name=name,
        **extra,
    )


def moved(array, row_step, bit):
    rows = lax.axis_size("row")
    cols = lax.axis_size("col")
    pairs = [
        (r * cols + c, (r + row_step) % rows * cols + (c ^ bit)) for r in range(rows) for c in range(cols)
    ]
    return lax.ppermute(array, ("row", "col"), pairs)


def local(fine_coeffs, fine_slot, neighbours, filter_matrix, kernel_ops):
    breadth = filter_matrix.shape[0]
    terms = kernel_ops.shape[0]
    runs = lax.axis_size("row")
    cols = lax.axis_size("col")
    held, volume = fine_coeffs.shape
    par_row = neighbours.shape[0]
    count = held // 8
    capacity = 2 * (held // runs)
    places = runs * capacity
    width = breadth * breadth
    hi_count = width // LANES
    groups = 2
    per = terms // groups
    uppers = range(0, cols, 2)

    slot_row = fine_slot.reshape(1, held)
    routing = dict(run_size=8 * par_row)
    sent = vmem_call(
        pack_kernel, (runs, capacity, volume + LANES), [((3 * held, volume), BF16)], "pack", room=60, runs=runs, **routing
    )(slot_row, fine_coeffs)
    got = lax.all_to_all(sent, "row", split_axis=0, concat_axis=0, tiled=True)

    first, second_high, second_low, merge_third, spread_third = pl.pallas_call(
        functools.partial(prepare_kernel, groups=groups),
        out_shape=[
            jax.ShapeDtypeStruct((terms * breadth, 3 * LANES), BF16),
            jax.ShapeDtypeStruct((terms, 3, breadth, LANES), BF16),
            jax.ShapeDtypeStruct((terms, 3, breadth, LANES), BF16),
            jax.ShapeDtypeStruct((groups, 2 * LANES, 2 * per * hi_count), BF16),
            jax.ShapeDtypeStruct((groups, 2, LANES, 3 * per * hi_count), BF16),
        ],
        compiler_params=pltpu.CompilerParams(vmem_limit_bytes=14 << 20),
        name="prepare",
    )(kernel_ops.reshape(terms * 9 * breadth, breadth))
    weights = (first, second_high, second_low)

    col_index = lax.axis_index("col")
    mine = lax.dynamic_slice_in_dim(neighbours, col_index * count, count, 0)[:, ::2]
    within = mine % par_row
    relation = (within // count) ^ col_index
    spot = (relation % 2) * (len(uppers) * count) + relation // 2 * count + within % count
    where = jnp.where(mine >= 0, spot, -1)

    filtered = vmem_call(
        filter_kernel,
        (count, breadth, width),
        [
            ((2 * places, volume), BF16),
            ((2, breadth * 4, width), BF16),
            ((2, width, width), BF16),
            ((12 * breadth, width), BF16),
        ],
        "filter",
        count=count,
    )(got, filter_matrix)

    parts = [moved(filtered, -1, u) for u in uppers]
    keep, send = spread_call(where, filtered, par_row, weights, spread_third, groups)
    parts, keep, send = lax.optimization_barrier((parts, keep, send))
    parts = parts + [moved(part, 0, 1) for part in parts]
    came = moved(send, 0, 1)

    terms_out = []
    for u in uppers:
        at = u // 2 * count
        terms_out.append(moved(keep[at : at + count] + came[at : at + count], 1, u))
    pieces = [merge_call(where, filtered, parts, weights, merge_third, groups)] + terms_out
    tail = volume // LANES
    results = vmem_call(
        unfilter_kernel,
        (runs, capacity, volume),
        [
            ((3 * count * breadth, width), BF16),
            ((2, width, width), BF16),
            ((64, volume), BF16),
        ],
        "unfilter",
        in_specs=[
            pl.BlockSpec((runs, capacity, LANES), lambda i: (0, 0, tail)),
            pl.BlockSpec((breadth, breadth), lambda i: (0, 0)),
        ]
        + [pl.BlockSpec((count, breadth, width), lambda i: (0, 0, 0))] * len(pieces),
        count=count,
        pieces=len(pieces),
    )(got, filter_matrix, *pieces)
    back = lax.all_to_all(results, "row", split_axis=0, concat_axis=0, tiled=True)
    return vmem_call(unpack_kernel, (held, volume), [((3 * places, volume), BF16)], "unpack", **routing)(slot_row, back)


def solution(mesh):
    in_specs = (P(("row", "col"), None), P(("row", "col")), P("row", None), P(), P())
    out_specs = P(("row", "col"), None)
    return jax.shard_map(local, mesh=mesh, in_specs=in_specs, out_specs=out_specs, check_vma=False)
```

```python
import functools

import jax
import jax.numpy as jnp
import numpy as np
from jax import lax
from jax.experimental import pallas as pl
from jax.experimental.pallas import tpu as pltpu
from jax.sharding import PartitionSpec as P

F32, BF16 = jnp.float32, jnp.bfloat16
LANES = 128
PAD = 8
UNROLL = True


def iota(shape, axis):
    return lax.broadcasted_iota(jnp.int32, shape, axis)


def split(x):
    high = x.astype(BF16)
    return high, (x - high.astype(F32)).astype(BF16)


def product(a, b):
    return jnp.dot(a, b, preferred_element_type=F32)


def exact_expand(x, hot):
    one = jnp.where(hot, 1.0, 0.0).astype(BF16)
    total = None
    for part in range(3):
        head = x.astype(BF16)
        piece = product(head, one)
        total = piece if total is None else total + piece
        x = x - head.astype(F32)
    return total


def prepare_kernel(ops, first, second_high, second_low, merge, spread, *, groups):
    breadth = ops.shape[1]
    terms = ops.shape[0] // (9 * breadth)
    lo_count = LANES // breadth
    hi_count = breadth // lo_count
    per = terms // groups

    def factor(term, axis, k):
        at = ((term * 3 + axis) * 3 + k) * breadth
        return ops[at : at + breadth]

    blank = jnp.zeros((breadth, LANES - 3 * breadth), F32)
    for term in range(terms):
        for k in range(3):
            value = factor(term, 0, k)
            high = value.astype(BF16).astype(F32)
            line = jnp.concatenate([high, high, value - high, blank], axis=1)
            first[term * breadth : (term + 1) * breadth, k * LANES : (k + 1) * LANES] = line.astype(BF16)
        at = (term * 9 + 6) * breadth
        turned = ops[at : at + 3 * breadth].T
        for k in range(3):
            high, low = split(jnp.concatenate([turned[:, k * breadth : (k + 1) * breadth]] * lo_count, axis=1))
            second_high[term, k] = high
            second_low[term, k] = low
    for g in range(groups):
        for inner in range(lo_count):
            strip = [
                jnp.concatenate(
                    [factor(g * per + t, 1, k)[:, inner * hi_count : (inner + 1) * hi_count] for t in range(per)], axis=1
                )
                for k in range(3)
            ]
            value = jnp.concatenate([strip[1], strip[0]], axis=1)
            high = value.astype(BF16).astype(F32)
            line = jnp.concatenate([high, high, value - high], axis=1)
            merge[g, inner * breadth : (inner + 1) * breadth] = line.astype(BF16)
            for s, k in enumerate((1, 2)):
                high = strip[k].astype(BF16).astype(F32)
                line = jnp.concatenate([high, high, strip[k] - high], axis=1)
                spread[g, s, inner * breadth : (inner + 1) * breadth] = line.astype(BF16)


class Loader:
    def __init__(self, sources, targets, sems):
        self.copies = [pltpu.make_async_copy(a, b, sems.at[i]) for i, (a, b) in enumerate(zip(sources, targets))]

    def start(self):
        for copy in self.copies:
            copy.start()

    def wait(self, chosen):
        for i in chosen:
            self.copies[i].wait()


def fill(xbuf, slot, block):
    breadth = block.shape[0]
    high, low = split(block)
    base = slot * LANES
    xbuf[base : base + breadth] = high
    xbuf[base + breadth : base + 2 * breadth] = low
    xbuf[base + 2 * breadth : base + 3 * breadth] = high


def place(ubuf, g, n, result):
    rows = result.shape[0]
    for h in range(result.shape[1] // LANES):
        ubuf[g, n, h, :rows] = result[:, h * LANES : (h + 1) * LANES]


def second_stage(ubuf, lbuf, tbuf, second_high, second_low, group, per, breadth, offsets, sides, recipes, emit):
    volumes, count, hi_count, stride = ubuf.shape[:4]
    lo_count = LANES // breadth
    wide = 2 * LANES
    flat = ubuf.reshape(volumes * count * hi_count * stride, LANES)
    block_mask = iota((LANES, LANES), 0) // breadth == iota((LANES, LANES), 1) // breadth
    zero_block = jnp.zeros((LANES, LANES), BF16)

    def pair_body(pair, carry):
        for spot, k in enumerate(offsets):
            row = spot * sides[0] * wide
            lane = spot * sides[1] * wide
            for half in range(2):
                term = group * per + pair * 2 + half
                high = jnp.concatenate([second_high[term, k]] * lo_count, axis=0)
                low = jnp.concatenate([second_low[term, k]] * lo_count, axis=0)
                high = jnp.where(block_mask, high, zero_block)
                low = jnp.where(block_mask, low, zero_block)
                tbuf[half, row : row + LANES, lane : lane + LANES] = high
                tbuf[half, row + LANES : row + wide, lane : lane + LANES] = high
                tbuf[half, row : row + LANES, lane + LANES : lane + wide] = low
        for half in range(2):
            term = pair * 2 + half
            for n in range(count):
                for g in range(volumes):
                    base = (g * count + n) * hi_count * stride + term * breadth
                    for a in range(0, breadth, 2):
                        pieces = [flat[pl.ds(base + a + d, hi_count, stride=stride), :] for d in range(2)]
                        high, low = split(jnp.concatenate(pieces, axis=0))
                        at = (n * breadth + a) * hi_count
                        lane = g * wide
                        lbuf[half, at : at + 2 * hi_count, lane : lane + LANES] = high
                        lbuf[half, at : at + 2 * hi_count, lane + LANES : lane + wide] = low
        results = []
        for half in range(2):
            line = []
            for (start, size), (row, rows), (lane, lanes) in recipes:
                full = product(
                    lbuf[half, :, start * wide : (start + size) * wide],
                    tbuf[half, row * wide : (row + rows) * wide, lane * wide : (lane + lanes) * wide],
                )
                for out in range(lanes):
                    line.append(full[:, out * wide : out * wide + LANES] + full[:, out * wide + LANES : (out + 1) * wide])
            results.append(line)
        for q in range(len(results[0])):
            for at in range(count * breadth):
                both = jnp.concatenate(
                    [results[half][q][at * hi_count : (at + 1) * hi_count] for half in range(2)], axis=0
                )
                high, low = split(both)
                emit(q, pair, at // 2, (at % 2) * LANES, high, low)
        return carry

    lax.fori_loop(0, per // 2, pair_body, 0, unroll=UNROLL)


def pick_diagonal(wide, breadth):
    lane_block = iota((breadth, wide.shape[1]), 1) % LANES // breadth
    total = wide[:breadth]
    for low in range(1, LANES // breadth):
        total = jnp.where(lane_block == low, wide[low * breadth : (low + 1) * breadth], total)
    return total


def turn_block(obuf, base, breadth, store):
    stride = breadth + PAD
    lo_count = LANES // breadth
    lane_of = iota((8, LANES), 1) // breadth
    for a in range(0, breadth, 8):
        for high in range(breadth // lo_count):
            level = [
                obuf[pl.ds(base + a * stride + high * lo_count + low, 8, stride=stride), :] for low in range(lo_count)
            ]
            step = 1
            while step < lo_count:
                own_side = (lane_of // step) % 2 == 0
                level = [
                    jnp.where(own_side, p, q) + pltpu.roll(jnp.where(own_side, q, p), step * breadth, 1)
                    for p, q in zip(level[::2], level[1::2])
                ]
                step *= 2
            store(a, high * LANES, level[0])


def merge_kernel(where, own, *refs, parts):
    sources = refs[:parts]
    remote = refs[parts : parts + 4]
    out = refs[parts + 4]
    first, second_high, second_low, third, weight_sems = refs[parts + 5 : parts + 10]
    vols, xbuf, ubuf, lbuf, tbuf, rbuf, obuf, sems = refs[parts + 10 :]
    loader = Loader(remote, (first, second_high, second_low, third), weight_sems)
    count, breadth, width = own.shape
    rows = first.shape[0] // third.shape[0]
    per = rows // breadth
    kgroup = per * breadth * breadth // LANES

    def copies(action):
        for n in range(count):
            for axis in range(3):
                slot = n * 3 + axis
                at = where[n, axis]
                start = 0
                for source in sources:
                    size = source.shape[0]

                    @pl.when((at >= start) & (at < start + size))
                    def _(source=source, start=start, slot=slot, at=at):
                        action(pltpu.make_async_copy(source.at[at - start], vols.at[slot], sems.at[slot]))

                    start += size

    copies(lambda c: c.start())
    loader.start()
    for n in range(count):
        for axis in range(3):

            @pl.when(where[n, axis] < 0)
            def _(slot=n * 3 + axis):
                vols[slot] = jnp.zeros((breadth, width), F32)

    tbuf[...] = jnp.zeros(tbuf.shape, BF16)
    xbuf[...] = jnp.zeros(xbuf.shape, BF16)
    copies(lambda c: c.wait())
    loader.wait((0,))
    stride = breadth + PAD

    def group_body(group, carry):
        top = pl.multiple_of(group * rows, 8)
        for n in range(count):
            fill(xbuf, 0, vols[n * 3])
            fill(xbuf, 1, own[n])
            place(ubuf, 0, n, product(first[pl.ds(top, rows), : 2 * LANES], xbuf[...]))
            for g, axis in ((1, 2), (2, 1)):
                fill(xbuf, 0, vols[n * 3 + axis])
                place(ubuf, g, n, product(first[pl.ds(top, rows), LANES : 2 * LANES], xbuf[:LANES]))

        @pl.when(group == 0)
        def _():
            loader.wait((1, 2, 3))

        def emit(q, pair, tile, lane, high, low):
            step = high.shape[0]
            row = pl.multiple_of(q * kgroup + pair * step, step)
            rbuf[tile, pl.ds(row, step), lane : lane + LANES] = high
            rbuf[tile, pl.ds(row + 2 * kgroup, step), lane : lane + LANES] = low
            rbuf[tile, pl.ds(row + 4 * kgroup, step), lane : lane + LANES] = high

        recipes = (((0, 2), (0, 2), (0, 1)), ((2, 1), (0, 1), (0, 1)))
        second_stage(
            ubuf, lbuf, tbuf, second_high, second_low, group, per, breadth, (1, 0), (1, 0), recipes, emit
        )
        for tile in range(count * breadth // 2):
            total = pick_diagonal(product(third[group], rbuf[tile]), breadth)
            for d in range(2):
                row = (tile * 2 + d) * stride
                old = jnp.where(group == 0, 0.0, obuf[row : row + breadth])
                obuf[row : row + breadth] = old + total[:, d * LANES : (d + 1) * LANES]
        return carry

    lax.fori_loop(0, third.shape[0], group_body, 0)
    for n in range(count):

        def store(a, lane, value, n=n):
            out[n, a : a + 8, lane : lane + LANES] = value

        turn_block(obuf, n * breadth * stride, breadth, store)


def spread_kernel(where, own, *refs):
    remote = refs[:4]
    keep, send, first, second_high, second_low, third, weight_sems = refs[4:11]
    xbuf, ubuf, lbuf, tbuf, rbuf, obuf, block = refs[11:]
    loader = Loader(remote, (first, second_high, second_low, third), weight_sems)
    count, breadth, width = own.shape
    rows = first.shape[0] // third.shape[0]
    per = rows // breadth
    kgroup = per * breadth * breadth // LANES
    half_slots = keep.shape[0]
    loader.start()
    keep[...] = jnp.zeros(keep.shape, F32)
    send[...] = jnp.zeros(send.shape, F32)
    tbuf[...] = jnp.zeros(tbuf.shape, BF16)
    xbuf[...] = jnp.zeros(xbuf.shape, BF16)
    loader.wait((0,))
    stride = breadth + PAD

    def group_body(group, carry):
        top = pl.multiple_of(group * rows, 8)
        for n in range(count):
            fill(xbuf, 0, own[n])
            for g in range(2):
                place(ubuf, g, n, product(first[pl.ds(top, rows), (1 + g) * LANES : (2 + g) * LANES], xbuf[...]))

        @pl.when(group == 0)
        def _():
            loader.wait((1, 2, 3))

        def emit(q, pair, tile, lane, high, low):
            step = high.shape[0]
            row = pl.multiple_of(q * 3 * kgroup + pair * step, step)
            rbuf[tile, pl.ds(row, step), lane : lane + LANES] = high
            rbuf[tile, pl.ds(row + kgroup, step), lane : lane + LANES] = low
            rbuf[tile, pl.ds(row + 2 * kgroup, step), lane : lane + LANES] = high

        recipes = (((1, 1), (0, 1), (0, 1)), ((0, 1), (0, 1), (0, 2)))
        second_stage(
            ubuf, lbuf, tbuf, second_high, second_low, group, per, breadth, (1, 2), (0, 1), recipes, emit
        )
        for tile in range(count * breadth // 2):
            for q in range(3):
                wide = product(third[group, 1 if q == 1 else 0], rbuf[tile, q * 3 * kgroup : (q + 1) * 3 * kgroup])
                total = pick_diagonal(wide, breadth)
                for d in range(2):
                    row = (tile * 2 + d) * stride
                    old = jnp.where(group == 0, 0.0, obuf[q, row : row + breadth])
                    obuf[q, row : row + breadth] = old + total[:, d * LANES : (d + 1) * LANES]
        return carry

    lax.fori_loop(0, third.shape[0], group_body, 0)
    for n in range(count):
        for q in range(3):

            def store(a, lane, value):
                block[a : a + 8, lane : lane + LANES] = value

            turn_block(obuf.at[q], n * breadth * stride, breadth, store)
            slot = where[n, q]

            @pl.when((slot >= 0) & (slot < half_slots))
            def _(slot=slot):
                keep[slot] = keep[slot] + block[...]

            @pl.when(slot >= half_slots)
            def _(slot=slot):
                send[slot - half_slots] = send[slot - half_slots] + block[...]


def stage_scratch(volumes, spots, recipes, count, breadth, per):
    hi_count = breadth * breadth // LANES
    return [
        pltpu.VMEM((volumes, count, hi_count, per * breadth + PAD, LANES), F32),
        pltpu.VMEM((2, count * breadth * hi_count, volumes * 2 * LANES), BF16),
        pltpu.VMEM((2, spots[0] * 2 * LANES, spots[1] * 2 * LANES), BF16),
        pltpu.VMEM((count * breadth // 2, recipes * 3 * per * hi_count, 2 * LANES), BF16),
    ]


def cost(count, breadth, per, units):
    return pl.CostEstimate(flops=units * per * 2 * count * breadth**4 * 200, transcendentals=0, bytes_accessed=1 << 22)


def stage_call(kernel, name, where, own, extra, weights, third, groups, out_shapes, scratch, units):
    first, second_high, second_low = weights
    breadth = own.shape[1]
    terms = second_high.shape[0]
    per = terms // groups
    return pl.pallas_call(
        kernel,
        out_shape=out_shapes,
        in_specs=[pl.BlockSpec(memory_space=pltpu.SMEM), pl.BlockSpec(memory_space=pltpu.VMEM)]
        + [pl.BlockSpec(memory_space=pl.ANY)] * len(extra)
        + [pl.BlockSpec(memory_space=pltpu.HBM)] * 4,
        out_specs=[pl.BlockSpec(memory_space=pltpu.VMEM)] * len(out_shapes),
        scratch_shapes=[pltpu.VMEM(array.shape, BF16) for array in (first, second_high, second_low, third)]
        + [pltpu.SemaphoreType.DMA((4,))]
        + scratch,
        compiler_params=pltpu.CompilerParams(vmem_limit_bytes=36 << 20),
        cost_estimate=cost(own.shape[0], breadth, terms, units),
        name=name,
    )(where, own, *extra, *[pltpu.with_memory_space_constraint(w, pltpu.HBM) for w in (first, second_high, second_low, third)])


def merge_call(where, own, parts, weights, third, groups):
    count, breadth, width = own.shape
    per = weights[1].shape[0] // groups
    scratch = stage_scratch(3, (2, 1), 2, count, breadth, per)
    scratch = (
        [pltpu.VMEM((count * 3, breadth, width), F32), pltpu.VMEM((2 * LANES, width), BF16)]
        + scratch
        + [pltpu.VMEM((count * breadth * (breadth + PAD), LANES), F32), pltpu.SemaphoreType.DMA((count * 3,))]
    )
    return stage_call(
        functools.partial(merge_kernel, parts=len(parts)),
        "merge",
        where,
        own,
        list(parts),
        weights,
        third,
        groups,
        [jax.ShapeDtypeStruct(own.shape, F32)],
        scratch,
        9,
    )[0]


def spread_call(where, own, slots, weights, third, groups):
    count, breadth, width = own.shape
    per = weights[1].shape[0] // groups
    scratch = stage_scratch(2, (1, 2), 3, count, breadth, per)
    scratch = (
        [pltpu.VMEM((LANES, width), BF16)]
        + scratch
        + [pltpu.VMEM((3, count * breadth * (breadth + PAD), LANES), F32), pltpu.VMEM((breadth, width), F32)]
    )
    shape = jax.ShapeDtypeStruct((slots // 2, breadth, width), F32)
    return stage_call(
        spread_kernel,
        "spread",
        where,
        own,
        [],
        weights,
        third,
        groups,
        [shape, shape],
        scratch,
        8,
    )


def to_row(column):
    size = column.shape[0]
    diagonal = iota((size, size), 0) == iota((size, size), 1)
    return jnp.sum(jnp.where(diagonal, column, 0.0), axis=0, keepdims=True)


def to_column(row):
    size = row.shape[1]
    diagonal = iota((size, size), 0) == iota((size, size), 1)
    return jnp.sum(jnp.where(diagonal, row, 0.0), axis=1, keepdims=True)


def place_row(slot_row, runs, run_size, capacity):
    held = slot_row.shape[1]
    run_row = jnp.zeros(slot_row.shape, F32)
    for r in range(1, runs):
        run_row = run_row + jnp.where(slot_row >= r * run_size, 1.0, 0.0)
    same = to_column(run_row) == run_row
    earlier = iota((held, held), 0) < iota((held, held), 1)
    before = jnp.sum(jnp.where(same & earlier, 1.0, 0.0), axis=0, keepdims=True)
    return run_row * capacity + before


def pack_kernel(slot_row, fine, out, stack, *, runs, run_size):
    held, volume = fine.shape
    capacity = out.shape[1]
    places = runs * capacity
    slots = slot_row[...]
    place = place_row(slots, runs, run_size, capacity)
    hit = iota((places, held), 0).astype(F32) == place
    ids = jnp.sum(jnp.where(hit, slots.astype(F32) + 1.0, 0.0), axis=1, keepdims=True)
    ids = jnp.broadcast_to(ids, (places, LANES))
    one = jnp.where(hit, 1.0, 0.0).astype(BF16)
    rest = fine[...]
    for part in range(3):
        head = rest.astype(BF16)
        stack[part * held : (part + 1) * held] = head
        rest = rest - head.astype(F32)
    packed = product(jnp.concatenate([one] * 3, axis=1), stack[...])
    for r in range(runs):
        out[r, :, :volume] = packed[r * capacity : (r + 1) * capacity]
        out[r, :, volume:] = ids[r * capacity : (r + 1) * capacity]


def unpack_kernel(slot_row, back, out, stack, *, run_size):
    held, volume = out.shape
    runs, capacity = back.shape[:2]
    places = runs * capacity
    place = to_column(place_row(slot_row[...], runs, run_size, capacity))
    hit = iota((held, places), 1).astype(F32) == place
    one = jnp.where(hit, 1.0, 0.0).astype(BF16)
    rest = jnp.concatenate([back[r] for r in range(runs)], axis=0)
    for part in range(3):
        head = rest.astype(BF16)
        stack[part * places : (part + 1) * places] = head
        rest = rest - head.astype(F32)
    out[...] = product(jnp.concatenate([one] * 3, axis=1), stack[...])


def child_code(ids, held):
    at = ids - 1.0
    return jnp.where(at < 0.0, -1.0, at - held * jnp.floor(at / held))


def row_code(index, count):
    inner = index & 7
    code = (inner >> 1) * 8 + (inner & 1) * 4 + (index >> 3)
    return jnp.where(inner < 2 * count, code.astype(F32), -2.0)


def child_rows(filter_matrix, count):
    breadth = filter_matrix.shape[0]
    half = breadth // 2
    lane = iota((breadth, half * 8), 1)
    inner = lane & 7
    hot = iota((breadth, half * 8), 0) == (inner & 1) * half + (lane >> 3)
    spread = exact_expand(filter_matrix, hot)
    return jnp.concatenate([jnp.where(inner >> 1 == n, spread, 0.0) for n in range(count)], axis=0)


def triple_lanes(x):
    high, low = split(x)
    return jnp.concatenate([high, high, low], axis=1)


def filter_kernel(got, filter_ref, out, stack, lines, cross, weave, *, count):
    runs, capacity, volume = got.shape
    volume = volume - LANES
    places = runs * capacity
    breadth = filter_ref.shape[0]
    half = breadth // 2
    width = out.shape[2]
    face = width // 4
    span = volume // face
    lo_count = LANES // breadth
    hi_count = breadth // lo_count
    matrix = filter_ref[...]
    turned = matrix.T
    lane = iota((breadth, width), 1)
    outer = lane // breadth
    across_z = exact_expand(turned, iota((breadth, width), 0) == lane % breadth)
    across_y = exact_expand(turned, iota((breadth, width), 0) == (outer % lo_count) * hi_count + outer // lo_count)
    for g in range(4):
        zs = across_z[(g & 1) * half : (g & 1) * half + half]
        for j in range(half):
            row = (g >> 1) * half + j
            high, low = split(zs * across_y[row : row + 1])
            at = (g * half + j) * half
            cross[0, at : at + half] = high
            cross[1, at : at + half] = low
    joined = jnp.concatenate([got[r] for r in range(runs)], axis=0)
    code = to_row(child_code(joined[:, volume : volume + 1], 8 * count))
    hit = row_code(iota((32, places), 0), count) == code
    one = jnp.where(hit, 1.0, 0.0).astype(BF16)
    high, low = split(joined[:, :volume])
    stack[:places] = high
    stack[places:] = low
    boxes = product(jnp.concatenate([one, one], axis=1), stack[...])
    for g in range(4):
        for i in range(0, span, 2):
            both = jnp.concatenate(
                [boxes[g * 8 : g * 8 + 8, (i + d) * face : (i + d + 1) * face] for d in range(2)], axis=0
            )
            high, low = split(both)
            lines[0, i * 8 : i * 8 + 16, g * face : (g + 1) * face] = high
            lines[1, i * 8 : i * 8 + 16, g * face : (g + 1) * face] = low
    total = product(lines[0], cross[0]) + product(lines[1], cross[0]) + product(lines[0], cross[1])
    high, low = split(total)
    size = total.shape[0]
    weave[:size] = high
    weave[size : 2 * size] = low
    weave[2 * size :] = high
    result = product(triple_lanes(child_rows(matrix, count)), weave[...])
    for n in range(count):
        out[n] = result[n * breadth : (n + 1) * breadth]


def unfilter_kernel(got, filter_ref, *refs, count, pieces):
    applied = refs[:pieces]
    out, weave, cross, stack = refs[pieces:]
    runs, capacity, volume = out.shape
    places = runs * capacity
    breadth = filter_ref.shape[0]
    half = breadth // 2
    width = applied[0].shape[2]
    face = width // 4
    size = count * breadth
    matrix = filter_ref[...]
    lane = iota((breadth, width), 1)
    octant = lane // face
    across_c = exact_expand(matrix, iota((breadth, width), 0) == octant % 2 * half + lane % half)
    across_b = exact_expand(matrix, iota((breadth, width), 0) == octant // 2 * half + lane // half % half)
    for b in range(breadth):
        high, low = split(across_c * across_b[b : b + 1])
        cross[0, b * breadth : (b + 1) * breadth] = high
        cross[1, b * breadth : (b + 1) * breadth] = low
    for n in range(count):
        total = applied[0][n]
        for piece in applied[1:]:
            total = total + piece[n]
        high, low = split(total)
        at = n * breadth
        weave[at : at + breadth] = high
        weave[size + at : size + at + breadth] = low
        weave[2 * size + at : 2 * size + at + breadth] = high
    lines = product(triple_lanes(child_rows(matrix, count).T), weave[...])
    high, low = split(lines)
    total = product(high, cross[0]) + product(low, cross[0]) + product(high, cross[1])
    for g in range(0, 4, 2):
        for i in range(total.shape[0] // 8):
            both = jnp.concatenate(
                [total[i * 8 : i * 8 + 8, (g + d) * face : (g + d + 1) * face] for d in range(2)], axis=0
            )
            high, low = split(both)
            stack[g * 8 : g * 8 + 16, i * face : (i + 1) * face] = high
            stack[32 + g * 8 : 32 + g * 8 + 16, i * face : (i + 1) * face] = low
    ids = jnp.concatenate([got[r] for r in range(runs)], axis=0)
    code = child_code(ids[:, :1], 8 * count)
    hit = row_code(iota((places, 32), 1), count) == code
    one = jnp.where(hit, 1.0, 0.0).astype(BF16)
    packed = product(jnp.concatenate([one, one], axis=1), stack[...])
    for r in range(runs):
        out[r] = packed[r * capacity : (r + 1) * capacity]


def vmem_call(kernel, out_shape, scratch, name, in_specs=None, room=14, **settings):
    extra = {} if in_specs is None else dict(grid=(1,), in_specs=in_specs)
    if in_specs is not None:
        rank = len(out_shape)
        extra["out_specs"] = pl.BlockSpec(out_shape, lambda i: (0,) * rank)
    return pl.pallas_call(
        functools.partial(kernel, **settings),
        out_shape=jax.ShapeDtypeStruct(out_shape, F32),
        scratch_shapes=[pltpu.VMEM(shape, dtype) for shape, dtype in scratch],
        compiler_params=pltpu.CompilerParams(vmem_limit_bytes=room << 20),
        name=name,
        **extra,
    )


def moved(array, row_step, bit):
    rows = lax.axis_size("row")
    cols = lax.axis_size("col")
    pairs = [
        (r * cols + c, (r + row_step) % rows * cols + (c ^ bit)) for r in range(rows) for c in range(cols)
    ]
    return lax.ppermute(array, ("row", "col"), pairs)


def local(fine_coeffs, fine_slot, neighbours, filter_matrix, kernel_ops):
    breadth = filter_matrix.shape[0]
    terms = kernel_ops.shape[0]
    runs = lax.axis_size("row")
    cols = lax.axis_size("col")
    held, volume = fine_coeffs.shape
    par_row = neighbours.shape[0]
    count = held // 8
    capacity = 2 * (held // runs)
    places = runs * capacity
    width = breadth * breadth
    hi_count = width // LANES
    groups = 2
    per = terms // groups
    uppers = range(0, cols, 2)

    slot_row = fine_slot.reshape(1, held)
    routing = dict(run_size=8 * par_row)
    sent = vmem_call(
        pack_kernel, (runs, capacity, volume + LANES), [((3 * held, volume), BF16)], "pack", room=60, runs=runs, **routing
    )(slot_row, fine_coeffs)
    got = lax.all_to_all(sent, "row", split_axis=0, concat_axis=0, tiled=True)

    first, second_high, second_low, merge_third, spread_third = pl.pallas_call(
        functools.partial(prepare_kernel, groups=groups),
        out_shape=[
            jax.ShapeDtypeStruct((terms * breadth, 3 * LANES), BF16),
            jax.ShapeDtypeStruct((terms, 3, breadth, LANES), BF16),
            jax.ShapeDtypeStruct((terms, 3, breadth, LANES), BF16),
            jax.ShapeDtypeStruct((groups, LANES, 6 * per * hi_count), BF16),
            jax.ShapeDtypeStruct((groups, 2, LANES, 3 * per * hi_count), BF16),
        ],
        compiler_params=pltpu.CompilerParams(vmem_limit_bytes=14 << 20),
        name="prepare",
    )(kernel_ops.reshape(terms * 9 * breadth, breadth))
    weights = (first, second_high, second_low)

    col_index = lax.axis_index("col")
    mine = lax.dynamic_slice_in_dim(neighbours, col_index * count, count, 0)[:, ::2]
    within = mine % par_row
    relation = (within // count) ^ col_index
    spot = (relation % 2) * (len(uppers) * count) + relation // 2 * count + within % count
    where = jnp.where(mine >= 0, spot, -1)

    filtered = vmem_call(
        filter_kernel,
        (count, breadth, width),
        [
            ((2 * places, volume), BF16),
            ((2, breadth * 4, width), BF16),
            ((2, width, width), BF16),
            ((12 * breadth, width), BF16),
        ],
        "filter",
        count=count,
    )(got, filter_matrix)

    parts = [moved(filtered, -1, u) for u in uppers]
    keep, send = spread_call(where, filtered, par_row, weights, spread_third, groups)
    parts, keep, send = lax.optimization_barrier((parts, keep, send))
    parts = parts + [moved(part, 0, 1) for part in parts]
    came = moved(send, 0, 1)

    terms_out = []
    for u in uppers:
        at = u // 2 * count
        terms_out.append(moved(keep[at : at + count] + came[at : at + count], 1, u))
    pieces = [merge_call(where, filtered, parts, weights, merge_third, groups)] + terms_out
    tail = volume // LANES
    results = vmem_call(
        unfilter_kernel,
        (runs, capacity, volume),
        [
            ((3 * count * breadth, width), BF16),
            ((2, width, width), BF16),
            ((64, volume), BF16),
        ],
        "unfilter",
        in_specs=[
            pl.BlockSpec((runs, capacity, LANES), lambda i: (0, 0, tail)),
            pl.BlockSpec((breadth, breadth), lambda i: (0, 0)),
        ]
        + [pl.BlockSpec((count, breadth, width), lambda i: (0, 0, 0))] * len(pieces),
        count=count,
        pieces=len(pieces),
    )(got, filter_matrix, *pieces)
    back = lax.all_to_all(results, "row", split_axis=0, concat_axis=0, tiled=True)
    return vmem_call(unpack_kernel, (held, volume), [((3 * places, volume), BF16)], "unpack", **routing)(slot_row, back)


def solution(mesh):
    in_specs = (P(("row", "col"), None), P(("row", "col")), P("row", None), P(), P())
    out_specs = P(("row", "col"), None)
    return jax.shard_map(local, mesh=mesh, in_specs=in_specs, out_specs=out_specs, check_vma=False)
```

```python
import functools

import jax
import jax.numpy as jnp
import numpy as np
from jax import lax
from jax.experimental import pallas as pl
from jax.experimental.pallas import tpu as pltpu
from jax.sharding import PartitionSpec as P

F32, BF16 = jnp.float32, jnp.bfloat16
LANES = 128
PAD = 8
UNROLL = True


def iota(shape, axis):
    return lax.broadcasted_iota(jnp.int32, shape, axis)


def split(x):
    high = x.astype(BF16)
    return high, (x - high.astype(F32)).astype(BF16)


def product(a, b):
    return jnp.dot(a, b, preferred_element_type=F32)


def exact_expand(x, hot):
    one = jnp.where(hot, 1.0, 0.0).astype(BF16)
    total = None
    for part in range(3):
        head = x.astype(BF16)
        piece = product(head, one)
        total = piece if total is None else total + piece
        x = x - head.astype(F32)
    return total


def prepare_kernel(ops, first, second_high, second_low, merge, spread, *, groups):
    breadth = ops.shape[1]
    terms = ops.shape[0] // (9 * breadth)
    lo_count = LANES // breadth
    hi_count = breadth // lo_count
    per = terms // groups

    def factor(term, axis, k):
        at = ((term * 3 + axis) * 3 + k) * breadth
        return ops[at : at + breadth]

    blank = jnp.zeros((breadth, LANES - 3 * breadth), F32)
    for term in range(terms):
        for k in range(3):
            value = factor(term, 0, k)
            high = value.astype(BF16).astype(F32)
            line = jnp.concatenate([high, high, value - high, blank], axis=1)
            first[term * breadth : (term + 1) * breadth, k * LANES : (k + 1) * LANES] = line.astype(BF16)
        at = (term * 9 + 6) * breadth
        turned = ops[at : at + 3 * breadth].T
        for k in range(3):
            high, low = split(jnp.concatenate([turned[:, k * breadth : (k + 1) * breadth]] * lo_count, axis=1))
            second_high[term, k] = high
            second_low[term, k] = low
    for g in range(groups):
        for inner in range(lo_count):
            strip = [
                jnp.concatenate(
                    [factor(g * per + t, 1, k)[:, inner * hi_count : (inner + 1) * hi_count] for t in range(per)], axis=1
                )
                for k in range(3)
            ]
            value = jnp.concatenate([strip[1], strip[0]], axis=1)
            high = value.astype(BF16).astype(F32)
            line = jnp.concatenate([high, high, value - high], axis=1)
            merge[g, inner * breadth : (inner + 1) * breadth] = line.astype(BF16)
            for s, k in enumerate((1, 2)):
                high = strip[k].astype(BF16).astype(F32)
                line = jnp.concatenate([high, high, strip[k] - high], axis=1)
                spread[g, s, inner * breadth : (inner + 1) * breadth] = line.astype(BF16)


class Loader:
    def __init__(self, sources, targets, sems):
        self.copies = [pltpu.make_async_copy(a, b, sems.at[i]) for i, (a, b) in enumerate(zip(sources, targets))]

    def start(self):
        for copy in self.copies:
            copy.start()

    def wait(self, chosen):
        for i in chosen:
            self.copies[i].wait()


def fill(xbuf, slot, block):
    breadth = block.shape[0]
    high, low = split(block)
    base = slot * LANES
    xbuf[base : base + breadth] = high
    xbuf[base + breadth : base + 2 * breadth] = low
    xbuf[base + 2 * breadth : base + 3 * breadth] = high


def place(ubuf, g, n, result):
    rows = result.shape[0]
    for h in range(result.shape[1] // LANES):
        ubuf[g, n, h, :rows] = result[:, h * LANES : (h + 1) * LANES]


def second_stage(ubuf, lbuf, tbuf, second_high, second_low, group, per, breadth, offsets, sides, recipes, emit):
    volumes, count, hi_count, stride = ubuf.shape[:4]
    lo_count = LANES // breadth
    wide = 2 * LANES
    flat = ubuf.reshape(volumes * count * hi_count * stride, LANES)
    block_mask = iota((LANES, LANES), 0) // breadth == iota((LANES, LANES), 1) // breadth
    zero_block = jnp.zeros((LANES, LANES), BF16)

    def pair_body(pair, carry):
        for spot, k in enumerate(offsets):
            row = spot * sides[0] * wide
            lane = spot * sides[1] * wide
            for half in range(2):
                term = group * per + pair * 2 + half
                high = jnp.concatenate([second_high[term, k]] * lo_count, axis=0)
                low = jnp.concatenate([second_low[term, k]] * lo_count, axis=0)
                high = jnp.where(block_mask, high, zero_block)
                low = jnp.where(block_mask, low, zero_block)
                tbuf[half, row : row + LANES, lane : lane + LANES] = high
                tbuf[half, row + LANES : row + wide, lane : lane + LANES] = high
                tbuf[half, row : row + LANES, lane + LANES : lane + wide] = low
        for half in range(2):
            term = pair * 2 + half
            for n in range(count):
                for g in range(volumes):
                    base = (g * count + n) * hi_count * stride + term * breadth
                    for a in range(0, breadth, 2):
                        pieces = [flat[pl.ds(base + a + d, hi_count, stride=stride), :] for d in range(2)]
                        high, low = split(jnp.concatenate(pieces, axis=0))
                        at = (n * breadth + a) * hi_count
                        lane = g * wide
                        lbuf[half, at : at + 2 * hi_count, lane : lane + LANES] = high
                        lbuf[half, at : at + 2 * hi_count, lane + LANES : lane + wide] = low
        results = []
        for half in range(2):
            line = []
            for (start, size), (row, rows), (lane, lanes) in recipes:
                full = product(
                    lbuf[half, :, start * wide : (start + size) * wide],
                    tbuf[half, row * wide : (row + rows) * wide, lane * wide : (lane + lanes) * wide],
                )
                for out in range(lanes):
                    line.append(full[:, out * wide : out * wide + LANES] + full[:, out * wide + LANES : (out + 1) * wide])
            results.append(line)
        for q in range(len(results[0])):
            for at in range(count * breadth):
                both = jnp.concatenate(
                    [results[half][q][at * hi_count : (at + 1) * hi_count] for half in range(2)], axis=0
                )
                high, low = split(both)
                emit(q, pair, at // 2, (at % 2) * LANES, high, low)
        return carry

    lax.fori_loop(0, per // 2, pair_body, 0, unroll=UNROLL)


def pick_diagonal(wide, breadth):
    lane_block = iota((breadth, wide.shape[1]), 1) % LANES // breadth
    total = wide[:breadth]
    for low in range(1, LANES // breadth):
        total = jnp.where(lane_block == low, wide[low * breadth : (low + 1) * breadth], total)
    return total


def turn_block(obuf, base, breadth, store):
    stride = breadth + PAD
    lo_count = LANES // breadth
    lane_of = iota((8, LANES), 1) // breadth
    for a in range(0, breadth, 8):
        for high in range(breadth // lo_count):
            level = [
                obuf[pl.ds(base + a * stride + high * lo_count + low, 8, stride=stride), :] for low in range(lo_count)
            ]
            step = 1
            while step < lo_count:
                own_side = (lane_of // step) % 2 == 0
                level = [
                    jnp.where(own_side, p, q) + pltpu.roll(jnp.where(own_side, q, p), step * breadth, 1)
                    for p, q in zip(level[::2], level[1::2])
                ]
                step *= 2
            store(a, high * LANES, level[0])


def merge_kernel(where, own, *refs, parts):
    sources = refs[:parts]
    remote = refs[parts : parts + 4]
    out = refs[parts + 4]
    first, second_high, second_low, third, weight_sems = refs[parts + 5 : parts + 10]
    vols, xbuf, ubuf, lbuf, tbuf, rbuf, obuf, sems = refs[parts + 10 :]
    loader = Loader(remote, (first, second_high, second_low, third), weight_sems)
    count, breadth, width = own.shape
    rows = first.shape[0] // third.shape[0]
    per = rows // breadth
    kgroup = per * breadth * breadth // LANES

    def copies(action):
        for n in range(count):
            for axis in range(3):
                slot = n * 3 + axis
                at = where[n, axis]
                start = 0
                for source in sources:
                    size = source.shape[0]

                    @pl.when((at >= start) & (at < start + size))
                    def _(source=source, start=start, slot=slot, at=at):
                        action(pltpu.make_async_copy(source.at[at - start], vols.at[slot], sems.at[slot]))

                    start += size

    copies(lambda c: c.start())
    loader.start()
    for n in range(count):
        for axis in range(3):

            @pl.when(where[n, axis] < 0)
            def _(slot=n * 3 + axis):
                vols[slot] = jnp.zeros((breadth, width), F32)

    tbuf[...] = jnp.zeros(tbuf.shape, BF16)
    xbuf[...] = jnp.zeros(xbuf.shape, BF16)
    copies(lambda c: c.wait())
    loader.wait((0,))
    stride = breadth + PAD

    def group_body(group, carry):
        top = pl.multiple_of(group * rows, 8)
        for n in range(count):
            fill(xbuf, 0, vols[n * 3])
            fill(xbuf, 1, own[n])
            place(ubuf, 0, n, product(first[pl.ds(top, rows), : 2 * LANES], xbuf[...]))
            for g, axis in ((1, 2), (2, 1)):
                fill(xbuf, 0, vols[n * 3 + axis])
                place(ubuf, g, n, product(first[pl.ds(top, rows), LANES : 2 * LANES], xbuf[:LANES]))

        @pl.when(group == 0)
        def _():
            loader.wait((1, 2, 3))

        def emit(q, pair, tile, lane, high, low):
            step = high.shape[0]
            row = pl.multiple_of(q * kgroup + pair * step, step)
            rbuf[tile, pl.ds(row, step), lane : lane + LANES] = high
            rbuf[tile, pl.ds(row + 2 * kgroup, step), lane : lane + LANES] = low
            rbuf[tile, pl.ds(row + 4 * kgroup, step), lane : lane + LANES] = high

        recipes = (((0, 2), (0, 2), (0, 1)), ((2, 1), (0, 1), (0, 1)))
        second_stage(
            ubuf, lbuf, tbuf, second_high, second_low, group, per, breadth, (1, 0), (1, 0), recipes, emit
        )
        for tile in range(count * breadth // 2):
            total = pick_diagonal(product(third[group], rbuf[tile]), breadth)
            for d in range(2):
                row = (tile * 2 + d) * stride
                old = jnp.where(group == 0, 0.0, obuf[row : row + breadth])
                obuf[row : row + breadth] = old + total[:, d * LANES : (d + 1) * LANES]
        return carry

    lax.fori_loop(0, third.shape[0], group_body, 0)
    for n in range(count):

        def store(a, lane, value, n=n):
            out[n, a : a + 8, lane : lane + LANES] = value

        turn_block(obuf, n * breadth * stride, breadth, store)


def spread_kernel(where, own, *refs):
    remote = refs[:4]
    keep, send, first, second_high, second_low, third, weight_sems = refs[4:11]
    xbuf, ubuf, lbuf, tbuf, rbuf, obuf, block = refs[11:]
    loader = Loader(remote, (first, second_high, second_low, third), weight_sems)
    count, breadth, width = own.shape
    rows = first.shape[0] // third.shape[0]
    per = rows // breadth
    kgroup = per * breadth * breadth // LANES
    half_slots = keep.shape[0]
    loader.start()
    keep[...] = jnp.zeros(keep.shape, F32)
    send[...] = jnp.zeros(send.shape, F32)
    tbuf[...] = jnp.zeros(tbuf.shape, BF16)
    xbuf[...] = jnp.zeros(xbuf.shape, BF16)
    loader.wait((0,))
    stride = breadth + PAD

    def group_body(group, carry):
        top = pl.multiple_of(group * rows, 8)
        for n in range(count):
            fill(xbuf, 0, own[n])
            for g in range(2):
                place(ubuf, g, n, product(first[pl.ds(top, rows), (1 + g) * LANES : (2 + g) * LANES], xbuf[...]))

        @pl.when(group == 0)
        def _():
            loader.wait((1, 2, 3))

        def emit(q, pair, tile, lane, high, low):
            step = high.shape[0]
            row = pl.multiple_of(q * 3 * kgroup + pair * step, step)
            rbuf[tile, pl.ds(row, step), lane : lane + LANES] = high
            rbuf[tile, pl.ds(row + kgroup, step), lane : lane + LANES] = low
            rbuf[tile, pl.ds(row + 2 * kgroup, step), lane : lane + LANES] = high

        recipes = (((1, 1), (0, 1), (0, 1)), ((0, 1), (0, 1), (0, 2)))
        second_stage(
            ubuf, lbuf, tbuf, second_high, second_low, group, per, breadth, (1, 2), (0, 1), recipes, emit
        )
        for tile in range(count * breadth // 2):
            for q in range(3):
                wide = product(third[group, 1 if q == 1 else 0], rbuf[tile, q * 3 * kgroup : (q + 1) * 3 * kgroup])
                total = pick_diagonal(wide, breadth)
                for d in range(2):
                    row = (tile * 2 + d) * stride
                    old = jnp.where(group == 0, 0.0, obuf[q, row : row + breadth])
                    obuf[q, row : row + breadth] = old + total[:, d * LANES : (d + 1) * LANES]
        return carry

    lax.fori_loop(0, third.shape[0], group_body, 0)
    for n in range(count):
        for q in range(3):

            def store(a, lane, value):
                block[a : a + 8, lane : lane + LANES] = value

            turn_block(obuf.at[q], n * breadth * stride, breadth, store)
            slot = where[n, q]

            @pl.when((slot >= 0) & (slot < half_slots))
            def _(slot=slot):
                keep[slot] = keep[slot] + block[...]

            @pl.when(slot >= half_slots)
            def _(slot=slot):
                send[slot - half_slots] = send[slot - half_slots] + block[...]


def stage_scratch(volumes, spots, recipes, count, breadth, per):
    hi_count = breadth * breadth // LANES
    return [
        pltpu.VMEM((volumes, count, hi_count, per * breadth + PAD, LANES), F32),
        pltpu.VMEM((2, count * breadth * hi_count, volumes * 2 * LANES), BF16),
        pltpu.VMEM((2, spots[0] * 2 * LANES, spots[1] * 2 * LANES), BF16),
        pltpu.VMEM((count * breadth // 2, recipes * 3 * per * hi_count, 2 * LANES), BF16),
    ]


def cost(count, breadth, per, units):
    return pl.CostEstimate(flops=units * per * 2 * count * breadth**4 * 200, transcendentals=0, bytes_accessed=1 << 22)


def stage_call(kernel, name, where, own, extra, weights, third, groups, out_shapes, scratch, units):
    first, second_high, second_low = weights
    breadth = own.shape[1]
    terms = second_high.shape[0]
    per = terms // groups
    return pl.pallas_call(
        kernel,
        out_shape=out_shapes,
        in_specs=[pl.BlockSpec(memory_space=pltpu.SMEM), pl.BlockSpec(memory_space=pltpu.VMEM)]
        + [pl.BlockSpec(memory_space=pl.ANY)] * len(extra)
        + [pl.BlockSpec(memory_space=pltpu.HBM)] * 4,
        out_specs=[pl.BlockSpec(memory_space=pltpu.VMEM)] * len(out_shapes),
        scratch_shapes=[pltpu.VMEM(array.shape, BF16) for array in (first, second_high, second_low, third)]
        + [pltpu.SemaphoreType.DMA((4,))]
        + scratch,
        compiler_params=pltpu.CompilerParams(vmem_limit_bytes=36 << 20),
        cost_estimate=cost(own.shape[0], breadth, terms, units),
        name=name,
    )(where, own, *extra, *[pltpu.with_memory_space_constraint(w, pltpu.HBM) for w in (first, second_high, second_low, third)])


def merge_call(where, own, parts, weights, third, groups):
    count, breadth, width = own.shape
    per = weights[1].shape[0] // groups
    scratch = stage_scratch(3, (2, 1), 2, count, breadth, per)
    scratch = (
        [pltpu.VMEM((count * 3, breadth, width), F32), pltpu.VMEM((2 * LANES, width), BF16)]
        + scratch
        + [pltpu.VMEM((count * breadth * (breadth + PAD), LANES), F32), pltpu.SemaphoreType.DMA((count * 3,))]
    )
    return stage_call(
        functools.partial(merge_kernel, parts=len(parts)),
        "merge",
        where,
        own,
        list(parts),
        weights,
        third,
        groups,
        [jax.ShapeDtypeStruct(own.shape, F32)],
        scratch,
        9,
    )[0]


def spread_call(where, own, slots, weights, third, groups):
    count, breadth, width = own.shape
    per = weights[1].shape[0] // groups
    scratch = stage_scratch(2, (1, 2), 3, count, breadth, per)
    scratch = (
        [pltpu.VMEM((LANES, width), BF16)]
        + scratch
        + [pltpu.VMEM((3, count * breadth * (breadth + PAD), LANES), F32), pltpu.VMEM((breadth, width), F32)]
    )
    shape = jax.ShapeDtypeStruct((slots // 2, breadth, width), F32)
    return stage_call(
        spread_kernel,
        "spread",
        where,
        own,
        [],
        weights,
        third,
        groups,
        [shape, shape],
        scratch,
        8,
    )


def to_row(column):
    size = column.shape[0]
    diagonal = iota((size, size), 0) == iota((size, size), 1)
    return jnp.sum(jnp.where(diagonal, column, 0.0), axis=0, keepdims=True)


def to_column(row):
    size = row.shape[1]
    diagonal = iota((size, size), 0) == iota((size, size), 1)
    return jnp.sum(jnp.where(diagonal, row, 0.0), axis=1, keepdims=True)


def place_row(slot_row, runs, run_size, capacity, row=None):
    held = slot_row.shape[1]
    run_row = jnp.zeros(slot_row.shape, F32)
    for r in range(1, runs):
        run_row = run_row + jnp.where(slot_row >= r * run_size, 1.0, 0.0)
    same = to_column(run_row) == run_row
    earlier = iota((held, held), 0) < iota((held, held), 1)
    before = jnp.sum(jnp.where(same & earlier, 1.0, 0.0), axis=0, keepdims=True)
    if row is not None:
        run_row = row.astype(F32) - run_row
        run_row = jnp.where(run_row < 0.0, run_row + runs, run_row)
    return run_row * capacity + before


def pack_kernel(slot_row, fine, out, stack, *, runs, run_size):
    held, volume = fine.shape
    capacity = out.shape[1]
    places = runs * capacity
    slots = slot_row[...]
    place = place_row(slots, runs, run_size, capacity)
    hit = iota((places, held), 0).astype(F32) == place
    ids = jnp.sum(jnp.where(hit, slots.astype(F32) + 1.0, 0.0), axis=1, keepdims=True)
    ids = jnp.broadcast_to(ids, (places, LANES))
    one = jnp.where(hit, 1.0, 0.0).astype(BF16)
    rest = fine[...]
    for part in range(3):
        head = rest.astype(BF16)
        stack[part * held : (part + 1) * held] = head
        rest = rest - head.astype(F32)
    packed = product(jnp.concatenate([one] * 3, axis=1), stack[...])
    for r in range(runs):
        out[r, :, :volume] = packed[r * capacity : (r + 1) * capacity]
        out[r, :, volume:] = ids[r * capacity : (r + 1) * capacity]


def unpack_kernel(row, slot_row, *refs, run_size):
    backs = refs[:-2]
    out, stack = refs[-2:]
    held, volume = out.shape
    runs = len(backs)
    capacity = backs[0].shape[0]
    places = runs * capacity
    place = to_column(place_row(slot_row[...], runs, run_size, capacity, row[0]))
    hit = iota((held, places), 1).astype(F32) == place
    one = jnp.where(hit, 1.0, 0.0).astype(BF16)
    rest = jnp.concatenate([back[...] for back in backs], axis=0)
    for part in range(3):
        head = rest.astype(BF16)
        stack[part * places : (part + 1) * places] = head
        rest = rest - head.astype(F32)
    out[...] = product(jnp.concatenate([one] * 3, axis=1), stack[...])


def child_code(ids, held):
    at = ids - 1.0
    return jnp.where(at < 0.0, -1.0, at - held * jnp.floor(at / held))


def row_code(index, count):
    inner = index & 7
    code = (inner >> 1) * 8 + (inner & 1) * 4 + (index >> 3)
    return jnp.where(inner < 2 * count, code.astype(F32), -2.0)


def child_rows(filter_matrix, count):
    breadth = filter_matrix.shape[0]
    half = breadth // 2
    lane = iota((breadth, half * 8), 1)
    inner = lane & 7
    hot = iota((breadth, half * 8), 0) == (inner & 1) * half + (lane >> 3)
    spread = exact_expand(filter_matrix, hot)
    return jnp.concatenate([jnp.where(inner >> 1 == n, spread, 0.0) for n in range(count)], axis=0)


def triple_lanes(x):
    high, low = split(x)
    return jnp.concatenate([high, high, low], axis=1)


def filter_kernel(got, filter_ref, out, stack, lines, cross, weave, *, count):
    runs, capacity, volume = got.shape
    volume = volume - LANES
    places = runs * capacity
    breadth = filter_ref.shape[0]
    half = breadth // 2
    width = out.shape[2]
    face = width // 4
    span = volume // face
    lo_count = LANES // breadth
    hi_count = breadth // lo_count
    matrix = filter_ref[...]
    turned = matrix.T
    lane = iota((breadth, width), 1)
    outer = lane // breadth
    across_z = exact_expand(turned, iota((breadth, width), 0) == lane % breadth)
    across_y = exact_expand(turned, iota((breadth, width), 0) == (outer % lo_count) * hi_count + outer // lo_count)
    for g in range(4):
        zs = across_z[(g & 1) * half : (g & 1) * half + half]
        for j in range(half):
            row = (g >> 1) * half + j
            high, low = split(zs * across_y[row : row + 1])
            at = (g * half + j) * half
            cross[0, at : at + half] = high
            cross[1, at : at + half] = low
    joined = jnp.concatenate([got[r] for r in range(runs)], axis=0)
    code = to_row(child_code(joined[:, volume : volume + 1], 8 * count))
    hit = row_code(iota((32, places), 0), count) == code
    one = jnp.where(hit, 1.0, 0.0).astype(BF16)
    high, low = split(joined[:, :volume])
    stack[:places] = high
    stack[places:] = low
    boxes = product(jnp.concatenate([one, one], axis=1), stack[...])
    for g in range(4):
        for i in range(0, span, 2):
            both = jnp.concatenate(
                [boxes[g * 8 : g * 8 + 8, (i + d) * face : (i + d + 1) * face] for d in range(2)], axis=0
            )
            high, low = split(both)
            lines[0, i * 8 : i * 8 + 16, g * face : (g + 1) * face] = high
            lines[1, i * 8 : i * 8 + 16, g * face : (g + 1) * face] = low
    total = product(lines[0], cross[0]) + product(lines[1], cross[0]) + product(lines[0], cross[1])
    high, low = split(total)
    size = total.shape[0]
    weave[:size] = high
    weave[size : 2 * size] = low
    weave[2 * size :] = high
    result = product(triple_lanes(child_rows(matrix, count)), weave[...])
    for n in range(count):
        out[n] = result[n * breadth : (n + 1) * breadth]


def unfilter_kernel(row, got, filter_ref, *refs, count, pieces):
    applied = refs[:pieces]
    runs = got.shape[0]
    outs = refs[pieces : pieces + runs]
    weave, cross, stack = refs[pieces + runs :]
    capacity, volume = outs[0].shape
    places = runs * capacity
    breadth = filter_ref.shape[0]
    half = breadth // 2
    width = applied[0].shape[2]
    face = width // 4
    size = count * breadth
    matrix = filter_ref[...]
    lane = iota((breadth, width), 1)
    octant = lane // face
    across_c = exact_expand(matrix, iota((breadth, width), 0) == octant % 2 * half + lane % half)
    across_b = exact_expand(matrix, iota((breadth, width), 0) == octant // 2 * half + lane // half % half)
    for b in range(breadth):
        high, low = split(across_c * across_b[b : b + 1])
        cross[0, b * breadth : (b + 1) * breadth] = high
        cross[1, b * breadth : (b + 1) * breadth] = low
    for n in range(count):
        total = applied[0][n]
        for piece in applied[1:]:
            total = total + piece[n]
        high, low = split(total)
        at = n * breadth
        weave[at : at + breadth] = high
        weave[size + at : size + at + breadth] = low
        weave[2 * size + at : 2 * size + at + breadth] = high
    lines = product(triple_lanes(child_rows(matrix, count).T), weave[...])
    high, low = split(lines)
    total = product(high, cross[0]) + product(low, cross[0]) + product(high, cross[1])
    for g in range(0, 4, 2):
        for i in range(total.shape[0] // 8):
            both = jnp.concatenate(
                [total[i * 8 : i * 8 + 8, (g + d) * face : (g + d + 1) * face] for d in range(2)], axis=0
            )
            high, low = split(both)
            stack[g * 8 : g * 8 + 16, i * face : (i + 1) * face] = high
            stack[32 + g * 8 : 32 + g * 8 + 16, i * face : (i + 1) * face] = low
    ids = jnp.concatenate([got[(row[0] + k) % runs] for k in range(runs)], axis=0)
    code = child_code(ids[:, :1], 8 * count)
    hit = row_code(iota((places, 32), 1), count) == code
    one = jnp.where(hit, 1.0, 0.0).astype(BF16)
    packed = product(jnp.concatenate([one, one], axis=1), stack[...])
    for k in range(runs):
        outs[k][...] = packed[k * capacity : (k + 1) * capacity]


def vmem_call(kernel, out_shape, scratch, name, in_specs=None, room=14, outputs=1, **settings):
    extra = {} if in_specs is None else dict(in_specs=in_specs)
    shapes = jax.ShapeDtypeStruct(out_shape, F32)
    if outputs > 1:
        shapes = [shapes] * outputs
    return pl.pallas_call(
        functools.partial(kernel, **settings),
        out_shape=shapes,
        scratch_shapes=[pltpu.VMEM(shape, dtype) for shape, dtype in scratch],
        compiler_params=pltpu.CompilerParams(vmem_limit_bytes=room << 20),
        name=name,
        **extra,
    )


def moved(array, row_step, bit):
    rows = lax.axis_size("row")
    cols = lax.axis_size("col")
    pairs = [
        (r * cols + c, (r + row_step) % rows * cols + (c ^ bit)) for r in range(rows) for c in range(cols)
    ]
    return lax.ppermute(array, ("row", "col"), pairs)


def local(fine_coeffs, fine_slot, neighbours, filter_matrix, kernel_ops):
    breadth = filter_matrix.shape[0]
    terms = kernel_ops.shape[0]
    runs = lax.axis_size("row")
    cols = lax.axis_size("col")
    held, volume = fine_coeffs.shape
    par_row = neighbours.shape[0]
    count = held // 8
    capacity = 2 * (held // runs)
    places = runs * capacity
    width = breadth * breadth
    hi_count = width // LANES
    groups = 2
    per = terms // groups
    uppers = range(0, cols, 2)

    slot_row = fine_slot.reshape(1, held)
    routing = dict(run_size=8 * par_row)
    sent = vmem_call(
        pack_kernel, (runs, capacity, volume + LANES), [((3 * held, volume), BF16)], "pack", room=60, runs=runs, **routing
    )(slot_row, fine_coeffs)
    got = lax.all_to_all(sent, "row", split_axis=0, concat_axis=0, tiled=True)

    first, second_high, second_low, merge_third, spread_third = pl.pallas_call(
        functools.partial(prepare_kernel, groups=groups),
        out_shape=[
            jax.ShapeDtypeStruct((terms * breadth, 3 * LANES), BF16),
            jax.ShapeDtypeStruct((terms, 3, breadth, LANES), BF16),
            jax.ShapeDtypeStruct((terms, 3, breadth, LANES), BF16),
            jax.ShapeDtypeStruct((groups, LANES, 6 * per * hi_count), BF16),
            jax.ShapeDtypeStruct((groups, 2, LANES, 3 * per * hi_count), BF16),
        ],
        compiler_params=pltpu.CompilerParams(vmem_limit_bytes=14 << 20),
        name="prepare",
    )(kernel_ops.reshape(terms * 9 * breadth, breadth))
    weights = (first, second_high, second_low)

    col_index = lax.axis_index("col")
    mine = lax.dynamic_slice_in_dim(neighbours, col_index * count, count, 0)[:, ::2]
    within = mine % par_row
    relation = (within // count) ^ col_index
    spot = (relation % 2) * (len(uppers) * count) + relation // 2 * count + within % count
    where = jnp.where(mine >= 0, spot, -1)

    filtered = vmem_call(
        filter_kernel,
        (count, breadth, width),
        [
            ((2 * places, volume), BF16),
            ((2, breadth * 4, width), BF16),
            ((2, width, width), BF16),
            ((12 * breadth, width), BF16),
        ],
        "filter",
        count=count,
    )(got, filter_matrix)

    parts = [moved(filtered, -1, u) for u in uppers]
    keep, send = spread_call(where, filtered, par_row, weights, spread_third, groups)
    parts, keep, send = lax.optimization_barrier((parts, keep, send))
    parts = parts + [moved(part, 0, 1) for part in parts]
    came = moved(send, 0, 1)

    terms_out = []
    for u in uppers:
        at = u // 2 * count
        terms_out.append(moved(keep[at : at + count] + came[at : at + count], 1, u))
    pieces = [merge_call(where, filtered, parts, weights, merge_third, groups)] + terms_out
    row = jnp.full((1,), lax.axis_index("row"), jnp.int32)
    scalar = pl.BlockSpec(memory_space=pltpu.SMEM)
    plain = pl.BlockSpec(memory_space=pltpu.VMEM)
    results = vmem_call(
        unfilter_kernel,
        (capacity, volume),
        [
            ((3 * count * breadth, width), BF16),
            ((2, width, width), BF16),
            ((64, volume), BF16),
        ],
        "unfilter",
        in_specs=[scalar] + [plain] * (2 + len(pieces)),
        outputs=runs,
        count=count,
        pieces=len(pieces),
    )(row, got[:, :, volume:], filter_matrix, *pieces)
    backs = [results[0]] + [moved(results[k], k, 0) for k in range(1, runs)]
    return vmem_call(
        unpack_kernel,
        (held, volume),
        [((3 * places, volume), BF16)],
        "unpack",
        in_specs=[scalar, plain] + [plain] * runs,
        **routing,
    )(row, slot_row, *backs)


def solution(mesh):
    in_specs = (P(("row", "col"), None), P(("row", "col")), P("row", None), P(), P())
    out_specs = P(("row", "col"), None)
    return jax.shard_map(local, mesh=mesh, in_specs=in_specs, out_specs=out_specs, check_vma=False)
```

```python
import functools

import jax
import jax.numpy as jnp
import numpy as np
from jax import lax
from jax.experimental import pallas as pl
from jax.experimental.pallas import tpu as pltpu
from jax.sharding import PartitionSpec as P

F32, BF16 = jnp.float32, jnp.bfloat16
LANES = 128
PAD = 8
UNROLL = True
ROOM = 60
PREP = 60


def iota(shape, axis):
    return lax.broadcasted_iota(jnp.int32, shape, axis)


def split(x):
    high = x.astype(BF16)
    return high, (x - high.astype(F32)).astype(BF16)


def product(a, b):
    return jnp.dot(a, b, preferred_element_type=F32)


def exact_expand(x, hot):
    one = jnp.where(hot, 1.0, 0.0).astype(BF16)
    total = None
    for part in range(3):
        head = x.astype(BF16)
        piece = product(head, one)
        total = piece if total is None else total + piece
        x = x - head.astype(F32)
    return total


def prepare_kernel(packed, first, second_high, second_low, merge, spread, ops, *, groups):
    terms = second_high.shape[0]
    breadth = second_high.shape[2]
    lo_count = LANES // breadth
    hi_count = breadth // lo_count
    per = terms // groups
    chunk = packed.shape[0] // terms
    for start in range(0, packed.shape[0], chunk):
        block = packed[start : start + chunk]
        for low in range(lo_count):
            turned = block if low == 0 else pltpu.roll(block, LANES - low * breadth, 1)
            ops[pl.ds(start * lo_count + low, chunk, stride=lo_count), :] = turned

    def factor(term, axis, k):
        at = ((term * 3 + axis) * 3 + k) * breadth
        return ops[at : at + breadth, :breadth]

    blank = jnp.zeros((breadth, LANES - 3 * breadth), F32)
    for term in range(terms):
        for k in range(3):
            value = factor(term, 0, k)
            high = value.astype(BF16).astype(F32)
            line = jnp.concatenate([high, high, value - high, blank], axis=1)
            first[term * breadth : (term + 1) * breadth, k * LANES : (k + 1) * LANES] = line.astype(BF16)
        at = (term * 9 + 6) * breadth
        turned = ops[at : at + 3 * breadth, :breadth].T
        for k in range(3):
            high, low = split(jnp.concatenate([turned[:, k * breadth : (k + 1) * breadth]] * lo_count, axis=1))
            second_high[term, k] = high
            second_low[term, k] = low
    for g in range(groups):
        for inner in range(lo_count):
            strip = [
                jnp.concatenate(
                    [factor(g * per + t, 1, k)[:, inner * hi_count : (inner + 1) * hi_count] for t in range(per)], axis=1
                )
                for k in range(3)
            ]
            value = jnp.concatenate([strip[1], strip[0]], axis=1)
            high = value.astype(BF16).astype(F32)
            line = jnp.concatenate([high, high, value - high], axis=1)
            merge[g, inner * breadth : (inner + 1) * breadth] = line.astype(BF16)
            for s, k in enumerate((1, 2)):
                high = strip[k].astype(BF16).astype(F32)
                line = jnp.concatenate([high, high, strip[k] - high], axis=1)
                spread[g, s, inner * breadth : (inner + 1) * breadth] = line.astype(BF16)


class Loader:
    def __init__(self, sources, targets, sems):
        self.copies = [pltpu.make_async_copy(a, b, sems.at[i]) for i, (a, b) in enumerate(zip(sources, targets))]

    def start(self):
        for copy in self.copies:
            copy.start()

    def wait(self, chosen):
        for i in chosen:
            self.copies[i].wait()


def fill(xbuf, slot, block):
    breadth = block.shape[0]
    high, low = split(block)
    base = slot * LANES
    xbuf[base : base + breadth] = high
    xbuf[base + breadth : base + 2 * breadth] = low
    xbuf[base + 2 * breadth : base + 3 * breadth] = high


def place(ubuf, g, n, result):
    rows = result.shape[0]
    for h in range(result.shape[1] // LANES):
        ubuf[g, n, h, :rows] = result[:, h * LANES : (h + 1) * LANES]


def second_stage(ubuf, lbuf, tbuf, second_high, second_low, group, per, breadth, offsets, sides, recipes, emit):
    volumes, count, hi_count, stride = ubuf.shape[:4]
    lo_count = LANES // breadth
    wide = 2 * LANES
    flat = ubuf.reshape(volumes * count * hi_count * stride, LANES)
    block_mask = iota((LANES, LANES), 0) // breadth == iota((LANES, LANES), 1) // breadth
    zero_block = jnp.zeros((LANES, LANES), BF16)

    def pair_body(pair, carry):
        for spot, k in enumerate(offsets):
            row = spot * sides[0] * wide
            lane = spot * sides[1] * wide
            for half in range(2):
                term = group * per + pair * 2 + half
                high = jnp.concatenate([second_high[term, k]] * lo_count, axis=0)
                low = jnp.concatenate([second_low[term, k]] * lo_count, axis=0)
                high = jnp.where(block_mask, high, zero_block)
                low = jnp.where(block_mask, low, zero_block)
                tbuf[half, row : row + LANES, lane : lane + LANES] = high
                tbuf[half, row + LANES : row + wide, lane : lane + LANES] = high
                tbuf[half, row : row + LANES, lane + LANES : lane + wide] = low
        for half in range(2):
            term = pair * 2 + half
            for n in range(count):
                for g in range(volumes):
                    base = (g * count + n) * hi_count * stride + term * breadth
                    for a in range(0, breadth, 2):
                        pieces = [flat[pl.ds(base + a + d, hi_count, stride=stride), :] for d in range(2)]
                        high, low = split(jnp.concatenate(pieces, axis=0))
                        at = (n * breadth + a) * hi_count
                        lane = g * wide
                        lbuf[half, at : at + 2 * hi_count, lane : lane + LANES] = high
                        lbuf[half, at : at + 2 * hi_count, lane + LANES : lane + wide] = low
        results = []
        for half in range(2):
            line = []
            for (start, size), (row, rows), (lane, lanes) in recipes:
                full = product(
                    lbuf[half, :, start * wide : (start + size) * wide],
                    tbuf[half, row * wide : (row + rows) * wide, lane * wide : (lane + lanes) * wide],
                )
                for out in range(lanes):
                    line.append(full[:, out * wide : out * wide + LANES] + full[:, out * wide + LANES : (out + 1) * wide])
            results.append(line)
        for q in range(len(results[0])):
            for at in range(count * breadth):
                both = jnp.concatenate(
                    [results[half][q][at * hi_count : (at + 1) * hi_count] for half in range(2)], axis=0
                )
                high, low = split(both)
                emit(q, pair, at // 2, (at % 2) * LANES, high, low)
        return carry

    lax.fori_loop(0, per // 2, pair_body, 0, unroll=UNROLL)


def pick_diagonal(wide, breadth):
    lane_block = iota((breadth, wide.shape[1]), 1) % LANES // breadth
    total = wide[:breadth]
    for low in range(1, LANES // breadth):
        total = jnp.where(lane_block == low, wide[low * breadth : (low + 1) * breadth], total)
    return total


def turn_block(obuf, base, breadth, store):
    stride = breadth + PAD
    lo_count = LANES // breadth
    lane_of = iota((8, LANES), 1) // breadth
    for a in range(0, breadth, 8):
        for high in range(breadth // lo_count):
            level = [
                obuf[pl.ds(base + a * stride + high * lo_count + low, 8, stride=stride), :] for low in range(lo_count)
            ]
            step = 1
            while step < lo_count:
                own_side = (lane_of // step) % 2 == 0
                level = [
                    jnp.where(own_side, p, q) + pltpu.roll(jnp.where(own_side, q, p), step * breadth, 1)
                    for p, q in zip(level[::2], level[1::2])
                ]
                step *= 2
            store(a, high * LANES, level[0])


def merge_kernel(where, own, *refs, parts):
    sources = refs[:parts]
    remote = refs[parts : parts + 4]
    out = refs[parts + 4]
    first, second_high, second_low, third, weight_sems = refs[parts + 5 : parts + 10]
    vols, xbuf, ubuf, lbuf, tbuf, rbuf, obuf, sems = refs[parts + 10 :]
    loader = Loader(remote, (first, second_high, second_low, third), weight_sems)
    count, breadth, width = own.shape
    rows = first.shape[0] // third.shape[0]
    per = rows // breadth
    kgroup = per * breadth * breadth // LANES

    def copies(action):
        for n in range(count):
            for axis in range(3):
                slot = n * 3 + axis
                at = where[n, axis]
                start = 0
                for source in sources:
                    size = source.shape[0]

                    @pl.when((at >= start) & (at < start + size))
                    def _(source=source, start=start, slot=slot, at=at):
                        action(pltpu.make_async_copy(source.at[at - start], vols.at[slot], sems.at[slot]))

                    start += size

    copies(lambda c: c.start())
    loader.start()
    for n in range(count):
        for axis in range(3):

            @pl.when(where[n, axis] < 0)
            def _(slot=n * 3 + axis):
                vols[slot] = jnp.zeros((breadth, width), F32)

    tbuf[...] = jnp.zeros(tbuf.shape, BF16)
    xbuf[...] = jnp.zeros(xbuf.shape, BF16)
    copies(lambda c: c.wait())
    loader.wait((0,))
    stride = breadth + PAD

    def group_body(group, carry):
        top = pl.multiple_of(group * rows, 8)
        for n in range(count):
            fill(xbuf, 0, vols[n * 3])
            fill(xbuf, 1, own[n])
            place(ubuf, 0, n, product(first[pl.ds(top, rows), : 2 * LANES], xbuf[...]))
            for g, axis in ((1, 2), (2, 1)):
                fill(xbuf, 0, vols[n * 3 + axis])
                place(ubuf, g, n, product(first[pl.ds(top, rows), LANES : 2 * LANES], xbuf[:LANES]))

        @pl.when(group == 0)
        def _():
            loader.wait((1, 2, 3))

        def emit(q, pair, tile, lane, high, low):
            step = high.shape[0]
            row = pl.multiple_of(q * kgroup + pair * step, step)
            rbuf[tile, pl.ds(row, step), lane : lane + LANES] = high
            rbuf[tile, pl.ds(row + 2 * kgroup, step), lane : lane + LANES] = low
            rbuf[tile, pl.ds(row + 4 * kgroup, step), lane : lane + LANES] = high

        recipes = (((0, 2), (0, 2), (0, 1)), ((2, 1), (0, 1), (0, 1)))
        second_stage(
            ubuf, lbuf, tbuf, second_high, second_low, group, per, breadth, (1, 0), (1, 0), recipes, emit
        )
        for tile in range(count * breadth // 2):
            total = pick_diagonal(product(third[group], rbuf[tile]), breadth)
            for d in range(2):
                row = (tile * 2 + d) * stride
                old = jnp.where(group == 0, 0.0, obuf[row : row + breadth])
                obuf[row : row + breadth] = old + total[:, d * LANES : (d + 1) * LANES]
        return carry

    lax.fori_loop(0, third.shape[0], group_body, 0)
    for n in range(count):

        def store(a, lane, value, n=n):
            out[n, a : a + 8, lane : lane + LANES] = value

        turn_block(obuf, n * breadth * stride, breadth, store)


def spread_kernel(where, own, *refs):
    remote = refs[:4]
    keep, send, first, second_high, second_low, third, weight_sems = refs[4:11]
    xbuf, ubuf, lbuf, tbuf, rbuf, obuf, block = refs[11:]
    loader = Loader(remote, (first, second_high, second_low, third), weight_sems)
    count, breadth, width = own.shape
    rows = first.shape[0] // third.shape[0]
    per = rows // breadth
    kgroup = per * breadth * breadth // LANES
    half_slots = keep.shape[0]
    loader.start()
    keep[...] = jnp.zeros(keep.shape, F32)
    send[...] = jnp.zeros(send.shape, F32)
    tbuf[...] = jnp.zeros(tbuf.shape, BF16)
    xbuf[...] = jnp.zeros(xbuf.shape, BF16)
    loader.wait((0,))
    stride = breadth + PAD

    def group_body(group, carry):
        top = pl.multiple_of(group * rows, 8)
        for n in range(count):
            fill(xbuf, 0, own[n])
            for g in range(2):
                place(ubuf, g, n, product(first[pl.ds(top, rows), (1 + g) * LANES : (2 + g) * LANES], xbuf[...]))

        @pl.when(group == 0)
        def _():
            loader.wait((1, 2, 3))

        def emit(q, pair, tile, lane, high, low):
            step = high.shape[0]
            row = pl.multiple_of(q * 3 * kgroup + pair * step, step)
            rbuf[tile, pl.ds(row, step), lane : lane + LANES] = high
            rbuf[tile, pl.ds(row + kgroup, step), lane : lane + LANES] = low
            rbuf[tile, pl.ds(row + 2 * kgroup, step), lane : lane + LANES] = high

        recipes = (((1, 1), (0, 1), (0, 1)), ((0, 1), (0, 1), (0, 2)))
        second_stage(
            ubuf, lbuf, tbuf, second_high, second_low, group, per, breadth, (1, 2), (0, 1), recipes, emit
        )
        for tile in range(count * breadth // 2):
            for q in range(3):
                wide = product(third[group, 1 if q == 1 else 0], rbuf[tile, q * 3 * kgroup : (q + 1) * 3 * kgroup])
                total = pick_diagonal(wide, breadth)
                for d in range(2):
                    row = (tile * 2 + d) * stride
                    old = jnp.where(group == 0, 0.0, obuf[q, row : row + breadth])
                    obuf[q, row : row + breadth] = old + total[:, d * LANES : (d + 1) * LANES]
        return carry

    lax.fori_loop(0, third.shape[0], group_body, 0)
    for n in range(count):
        for q in range(3):

            def store(a, lane, value):
                block[a : a + 8, lane : lane + LANES] = value

            turn_block(obuf.at[q], n * breadth * stride, breadth, store)
            slot = where[n, q]

            @pl.when((slot >= 0) & (slot < half_slots))
            def _(slot=slot):
                keep[slot] = keep[slot] + block[...]

            @pl.when(slot >= half_slots)
            def _(slot=slot):
                send[slot - half_slots] = send[slot - half_slots] + block[...]


def stage_scratch(volumes, spots, recipes, count, breadth, per):
    hi_count = breadth * breadth // LANES
    return [
        pltpu.VMEM((volumes, count, hi_count, per * breadth + PAD, LANES), F32),
        pltpu.VMEM((2, count * breadth * hi_count, volumes * 2 * LANES), BF16),
        pltpu.VMEM((2, spots[0] * 2 * LANES, spots[1] * 2 * LANES), BF16),
        pltpu.VMEM((count * breadth // 2, recipes * 3 * per * hi_count, 2 * LANES), BF16),
    ]


def cost(count, breadth, per, units):
    return pl.CostEstimate(flops=units * per * 2 * count * breadth**4 * 200, transcendentals=0, bytes_accessed=1 << 22)


def stage_call(kernel, name, where, own, extra, weights, third, groups, out_shapes, scratch, units):
    first, second_high, second_low = weights
    breadth = own.shape[1]
    terms = second_high.shape[0]
    per = terms // groups
    return pl.pallas_call(
        kernel,
        out_shape=out_shapes,
        in_specs=[pl.BlockSpec(memory_space=pltpu.SMEM), pl.BlockSpec(memory_space=pltpu.VMEM)]
        + [pl.BlockSpec(memory_space=pl.ANY)] * len(extra)
        + [pl.BlockSpec(memory_space=pltpu.HBM)] * 4,
        out_specs=[pl.BlockSpec(memory_space=pltpu.VMEM)] * len(out_shapes),
        scratch_shapes=[pltpu.VMEM(array.shape, BF16) for array in (first, second_high, second_low, third)]
        + [pltpu.SemaphoreType.DMA((4,))]
        + scratch,
        compiler_params=pltpu.CompilerParams(vmem_limit_bytes=36 << 20),
        cost_estimate=cost(own.shape[0], breadth, terms, units),
        name=name,
    )(where, own, *extra, *[pltpu.with_memory_space_constraint(w, pltpu.HBM) for w in (first, second_high, second_low, third)])


def merge_call(where, own, parts, weights, third, groups):
    count, breadth, width = own.shape
    per = weights[1].shape[0] // groups
    scratch = stage_scratch(3, (2, 1), 2, count, breadth, per)
    scratch = (
        [pltpu.VMEM((count * 3, breadth, width), F32), pltpu.VMEM((2 * LANES, width), BF16)]
        + scratch
        + [pltpu.VMEM((count * breadth * (breadth + PAD), LANES), F32), pltpu.SemaphoreType.DMA((count * 3,))]
    )
    return stage_call(
        functools.partial(merge_kernel, parts=len(parts)),
        "merge",
        where,
        own,
        list(parts),
        weights,
        third,
        groups,
        [jax.ShapeDtypeStruct(own.shape, F32)],
        scratch,
        9,
    )[0]


def spread_call(where, own, slots, weights, third, groups):
    count, breadth, width = own.shape
    per = weights[1].shape[0] // groups
    scratch = stage_scratch(2, (1, 2), 3, count, breadth, per)
    scratch = (
        [pltpu.VMEM((LANES, width), BF16)]
        + scratch
        + [pltpu.VMEM((3, count * breadth * (breadth + PAD), LANES), F32), pltpu.VMEM((breadth, width), F32)]
    )
    shape = jax.ShapeDtypeStruct((slots // 2, breadth, width), F32)
    return stage_call(
        spread_kernel,
        "spread",
        where,
        own,
        [],
        weights,
        third,
        groups,
        [shape, shape],
        scratch,
        8,
    )


def to_row(column):
    size = column.shape[0]
    diagonal = iota((size, size), 0) == iota((size, size), 1)
    return jnp.sum(jnp.where(diagonal, column, 0.0), axis=0, keepdims=True)


def to_column(row):
    size = row.shape[1]
    diagonal = iota((size, size), 0) == iota((size, size), 1)
    return jnp.sum(jnp.where(diagonal, row, 0.0), axis=1, keepdims=True)


def place_row(slot_row, row, runs, run_size, capacity):
    held = slot_row.shape[1]
    run_row = jnp.zeros(slot_row.shape, F32)
    for r in range(1, runs):
        run_row = run_row + jnp.where(slot_row >= r * run_size, 1.0, 0.0)
    same = to_column(run_row) == run_row
    earlier = iota((held, held), 0) < iota((held, held), 1)
    before = jnp.sum(jnp.where(same & earlier, 1.0, 0.0), axis=0, keepdims=True)
    far_row = run_row - row.astype(F32)
    far_row = jnp.where(far_row < 0.0, far_row + runs, far_row)
    return far_row * capacity + before


def pack_kernel(row, slot_row, fine, *refs, run_size):
    outs, stack = refs[:-1], refs[-1]
    held, volume = fine.shape
    runs = len(outs)
    capacity = outs[0].shape[0]
    places = runs * capacity
    slots = slot_row[...]
    place = place_row(slots, row[0], runs, run_size, capacity)
    hit = iota((places, held), 0).astype(F32) == place
    ids = jnp.sum(jnp.where(hit, slots.astype(F32) + 1.0, 0.0), axis=1, keepdims=True)
    ids = jnp.broadcast_to(ids, (places, LANES))
    one = jnp.where(hit, 1.0, 0.0).astype(BF16)
    rest = fine[...]
    for part in range(3):
        head = rest.astype(BF16)
        stack[part * held : (part + 1) * held] = head
        rest = rest - head.astype(F32)
    packed = product(jnp.concatenate([one] * 3, axis=1), stack[...])
    for k in range(runs):
        outs[k][:, :volume] = packed[k * capacity : (k + 1) * capacity]
        outs[k][:, volume:] = ids[k * capacity : (k + 1) * capacity]


def unpack_kernel(row, slot_row, *refs, run_size):
    backs = refs[:-2]
    out, stack = refs[-2:]
    held, volume = out.shape
    runs = len(backs)
    capacity = backs[0].shape[0]
    places = runs * capacity
    place = to_column(place_row(slot_row[...], row[0], runs, run_size, capacity))
    hit = iota((held, places), 1).astype(F32) == place
    one = jnp.where(hit, 1.0, 0.0).astype(BF16)
    rest = jnp.concatenate([back[...] for back in backs], axis=0)
    for part in range(3):
        head = rest.astype(BF16)
        stack[part * places : (part + 1) * places] = head
        rest = rest - head.astype(F32)
    out[...] = product(jnp.concatenate([one] * 3, axis=1), stack[...])


def child_code(ids, held):
    at = ids - 1.0
    return jnp.where(at < 0.0, -1.0, at - held * jnp.floor(at / held))


def row_code(index, count):
    inner = index & 7
    code = (inner >> 1) * 8 + (inner & 1) * 4 + (index >> 3)
    return jnp.where(inner < 2 * count, code.astype(F32), -2.0)


def child_rows(filter_matrix, count):
    breadth = filter_matrix.shape[0]
    half = breadth // 2
    lane = iota((breadth, half * 8), 1)
    inner = lane & 7
    hot = iota((breadth, half * 8), 0) == (inner & 1) * half + (lane >> 3)
    spread = exact_expand(filter_matrix, hot)
    return jnp.concatenate([jnp.where(inner >> 1 == n, spread, 0.0) for n in range(count)], axis=0)


def triple_lanes(x):
    high, low = split(x)
    return jnp.concatenate([high, high, low], axis=1)


def filter_kernel(filter_ref, *refs, count):
    got = refs[:-6]
    out, ids, stack, lines, cross, weave = refs[-6:]
    runs = len(got)
    capacity, volume = got[0].shape
    volume = volume - LANES
    places = runs * capacity
    breadth = filter_ref.shape[0]
    half = breadth // 2
    width = out.shape[2]
    face = width // 4
    span = volume // face
    lo_count = LANES // breadth
    hi_count = breadth // lo_count
    matrix = filter_ref[...]
    turned = matrix.T
    lane = iota((breadth, width), 1)
    outer = lane // breadth
    across_z = exact_expand(turned, iota((breadth, width), 0) == lane % breadth)
    across_y = exact_expand(turned, iota((breadth, width), 0) == (outer % lo_count) * hi_count + outer // lo_count)
    for g in range(4):
        zs = across_z[(g & 1) * half : (g & 1) * half + half]
        for j in range(half):
            row = (g >> 1) * half + j
            high, low = split(zs * across_y[row : row + 1])
            at = (g * half + j) * half
            cross[0, at : at + half] = high
            cross[1, at : at + half] = low
    joined = jnp.concatenate([piece[...] for piece in got], axis=0)
    ids[...] = jnp.concatenate([got[(runs - k) % runs][:, volume:] for k in range(runs)], axis=0)
    code = to_row(child_code(joined[:, volume : volume + 1], 8 * count))
    hit = row_code(iota((32, places), 0), count) == code
    one = jnp.where(hit, 1.0, 0.0).astype(BF16)
    high, low = split(joined[:, :volume])
    stack[:places] = high
    stack[places:] = low
    boxes = product(jnp.concatenate([one, one], axis=1), stack[...])
    for g in range(4):
        for i in range(0, span, 2):
            both = jnp.concatenate(
                [boxes[g * 8 : g * 8 + 8, (i + d) * face : (i + d + 1) * face] for d in range(2)], axis=0
            )
            high, low = split(both)
            lines[0, i * 8 : i * 8 + 16, g * face : (g + 1) * face] = high
            lines[1, i * 8 : i * 8 + 16, g * face : (g + 1) * face] = low
    total = product(lines[0], cross[0]) + product(lines[1], cross[0]) + product(lines[0], cross[1])
    high, low = split(total)
    size = total.shape[0]
    weave[:size] = high
    weave[size : 2 * size] = low
    weave[2 * size :] = high
    result = product(triple_lanes(child_rows(matrix, count)), weave[...])
    for n in range(count):
        out[n] = result[n * breadth : (n + 1) * breadth]


def unfilter_kernel(filter_ref, ids, *refs, count, runs):
    outs = refs[-3 - runs : -3]
    applied = refs[: -3 - runs]
    weave, cross, stack = refs[-3:]
    capacity, volume = outs[0].shape
    places = runs * capacity
    breadth = filter_ref.shape[0]
    half = breadth // 2
    width = applied[0].shape[2]
    face = width // 4
    size = count * breadth
    matrix = filter_ref[...]
    lane = iota((breadth, width), 1)
    octant = lane // face
    across_c = exact_expand(matrix, iota((breadth, width), 0) == octant % 2 * half + lane % half)
    across_b = exact_expand(matrix, iota((breadth, width), 0) == octant // 2 * half + lane // half % half)
    for b in range(breadth):
        high, low = split(across_c * across_b[b : b + 1])
        cross[0, b * breadth : (b + 1) * breadth] = high
        cross[1, b * breadth : (b + 1) * breadth] = low
    for n in range(count):
        total = applied[0][n]
        for piece in applied[1:]:
            total = total + piece[n]
        high, low = split(total)
        at = n * breadth
        weave[at : at + breadth] = high
        weave[size + at : size + at + breadth] = low
        weave[2 * size + at : 2 * size + at + breadth] = high
    lines = product(triple_lanes(child_rows(matrix, count).T), weave[...])
    high, low = split(lines)
    total = product(high, cross[0]) + product(low, cross[0]) + product(high, cross[1])
    for g in range(0, 4, 2):
        for i in range(total.shape[0] // 8):
            both = jnp.concatenate(
                [total[i * 8 : i * 8 + 8, (g + d) * face : (g + d + 1) * face] for d in range(2)], axis=0
            )
            high, low = split(both)
            stack[g * 8 : g * 8 + 16, i * face : (i + 1) * face] = high
            stack[32 + g * 8 : 32 + g * 8 + 16, i * face : (i + 1) * face] = low
    code = child_code(ids[:, :1], 8 * count)
    hit = row_code(iota((places, 32), 1), count) == code
    one = jnp.where(hit, 1.0, 0.0).astype(BF16)
    packed = product(jnp.concatenate([one, one], axis=1), stack[...])
    for k in range(runs):
        outs[k][...] = packed[k * capacity : (k + 1) * capacity]


def vmem_call(kernel, out_shape, scratch, name, in_specs=None, room=14, outputs=1, **settings):
    extra = {} if in_specs is None else dict(in_specs=in_specs)
    if isinstance(out_shape, list):
        shapes = [jax.ShapeDtypeStruct(shape, F32) for shape in out_shape]
    else:
        shapes = jax.ShapeDtypeStruct(out_shape, F32)
    if outputs > 1:
        shapes = [shapes] * outputs
    return pl.pallas_call(
        functools.partial(kernel, **settings),
        out_shape=shapes,
        scratch_shapes=[pltpu.VMEM(shape, dtype) for shape, dtype in scratch],
        compiler_params=pltpu.CompilerParams(vmem_limit_bytes=room << 20),
        name=name,
        **extra,
    )


def moved(array, row_step, bit):
    rows = lax.axis_size("row")
    cols = lax.axis_size("col")
    pairs = [
        (r * cols + c, (r + row_step) % rows * cols + (c ^ bit)) for r in range(rows) for c in range(cols)
    ]
    return lax.ppermute(array, ("row", "col"), pairs)


def local(fine_coeffs, fine_slot, neighbours, filter_matrix, kernel_ops):
    breadth = filter_matrix.shape[0]
    terms = kernel_ops.shape[0]
    runs = lax.axis_size("row")
    cols = lax.axis_size("col")
    held, volume = fine_coeffs.shape
    par_row = neighbours.shape[0]
    count = held // 8
    capacity = 2 * (held // runs)
    places = runs * capacity
    width = breadth * breadth
    hi_count = width // LANES
    groups = 2
    per = terms // groups
    uppers = range(0, cols, 2)

    slot_row = fine_slot.reshape(1, held)
    routing = dict(run_size=8 * par_row)
    row = jnp.full((1,), lax.axis_index("row"), jnp.int32)
    scalar = pl.BlockSpec(memory_space=pltpu.SMEM)
    plain = pl.BlockSpec(memory_space=pltpu.VMEM)
    sent = vmem_call(
        pack_kernel,
        (capacity, volume + LANES),
        [((3 * held, volume), BF16)],
        "pack",
        in_specs=[scalar, plain, plain],
        room=ROOM,
        outputs=runs,
        **routing,
    )(row, slot_row, fine_coeffs)
    got = [sent[0]] + [moved(sent[k], k, 0) for k in range(1, runs)]

    first, second_high, second_low, merge_third, spread_third = pl.pallas_call(
        functools.partial(prepare_kernel, groups=groups),
        out_shape=[
            jax.ShapeDtypeStruct((terms * breadth, 3 * LANES), BF16),
            jax.ShapeDtypeStruct((terms, 3, breadth, LANES), BF16),
            jax.ShapeDtypeStruct((terms, 3, breadth, LANES), BF16),
            jax.ShapeDtypeStruct((groups, LANES, 6 * per * hi_count), BF16),
            jax.ShapeDtypeStruct((groups, 2, LANES, 3 * per * hi_count), BF16),
        ],
        scratch_shapes=[pltpu.VMEM((terms * 9 * breadth, LANES), F32)],
        compiler_params=pltpu.CompilerParams(vmem_limit_bytes=PREP << 20),
        name="prepare",
    )(kernel_ops.reshape(terms * 9 * hi_count, LANES))
    weights = (first, second_high, second_low)

    col_index = lax.axis_index("col")
    mine = lax.dynamic_slice_in_dim(neighbours, col_index * count, count, 0)[:, ::2]
    within = mine % par_row
    relation = (within // count) ^ col_index
    spot = (relation % 2) * (len(uppers) * count) + relation // 2 * count + within % count
    where = jnp.where(mine >= 0, spot, -1)

    filtered, ids = vmem_call(
        filter_kernel,
        [(count, breadth, width), (places, LANES)],
        [
            ((2 * places, volume), BF16),
            ((2, breadth * 4, width), BF16),
            ((2, width, width), BF16),
            ((12 * breadth, width), BF16),
        ],
        "filter",
        count=count,
    )(filter_matrix, *got)

    parts = [moved(filtered, -1, u) for u in uppers]
    keep, send = spread_call(where, filtered, par_row, weights, spread_third, groups)
    parts, keep, send = lax.optimization_barrier((parts, keep, send))
    parts = parts + [moved(part, 0, 1) for part in parts]
    came = moved(send, 0, 1)

    terms_out = []
    for u in uppers:
        at = u // 2 * count
        terms_out.append(moved(keep[at : at + count] + came[at : at + count], 1, u))
    pieces = [merge_call(where, filtered, parts, weights, merge_third, groups)] + terms_out
    results = vmem_call(
        unfilter_kernel,
        (capacity, volume),
        [
            ((3 * count * breadth, width), BF16),
            ((2, width, width), BF16),
            ((64, volume), BF16),
        ],
        "unfilter",
        in_specs=[plain] * (2 + len(pieces)),
        outputs=runs,
        count=count,
        runs=runs,
    )(filter_matrix, ids, *pieces)
    backs = [results[0]] + [moved(results[runs - j], -j, 0) for j in range(1, runs)]
    return vmem_call(
        unpack_kernel,
        (held, volume),
        [((3 * places, volume), BF16)],
        "unpack",
        in_specs=[scalar, plain] + [plain] * runs,
        **routing,
    )(row, slot_row, *backs)


def solution(mesh):
    in_specs = (P(("row", "col"), None), P(("row", "col")), P("row", None), P(), P())
    out_specs = P(("row", "col"), None)
    return jax.shard_map(local, mesh=mesh, in_specs=in_specs, out_specs=out_specs, check_vma=False)
```

```python
import functools

import jax
import jax.numpy as jnp
import numpy as np
from jax import lax
from jax.experimental import pallas as pl
from jax.experimental.pallas import tpu as pltpu
from jax.sharding import PartitionSpec as P

F32, BF16 = jnp.float32, jnp.bfloat16
LANES = 128
PAD = 8
UNROLL = True
ROOM = 60
PREP = 14


def iota(shape, axis):
    return lax.broadcasted_iota(jnp.int32, shape, axis)


def split(x):
    high = x.astype(BF16)
    return high, (x - high.astype(F32)).astype(BF16)


def product(a, b):
    return jnp.dot(a, b, preferred_element_type=F32)


def exact_expand(x, hot):
    one = jnp.where(hot, 1.0, 0.0).astype(BF16)
    total = None
    for part in range(3):
        head = x.astype(BF16)
        piece = product(head, one)
        total = piece if total is None else total + piece
        x = x - head.astype(F32)
    return total


def prepare_kernel(packed, first, second_high, second_low, merge, spread, ops, *, groups):
    terms = second_high.shape[0]
    breadth = second_high.shape[2]
    lo_count = LANES // breadth
    hi_count = breadth // lo_count
    per = terms // groups
    chunk = packed.shape[0] // terms
    for start in range(0, packed.shape[0], chunk):
        block = packed[start : start + chunk]
        for low in range(lo_count):
            turned = block if low == 0 else pltpu.roll(block, LANES - low * breadth, 1)
            ops[pl.ds(start * lo_count + low, chunk, stride=lo_count), :] = turned

    def factor(term, axis, k):
        at = ((term * 3 + axis) * 3 + k) * breadth
        return ops[at : at + breadth, :breadth]

    blank = jnp.zeros((breadth, LANES - 3 * breadth), F32)
    for term in range(terms):
        for k in range(3):
            value = factor(term, 0, k)
            high = value.astype(BF16).astype(F32)
            line = jnp.concatenate([high, high, value - high, blank], axis=1)
            first[term * breadth : (term + 1) * breadth, k * LANES : (k + 1) * LANES] = line.astype(BF16)
        at = (term * 9 + 6) * breadth
        turned = ops[at : at + 3 * breadth, :breadth].T
        for k in range(3):
            high, low = split(jnp.concatenate([turned[:, k * breadth : (k + 1) * breadth]] * lo_count, axis=1))
            second_high[term, k] = high
            second_low[term, k] = low
    for g in range(groups):
        for inner in range(lo_count):
            strip = [
                jnp.concatenate(
                    [factor(g * per + t, 1, k)[:, inner * hi_count : (inner + 1) * hi_count] for t in range(per)], axis=1
                )
                for k in range(3)
            ]
            value = jnp.concatenate([strip[1], strip[0]], axis=1)
            high = value.astype(BF16).astype(F32)
            line = jnp.concatenate([high, high, value - high], axis=1)
            merge[g, inner * breadth : (inner + 1) * breadth] = line.astype(BF16)
            for s, k in enumerate((1, 2)):
                high = strip[k].astype(BF16).astype(F32)
                line = jnp.concatenate([high, high, strip[k] - high], axis=1)
                spread[g, s, inner * breadth : (inner + 1) * breadth] = line.astype(BF16)


def fill(xbuf, slot, block):
    breadth = block.shape[0]
    high, low = split(block)
    base = slot * LANES
    xbuf[base : base + breadth] = high
    xbuf[base + breadth : base + 2 * breadth] = low
    xbuf[base + 2 * breadth : base + 3 * breadth] = high


def place(ubuf, g, n, result):
    rows = result.shape[0]
    for h in range(result.shape[1] // LANES):
        ubuf[g, n, h, :rows] = result[:, h * LANES : (h + 1) * LANES]


def second_stage(ubuf, lbuf, tbuf, second_high, second_low, group, per, breadth, offsets, sides, recipes, emit):
    volumes, count, hi_count, stride = ubuf.shape[:4]
    lo_count = LANES // breadth
    wide = 2 * LANES
    flat = ubuf.reshape(volumes * count * hi_count * stride, LANES)
    block_mask = iota((LANES, LANES), 0) // breadth == iota((LANES, LANES), 1) // breadth
    zero_block = jnp.zeros((LANES, LANES), BF16)

    def pair_body(pair, carry):
        for spot, k in enumerate(offsets):
            row = spot * sides[0] * wide
            lane = spot * sides[1] * wide
            for half in range(2):
                term = group * per + pair * 2 + half
                high = jnp.concatenate([second_high[term, k]] * lo_count, axis=0)
                low = jnp.concatenate([second_low[term, k]] * lo_count, axis=0)
                high = jnp.where(block_mask, high, zero_block)
                low = jnp.where(block_mask, low, zero_block)
                tbuf[half, row : row + LANES, lane : lane + LANES] = high
                tbuf[half, row + LANES : row + wide, lane : lane + LANES] = high
                tbuf[half, row : row + LANES, lane + LANES : lane + wide] = low
        for half in range(2):
            term = pair * 2 + half
            for n in range(count):
                for g in range(volumes):
                    base = (g * count + n) * hi_count * stride + term * breadth
                    for a in range(0, breadth, 2):
                        pieces = [flat[pl.ds(base + a + d, hi_count, stride=stride), :] for d in range(2)]
                        high, low = split(jnp.concatenate(pieces, axis=0))
                        at = (n * breadth + a) * hi_count
                        lane = g * wide
                        lbuf[half, at : at + 2 * hi_count, lane : lane + LANES] = high
                        lbuf[half, at : at + 2 * hi_count, lane + LANES : lane + wide] = low
        results = []
        for half in range(2):
            line = []
            for (start, size), (row, rows), (lane, lanes) in recipes:
                full = product(
                    lbuf[half, :, start * wide : (start + size) * wide],
                    tbuf[half, row * wide : (row + rows) * wide, lane * wide : (lane + lanes) * wide],
                )
                for out in range(lanes):
                    line.append(full[:, out * wide : out * wide + LANES] + full[:, out * wide + LANES : (out + 1) * wide])
            results.append(line)
        for q in range(len(results[0])):
            for at in range(count * breadth):
                both = jnp.concatenate(
                    [results[half][q][at * hi_count : (at + 1) * hi_count] for half in range(2)], axis=0
                )
                high, low = split(both)
                emit(q, pair, at // 2, (at % 2) * LANES, high, low)
        return carry

    lax.fori_loop(0, per // 2, pair_body, 0, unroll=UNROLL)


def pick_diagonal(wide, breadth):
    lane_block = iota((breadth, wide.shape[1]), 1) % LANES // breadth
    total = wide[:breadth]
    for low in range(1, LANES // breadth):
        total = jnp.where(lane_block == low, wide[low * breadth : (low + 1) * breadth], total)
    return total


def turn_block(obuf, base, breadth, store):
    stride = breadth + PAD
    lo_count = LANES // breadth
    lane_of = iota((8, LANES), 1) // breadth
    for a in range(0, breadth, 8):
        for high in range(breadth // lo_count):
            level = [
                obuf[pl.ds(base + a * stride + high * lo_count + low, 8, stride=stride), :] for low in range(lo_count)
            ]
            step = 1
            while step < lo_count:
                own_side = (lane_of // step) % 2 == 0
                level = [
                    jnp.where(own_side, p, q) + pltpu.roll(jnp.where(own_side, q, p), step * breadth, 1)
                    for p, q in zip(level[::2], level[1::2])
                ]
                step *= 2
            store(a, high * LANES, level[0])


def merge_kernel(where, own, *refs, parts):
    sources = refs[:parts]
    first, second_high, second_low, third, out = refs[parts : parts + 5]
    vols, xbuf, ubuf, lbuf, tbuf, rbuf, obuf, sems = refs[parts + 5 :]
    count, breadth, width = own.shape
    rows = first.shape[0] // third.shape[0]
    per = rows // breadth
    kgroup = per * breadth * breadth // LANES

    def copies(action):
        for n in range(count):
            for axis in range(3):
                slot = n * 3 + axis
                at = where[n, axis]
                start = 0
                for source in sources:
                    size = source.shape[0]

                    @pl.when((at >= start) & (at < start + size))
                    def _(source=source, start=start, slot=slot, at=at):
                        action(pltpu.make_async_copy(source.at[at - start], vols.at[slot], sems.at[slot]))

                    start += size

    copies(lambda c: c.start())
    for n in range(count):
        for axis in range(3):

            @pl.when(where[n, axis] < 0)
            def _(slot=n * 3 + axis):
                vols[slot] = jnp.zeros((breadth, width), F32)

    tbuf[...] = jnp.zeros(tbuf.shape, BF16)
    xbuf[...] = jnp.zeros(xbuf.shape, BF16)
    copies(lambda c: c.wait())
    stride = breadth + PAD

    def group_body(group, carry):
        top = pl.multiple_of(group * rows, 8)
        for n in range(count):
            fill(xbuf, 0, vols[n * 3])
            fill(xbuf, 1, own[n])
            place(ubuf, 0, n, product(first[pl.ds(top, rows), : 2 * LANES], xbuf[...]))
            for g, axis in ((1, 2), (2, 1)):
                fill(xbuf, 0, vols[n * 3 + axis])
                place(ubuf, g, n, product(first[pl.ds(top, rows), LANES : 2 * LANES], xbuf[:LANES]))

        def emit(q, pair, tile, lane, high, low):
            step = high.shape[0]
            row = pl.multiple_of(q * kgroup + pair * step, step)
            rbuf[tile, pl.ds(row, step), lane : lane + LANES] = high
            rbuf[tile, pl.ds(row + 2 * kgroup, step), lane : lane + LANES] = low
            rbuf[tile, pl.ds(row + 4 * kgroup, step), lane : lane + LANES] = high

        recipes = (((0, 2), (0, 2), (0, 1)), ((2, 1), (0, 1), (0, 1)))
        second_stage(
            ubuf, lbuf, tbuf, second_high, second_low, group, per, breadth, (1, 0), (1, 0), recipes, emit
        )
        for tile in range(count * breadth // 2):
            total = pick_diagonal(product(third[group], rbuf[tile]), breadth)
            for d in range(2):
                row = (tile * 2 + d) * stride
                old = jnp.where(group == 0, 0.0, obuf[row : row + breadth])
                obuf[row : row + breadth] = old + total[:, d * LANES : (d + 1) * LANES]
        return carry

    lax.fori_loop(0, third.shape[0], group_body, 0)
    for n in range(count):

        def store(a, lane, value, n=n):
            out[n, a : a + 8, lane : lane + LANES] = value

        turn_block(obuf, n * breadth * stride, breadth, store)


def spread_kernel(where, own, *refs):
    first, second_high, second_low, third, keep, send = refs[:6]
    xbuf, ubuf, lbuf, tbuf, rbuf, obuf, block = refs[6:]
    count, breadth, width = own.shape
    rows = first.shape[0] // third.shape[0]
    per = rows // breadth
    kgroup = per * breadth * breadth // LANES
    half_slots = keep.shape[0]
    keep[...] = jnp.zeros(keep.shape, F32)
    send[...] = jnp.zeros(send.shape, F32)
    tbuf[...] = jnp.zeros(tbuf.shape, BF16)
    xbuf[...] = jnp.zeros(xbuf.shape, BF16)
    stride = breadth + PAD

    def group_body(group, carry):
        top = pl.multiple_of(group * rows, 8)
        for n in range(count):
            fill(xbuf, 0, own[n])
            for g in range(2):
                place(ubuf, g, n, product(first[pl.ds(top, rows), (1 + g) * LANES : (2 + g) * LANES], xbuf[...]))

        def emit(q, pair, tile, lane, high, low):
            step = high.shape[0]
            row = pl.multiple_of(q * 3 * kgroup + pair * step, step)
            rbuf[tile, pl.ds(row, step), lane : lane + LANES] = high
            rbuf[tile, pl.ds(row + kgroup, step), lane : lane + LANES] = low
            rbuf[tile, pl.ds(row + 2 * kgroup, step), lane : lane + LANES] = high

        recipes = (((1, 1), (0, 1), (0, 1)), ((0, 1), (0, 1), (0, 2)))
        second_stage(
            ubuf, lbuf, tbuf, second_high, second_low, group, per, breadth, (1, 2), (0, 1), recipes, emit
        )
        for tile in range(count * breadth // 2):
            for q in range(3):
                wide = product(third[group, 1 if q == 1 else 0], rbuf[tile, q * 3 * kgroup : (q + 1) * 3 * kgroup])
                total = pick_diagonal(wide, breadth)
                for d in range(2):
                    row = (tile * 2 + d) * stride
                    old = jnp.where(group == 0, 0.0, obuf[q, row : row + breadth])
                    obuf[q, row : row + breadth] = old + total[:, d * LANES : (d + 1) * LANES]
        return carry

    lax.fori_loop(0, third.shape[0], group_body, 0)
    for n in range(count):
        for q in range(3):

            def store(a, lane, value):
                block[a : a + 8, lane : lane + LANES] = value

            turn_block(obuf.at[q], n * breadth * stride, breadth, store)
            slot = where[n, q]

            @pl.when((slot >= 0) & (slot < half_slots))
            def _(slot=slot):
                keep[slot] = keep[slot] + block[...]

            @pl.when(slot >= half_slots)
            def _(slot=slot):
                send[slot - half_slots] = send[slot - half_slots] + block[...]


def stage_scratch(volumes, spots, recipes, count, breadth, per):
    hi_count = breadth * breadth // LANES
    return [
        pltpu.VMEM((volumes, count, hi_count, per * breadth + PAD, LANES), F32),
        pltpu.VMEM((2, count * breadth * hi_count, volumes * 2 * LANES), BF16),
        pltpu.VMEM((2, spots[0] * 2 * LANES, spots[1] * 2 * LANES), BF16),
        pltpu.VMEM((count * breadth // 2, recipes * 3 * per * hi_count, 2 * LANES), BF16),
    ]


def cost(count, breadth, per, units):
    return pl.CostEstimate(flops=units * per * 2 * count * breadth**4 * 200, transcendentals=0, bytes_accessed=1 << 22)


def stage_call(kernel, name, where, own, extra, weights, third, groups, out_shapes, scratch, units):
    first, second_high, second_low = weights
    breadth = own.shape[1]
    terms = second_high.shape[0]
    per = terms // groups
    return pl.pallas_call(
        kernel,
        out_shape=out_shapes,
        in_specs=[pl.BlockSpec(memory_space=pltpu.SMEM), pl.BlockSpec(memory_space=pltpu.VMEM)]
        + [pl.BlockSpec(memory_space=pl.ANY)] * len(extra)
        + [pl.BlockSpec(memory_space=pltpu.VMEM)] * 4,
        out_specs=[pl.BlockSpec(memory_space=pltpu.VMEM)] * len(out_shapes),
        scratch_shapes=scratch,
        compiler_params=pltpu.CompilerParams(vmem_limit_bytes=36 << 20),
        cost_estimate=cost(own.shape[0], breadth, terms, units),
        name=name,
    )(where, own, *extra, first, second_high, second_low, third)


def merge_call(where, own, parts, weights, third, groups):
    count, breadth, width = own.shape
    per = weights[1].shape[0] // groups
    scratch = stage_scratch(3, (2, 1), 2, count, breadth, per)
    scratch = (
        [pltpu.VMEM((count * 3, breadth, width), F32), pltpu.VMEM((2 * LANES, width), BF16)]
        + scratch
        + [pltpu.VMEM((count * breadth * (breadth + PAD), LANES), F32), pltpu.SemaphoreType.DMA((count * 3,))]
    )
    return stage_call(
        functools.partial(merge_kernel, parts=len(parts)),
        "merge",
        where,
        own,
        list(parts),
        weights,
        third,
        groups,
        [jax.ShapeDtypeStruct(own.shape, F32)],
        scratch,
        9,
    )[0]


def spread_call(where, own, slots, weights, third, groups):
    count, breadth, width = own.shape
    per = weights[1].shape[0] // groups
    scratch = stage_scratch(2, (1, 2), 3, count, breadth, per)
    scratch = (
        [pltpu.VMEM((LANES, width), BF16)]
        + scratch
        + [pltpu.VMEM((3, count * breadth * (breadth + PAD), LANES), F32), pltpu.VMEM((breadth, width), F32)]
    )
    shape = jax.ShapeDtypeStruct((slots // 2, breadth, width), F32)
    return stage_call(
        spread_kernel,
        "spread",
        where,
        own,
        [],
        weights,
        third,
        groups,
        [shape, shape],
        scratch,
        8,
    )


def to_row(column):
    size = column.shape[0]
    diagonal = iota((size, size), 0) == iota((size, size), 1)
    return jnp.sum(jnp.where(diagonal, column, 0.0), axis=0, keepdims=True)


def to_column(row):
    size = row.shape[1]
    diagonal = iota((size, size), 0) == iota((size, size), 1)
    return jnp.sum(jnp.where(diagonal, row, 0.0), axis=1, keepdims=True)


def place_row(slot_row, row, runs, run_size, capacity):
    held = slot_row.shape[1]
    run_row = jnp.zeros(slot_row.shape, F32)
    for r in range(1, runs):
        run_row = run_row + jnp.where(slot_row >= r * run_size, 1.0, 0.0)
    same = to_column(run_row) == run_row
    earlier = iota((held, held), 0) < iota((held, held), 1)
    before = jnp.sum(jnp.where(same & earlier, 1.0, 0.0), axis=0, keepdims=True)
    far_row = run_row - row.astype(F32)
    far_row = jnp.where(far_row < 0.0, far_row + runs, far_row)
    return far_row * capacity + before


def pack_kernel(row, slot_row, fine, *refs, run_size):
    outs, stack = refs[:-1], refs[-1]
    held, volume = fine.shape
    runs = len(outs)
    capacity = outs[0].shape[0]
    places = runs * capacity
    slots = slot_row[...]
    place = place_row(slots, row[0], runs, run_size, capacity)
    hit = iota((places, held), 0).astype(F32) == place
    ids = jnp.sum(jnp.where(hit, slots.astype(F32) + 1.0, 0.0), axis=1, keepdims=True)
    ids = jnp.broadcast_to(ids, (places, LANES))
    one = jnp.where(hit, 1.0, 0.0).astype(BF16)
    rest = fine[...]
    for part in range(3):
        head = rest.astype(BF16)
        stack[part * held : (part + 1) * held] = head
        rest = rest - head.astype(F32)
    packed = product(jnp.concatenate([one] * 3, axis=1), stack[...])
    for k in range(runs):
        outs[k][:, :volume] = packed[k * capacity : (k + 1) * capacity]
        outs[k][:, volume:] = ids[k * capacity : (k + 1) * capacity]


def unpack_kernel(row, slot_row, *refs, run_size):
    backs = refs[:-2]
    out, stack = refs[-2:]
    held, volume = out.shape
    runs = len(backs)
    capacity = backs[0].shape[0]
    places = runs * capacity
    place = to_column(place_row(slot_row[...], row[0], runs, run_size, capacity))
    hit = iota((held, places), 1).astype(F32) == place
    one = jnp.where(hit, 1.0, 0.0).astype(BF16)
    rest = jnp.concatenate([back[...] for back in backs], axis=0)
    for part in range(3):
        head = rest.astype(BF16)
        stack[part * places : (part + 1) * places] = head
        rest = rest - head.astype(F32)
    out[...] = product(jnp.concatenate([one] * 3, axis=1), stack[...])


def child_code(ids, held):
    at = ids - 1.0
    return jnp.where(at < 0.0, -1.0, at - held * jnp.floor(at / held))


def row_code(index, count):
    inner = index & 7
    code = (inner >> 1) * 8 + (inner & 1) * 4 + (index >> 3)
    return jnp.where(inner < 2 * count, code.astype(F32), -2.0)


def child_rows(filter_matrix, count):
    breadth = filter_matrix.shape[0]
    half = breadth // 2
    lane = iota((breadth, half * 8), 1)
    inner = lane & 7
    hot = iota((breadth, half * 8), 0) == (inner & 1) * half + (lane >> 3)
    spread = exact_expand(filter_matrix, hot)
    return jnp.concatenate([jnp.where(inner >> 1 == n, spread, 0.0) for n in range(count)], axis=0)


def triple_lanes(x):
    high, low = split(x)
    return jnp.concatenate([high, high, low], axis=1)


def filter_kernel(filter_ref, *refs, count):
    got = refs[:-6]
    out, ids, stack, lines, cross, weave = refs[-6:]
    runs = len(got)
    capacity, volume = got[0].shape
    volume = volume - LANES
    places = runs * capacity
    breadth = filter_ref.shape[0]
    half = breadth // 2
    width = out.shape[2]
    face = width // 4
    span = volume // face
    lo_count = LANES // breadth
    hi_count = breadth // lo_count
    matrix = filter_ref[...]
    turned = matrix.T
    lane = iota((breadth, width), 1)
    outer = lane // breadth
    across_z = exact_expand(turned, iota((breadth, width), 0) == lane % breadth)
    across_y = exact_expand(turned, iota((breadth, width), 0) == (outer % lo_count) * hi_count + outer // lo_count)
    for g in range(4):
        zs = across_z[(g & 1) * half : (g & 1) * half + half]
        for j in range(half):
            row = (g >> 1) * half + j
            high, low = split(zs * across_y[row : row + 1])
            at = (g * half + j) * half
            cross[0, at : at + half] = high
            cross[1, at : at + half] = low
    joined = jnp.concatenate([piece[...] for piece in got], axis=0)
    ids[...] = jnp.concatenate([got[(runs - k) % runs][:, volume:] for k in range(runs)], axis=0)
    code = to_row(child_code(joined[:, volume : volume + 1], 8 * count))
    hit = row_code(iota((32, places), 0), count) == code
    one = jnp.where(hit, 1.0, 0.0).astype(BF16)
    high, low = split(joined[:, :volume])
    stack[:places] = high
    stack[places:] = low
    boxes = product(jnp.concatenate([one, one], axis=1), stack[...])
    for g in range(4):
        for i in range(0, span, 2):
            both = jnp.concatenate(
                [boxes[g * 8 : g * 8 + 8, (i + d) * face : (i + d + 1) * face] for d in range(2)], axis=0
            )
            high, low = split(both)
            lines[0, i * 8 : i * 8 + 16, g * face : (g + 1) * face] = high
            lines[1, i * 8 : i * 8 + 16, g * face : (g + 1) * face] = low
    total = product(lines[0], cross[0]) + product(lines[1], cross[0]) + product(lines[0], cross[1])
    high, low = split(total)
    size = total.shape[0]
    weave[:size] = high
    weave[size : 2 * size] = low
    weave[2 * size :] = high
    result = product(triple_lanes(child_rows(matrix, count)), weave[...])
    for n in range(count):
        out[n] = result[n * breadth : (n + 1) * breadth]


def unfilter_kernel(filter_ref, ids, *refs, count, runs):
    outs = refs[-3 - runs : -3]
    applied = refs[: -3 - runs]
    weave, cross, stack = refs[-3:]
    capacity, volume = outs[0].shape
    places = runs * capacity
    breadth = filter_ref.shape[0]
    half = breadth // 2
    width = applied[0].shape[2]
    face = width // 4
    size = count * breadth
    matrix = filter_ref[...]
    lane = iota((breadth, width), 1)
    octant = lane // face
    across_c = exact_expand(matrix, iota((breadth, width), 0) == octant % 2 * half + lane % half)
    across_b = exact_expand(matrix, iota((breadth, width), 0) == octant // 2 * half + lane // half % half)
    for b in range(breadth):
        high, low = split(across_c * across_b[b : b + 1])
        cross[0, b * breadth : (b + 1) * breadth] = high
        cross[1, b * breadth : (b + 1) * breadth] = low
    for n in range(count):
        total = applied[0][n]
        for piece in applied[1:]:
            total = total + piece[n]
        high, low = split(total)
        at = n * breadth
        weave[at : at + breadth] = high
        weave[size + at : size + at + breadth] = low
        weave[2 * size + at : 2 * size + at + breadth] = high
    lines = product(triple_lanes(child_rows(matrix, count).T), weave[...])
    high, low = split(lines)
    total = product(high, cross[0]) + product(low, cross[0]) + product(high, cross[1])
    for g in range(0, 4, 2):
        for i in range(total.shape[0] // 8):
            both = jnp.concatenate(
                [total[i * 8 : i * 8 + 8, (g + d) * face : (g + d + 1) * face] for d in range(2)], axis=0
            )
            high, low = split(both)
            stack[g * 8 : g * 8 + 16, i * face : (i + 1) * face] = high
            stack[32 + g * 8 : 32 + g * 8 + 16, i * face : (i + 1) * face] = low
    code = child_code(ids[:, :1], 8 * count)
    hit = row_code(iota((places, 32), 1), count) == code
    one = jnp.where(hit, 1.0, 0.0).astype(BF16)
    packed = product(jnp.concatenate([one, one], axis=1), stack[...])
    for k in range(runs):
        outs[k][...] = packed[k * capacity : (k + 1) * capacity]


def vmem_call(kernel, out_shape, scratch, name, in_specs=None, room=14, outputs=1, **settings):
    extra = {} if in_specs is None else dict(in_specs=in_specs)
    if isinstance(out_shape, list):
        shapes = [jax.ShapeDtypeStruct(shape, F32) for shape in out_shape]
    else:
        shapes = jax.ShapeDtypeStruct(out_shape, F32)
    if outputs > 1:
        shapes = [shapes] * outputs
    return pl.pallas_call(
        functools.partial(kernel, **settings),
        out_shape=shapes,
        scratch_shapes=[pltpu.VMEM(shape, dtype) for shape, dtype in scratch],
        compiler_params=pltpu.CompilerParams(vmem_limit_bytes=room << 20),
        name=name,
        **extra,
    )


def moved(array, row_step, bit):
    rows = lax.axis_size("row")
    cols = lax.axis_size("col")
    pairs = [
        (r * cols + c, (r + row_step) % rows * cols + (c ^ bit)) for r in range(rows) for c in range(cols)
    ]
    return lax.ppermute(array, ("row", "col"), pairs)


def local(fine_coeffs, fine_slot, neighbours, filter_matrix, kernel_ops):
    breadth = filter_matrix.shape[0]
    terms = kernel_ops.shape[0]
    runs = lax.axis_size("row")
    cols = lax.axis_size("col")
    held, volume = fine_coeffs.shape
    par_row = neighbours.shape[0]
    count = held // 8
    capacity = 2 * (held // runs)
    places = runs * capacity
    width = breadth * breadth
    hi_count = width // LANES
    groups = 2
    per = terms // groups
    uppers = range(0, cols, 2)

    slot_row = fine_slot.reshape(1, held)
    routing = dict(run_size=8 * par_row)
    row = jnp.full((1,), lax.axis_index("row"), jnp.int32)
    scalar = pl.BlockSpec(memory_space=pltpu.SMEM)
    plain = pl.BlockSpec(memory_space=pltpu.VMEM)
    sent = vmem_call(
        pack_kernel,
        (capacity, volume + LANES),
        [((3 * held, volume), BF16)],
        "pack",
        in_specs=[scalar, plain, plain],
        room=ROOM,
        outputs=runs,
        **routing,
    )(row, slot_row, fine_coeffs)
    got = [sent[0]] + [moved(sent[k], k, 0) for k in range(1, runs)]

    first, second_high, second_low, merge_third, spread_third = pl.pallas_call(
        functools.partial(prepare_kernel, groups=groups),
        out_shape=[
            jax.ShapeDtypeStruct((terms * breadth, 3 * LANES), BF16),
            jax.ShapeDtypeStruct((terms, 3, breadth, LANES), BF16),
            jax.ShapeDtypeStruct((terms, 3, breadth, LANES), BF16),
            jax.ShapeDtypeStruct((groups, LANES, 6 * per * hi_count), BF16),
            jax.ShapeDtypeStruct((groups, 2, LANES, 3 * per * hi_count), BF16),
        ],
        scratch_shapes=[pltpu.VMEM((terms * 9 * breadth, LANES), F32)],
        compiler_params=pltpu.CompilerParams(vmem_limit_bytes=PREP << 20),
        name="prepare",
    )(kernel_ops.reshape(terms * 9 * hi_count, LANES))
    weights = (first, second_high, second_low)

    col_index = lax.axis_index("col")
    mine = lax.dynamic_slice_in_dim(neighbours, col_index * count, count, 0)[:, ::2]
    within = mine % par_row
    relation = (within // count) ^ col_index
    spot = (relation % 2) * (len(uppers) * count) + relation // 2 * count + within % count
    where = jnp.where(mine >= 0, spot, -1)

    filtered, ids = vmem_call(
        filter_kernel,
        [(count, breadth, width), (places, LANES)],
        [
            ((2 * places, volume), BF16),
            ((2, breadth * 4, width), BF16),
            ((2, width, width), BF16),
            ((12 * breadth, width), BF16),
        ],
        "filter",
        count=count,
    )(filter_matrix, *got)

    parts = [moved(filtered, -1, u) for u in uppers]
    keep, send = spread_call(where, filtered, par_row, weights, spread_third, groups)
    parts, keep, send = lax.optimization_barrier((parts, keep, send))
    parts = parts + [moved(part, 0, 1) for part in parts]
    came = moved(send, 0, 1)

    terms_out = []
    for u in uppers:
        at = u // 2 * count
        terms_out.append(moved(keep[at : at + count] + came[at : at + count], 1, u))
    pieces = [merge_call(where, filtered, parts, weights, merge_third, groups)] + terms_out
    results = vmem_call(
        unfilter_kernel,
        (capacity, volume),
        [
            ((3 * count * breadth, width), BF16),
            ((2, width, width), BF16),
            ((64, volume), BF16),
        ],
        "unfilter",
        in_specs=[plain] * (2 + len(pieces)),
        outputs=runs,
        count=count,
        runs=runs,
    )(filter_matrix, ids, *pieces)
    backs = [results[0]] + [moved(results[runs - j], -j, 0) for j in range(1, runs)]
    return vmem_call(
        unpack_kernel,
        (held, volume),
        [((3 * places, volume), BF16)],
        "unpack",
        in_specs=[scalar, plain] + [plain] * runs,
        **routing,
    )(row, slot_row, *backs)


def solution(mesh):
    in_specs = (P(("row", "col"), None), P(("row", "col")), P("row", None), P(), P())
    out_specs = P(("row", "col"), None)
    return jax.shard_map(local, mesh=mesh, in_specs=in_specs, out_specs=out_specs, check_vma=False)
```

```python
import functools

import jax
import jax.numpy as jnp
import numpy as np
from jax import lax
from jax.experimental import pallas as pl
from jax.experimental.pallas import tpu as pltpu
from jax.sharding import PartitionSpec as P

F32, BF16 = jnp.float32, jnp.bfloat16
LANES = 128
PAD = 8
UNROLL = True
ROOM = 60
PREP = 14


def iota(shape, axis):
    return lax.broadcasted_iota(jnp.int32, shape, axis)


def split(x):
    high = x.astype(BF16)
    return high, (x - high.astype(F32)).astype(BF16)


def product(a, b):
    return jnp.dot(a, b, preferred_element_type=F32)


def exact_expand(x, hot):
    one = jnp.where(hot, 1.0, 0.0).astype(BF16)
    total = None
    for part in range(3):
        head = x.astype(BF16)
        piece = product(head, one)
        total = piece if total is None else total + piece
        x = x - head.astype(F32)
    return total


def prepare_kernel(packed, first, second_high, second_low, merge, spread, ops, *, groups):
    terms = second_high.shape[0]
    breadth = second_high.shape[2]
    lo_count = LANES // breadth
    hi_count = breadth // lo_count
    per = terms // groups
    stride = breadth + PAD
    for axis in range(3):
        for k in range(3):
            for high in range(hi_count):
                block = packed[axis, k, :, high * LANES : (high + 1) * LANES]
                for low in range(lo_count):
                    turned = block if low == 0 else pltpu.roll(block, LANES - low * breadth, 1)
                    at = (axis * 3 + k) * terms * stride + high * lo_count + low
                    ops[pl.ds(at, terms, stride=stride), :] = turned

    def factor(term, axis, k):
        at = ((axis * 3 + k) * terms + term) * stride
        return ops[at : at + breadth, :breadth]

    blank = jnp.zeros((breadth, LANES - 3 * breadth), F32)
    for term in range(terms):
        for k in range(3):
            value = factor(term, 0, k)
            high = value.astype(BF16).astype(F32)
            line = jnp.concatenate([high, high, value - high, blank], axis=1)
            first[term * breadth : (term + 1) * breadth, k * LANES : (k + 1) * LANES] = line.astype(BF16)
        turned = jnp.concatenate([factor(term, 2, k) for k in range(3)], axis=0).T
        for k in range(3):
            high, low = split(jnp.concatenate([turned[:, k * breadth : (k + 1) * breadth]] * lo_count, axis=1))
            second_high[term, k] = high
            second_low[term, k] = low
    for g in range(groups):
        for inner in range(lo_count):
            strip = [
                jnp.concatenate(
                    [factor(g * per + t, 1, k)[:, inner * hi_count : (inner + 1) * hi_count] for t in range(per)], axis=1
                )
                for k in range(3)
            ]
            value = jnp.concatenate([strip[1], strip[0]], axis=1)
            high = value.astype(BF16).astype(F32)
            line = jnp.concatenate([high, high, value - high], axis=1)
            merge[g, inner * breadth : (inner + 1) * breadth] = line.astype(BF16)
            for s, k in enumerate((1, 2)):
                high = strip[k].astype(BF16).astype(F32)
                line = jnp.concatenate([high, high, strip[k] - high], axis=1)
                spread[g, s, inner * breadth : (inner + 1) * breadth] = line.astype(BF16)


def fill(xbuf, slot, block):
    breadth = block.shape[0]
    high, low = split(block)
    base = slot * LANES
    xbuf[base : base + breadth] = high
    xbuf[base + breadth : base + 2 * breadth] = low
    xbuf[base + 2 * breadth : base + 3 * breadth] = high


def place(ubuf, g, n, result):
    rows = result.shape[0]
    for h in range(result.shape[1] // LANES):
        ubuf[g, n, h, :rows] = result[:, h * LANES : (h + 1) * LANES]


def second_stage(ubuf, lbuf, tbuf, second_high, second_low, group, per, breadth, offsets, sides, recipes, emit):
    volumes, count, hi_count, stride = ubuf.shape[:4]
    lo_count = LANES // breadth
    wide = 2 * LANES
    flat = ubuf.reshape(volumes * count * hi_count * stride, LANES)
    block_mask = iota((LANES, LANES), 0) // breadth == iota((LANES, LANES), 1) // breadth
    zero_block = jnp.zeros((LANES, LANES), BF16)

    def pair_body(pair, carry):
        for spot, k in enumerate(offsets):
            row = spot * sides[0] * wide
            lane = spot * sides[1] * wide
            for half in range(2):
                term = group * per + pair * 2 + half
                high = jnp.concatenate([second_high[term, k]] * lo_count, axis=0)
                low = jnp.concatenate([second_low[term, k]] * lo_count, axis=0)
                high = jnp.where(block_mask, high, zero_block)
                low = jnp.where(block_mask, low, zero_block)
                tbuf[half, row : row + LANES, lane : lane + LANES] = high
                tbuf[half, row + LANES : row + wide, lane : lane + LANES] = high
                tbuf[half, row : row + LANES, lane + LANES : lane + wide] = low
        for half in range(2):
            term = pair * 2 + half
            for n in range(count):
                for g in range(volumes):
                    base = (g * count + n) * hi_count * stride + term * breadth
                    for a in range(0, breadth, 2):
                        pieces = [flat[pl.ds(base + a + d, hi_count, stride=stride), :] for d in range(2)]
                        high, low = split(jnp.concatenate(pieces, axis=0))
                        at = (n * breadth + a) * hi_count
                        lane = g * wide
                        lbuf[half, at : at + 2 * hi_count, lane : lane + LANES] = high
                        lbuf[half, at : at + 2 * hi_count, lane + LANES : lane + wide] = low
        results = []
        for half in range(2):
            line = []
            for (start, size), (row, rows), (lane, lanes) in recipes:
                full = product(
                    lbuf[half, :, start * wide : (start + size) * wide],
                    tbuf[half, row * wide : (row + rows) * wide, lane * wide : (lane + lanes) * wide],
                )
                for out in range(lanes):
                    line.append(full[:, out * wide : out * wide + LANES] + full[:, out * wide + LANES : (out + 1) * wide])
            results.append(line)
        for q in range(len(results[0])):
            for at in range(count * breadth):
                both = jnp.concatenate(
                    [results[half][q][at * hi_count : (at + 1) * hi_count] for half in range(2)], axis=0
                )
                high, low = split(both)
                emit(q, pair, at // 2, (at % 2) * LANES, high, low)
        return carry

    lax.fori_loop(0, per // 2, pair_body, 0, unroll=UNROLL)


def pick_diagonal(wide, breadth):
    lane_block = iota((breadth, wide.shape[1]), 1) % LANES // breadth
    total = wide[:breadth]
    for low in range(1, LANES // breadth):
        total = jnp.where(lane_block == low, wide[low * breadth : (low + 1) * breadth], total)
    return total


def turn_block(obuf, base, breadth, store):
    stride = breadth + PAD
    lo_count = LANES // breadth
    lane_of = iota((8, LANES), 1) // breadth
    for a in range(0, breadth, 8):
        for high in range(breadth // lo_count):
            level = [
                obuf[pl.ds(base + a * stride + high * lo_count + low, 8, stride=stride), :] for low in range(lo_count)
            ]
            step = 1
            while step < lo_count:
                own_side = (lane_of // step) % 2 == 0
                level = [
                    jnp.where(own_side, p, q) + pltpu.roll(jnp.where(own_side, q, p), step * breadth, 1)
                    for p, q in zip(level[::2], level[1::2])
                ]
                step *= 2
            store(a, high * LANES, level[0])


def merge_kernel(where, own, *refs, parts):
    sources = refs[:parts]
    first, second_high, second_low, third, out = refs[parts : parts + 5]
    vols, xbuf, ubuf, lbuf, tbuf, rbuf, obuf, sems = refs[parts + 5 :]
    count, breadth, width = own.shape
    rows = first.shape[0] // third.shape[0]
    per = rows // breadth
    kgroup = per * breadth * breadth // LANES

    def copies(action):
        for n in range(count):
            for axis in range(3):
                slot = n * 3 + axis
                at = where[n, axis]
                start = 0
                for source in sources:
                    size = source.shape[0]

                    @pl.when((at >= start) & (at < start + size))
                    def _(source=source, start=start, slot=slot, at=at):
                        action(pltpu.make_async_copy(source.at[at - start], vols.at[slot], sems.at[slot]))

                    start += size

    copies(lambda c: c.start())
    for n in range(count):
        for axis in range(3):

            @pl.when(where[n, axis] < 0)
            def _(slot=n * 3 + axis):
                vols[slot] = jnp.zeros((breadth, width), F32)

    tbuf[...] = jnp.zeros(tbuf.shape, BF16)
    xbuf[...] = jnp.zeros(xbuf.shape, BF16)
    copies(lambda c: c.wait())
    stride = breadth + PAD

    def group_body(group, carry):
        top = pl.multiple_of(group * rows, 8)
        for n in range(count):
            fill(xbuf, 0, vols[n * 3])
            fill(xbuf, 1, own[n])
            place(ubuf, 0, n, product(first[pl.ds(top, rows), : 2 * LANES], xbuf[...]))
            for g, axis in ((1, 2), (2, 1)):
                fill(xbuf, 0, vols[n * 3 + axis])
                place(ubuf, g, n, product(first[pl.ds(top, rows), LANES : 2 * LANES], xbuf[:LANES]))

        def emit(q, pair, tile, lane, high, low):
            step = high.shape[0]
            row = pl.multiple_of(q * kgroup + pair * step, step)
            rbuf[tile, pl.ds(row, step), lane : lane + LANES] = high
            rbuf[tile, pl.ds(row + 2 * kgroup, step), lane : lane + LANES] = low
            rbuf[tile, pl.ds(row + 4 * kgroup, step), lane : lane + LANES] = high

        recipes = (((0, 2), (0, 2), (0, 1)), ((2, 1), (0, 1), (0, 1)))
        second_stage(
            ubuf, lbuf, tbuf, second_high, second_low, group, per, breadth, (1, 0), (1, 0), recipes, emit
        )
        for tile in range(count * breadth // 2):
            total = pick_diagonal(product(third[group], rbuf[tile]), breadth)
            for d in range(2):
                row = (tile * 2 + d) * stride
                old = jnp.where(group == 0, 0.0, obuf[row : row + breadth])
                obuf[row : row + breadth] = old + total[:, d * LANES : (d + 1) * LANES]
        return carry

    lax.fori_loop(0, third.shape[0], group_body, 0)
    for n in range(count):

        def store(a, lane, value, n=n):
            out[n, a : a + 8, lane : lane + LANES] = value

        turn_block(obuf, n * breadth * stride, breadth, store)


def spread_kernel(where, own, *refs):
    first, second_high, second_low, third, keep, send = refs[:6]
    xbuf, ubuf, lbuf, tbuf, rbuf, obuf, block = refs[6:]
    count, breadth, width = own.shape
    rows = first.shape[0] // third.shape[0]
    per = rows // breadth
    kgroup = per * breadth * breadth // LANES
    half_slots = keep.shape[0]
    keep[...] = jnp.zeros(keep.shape, F32)
    send[...] = jnp.zeros(send.shape, F32)
    tbuf[...] = jnp.zeros(tbuf.shape, BF16)
    xbuf[...] = jnp.zeros(xbuf.shape, BF16)
    stride = breadth + PAD

    def group_body(group, carry):
        top = pl.multiple_of(group * rows, 8)
        for n in range(count):
            fill(xbuf, 0, own[n])
            for g in range(2):
                place(ubuf, g, n, product(first[pl.ds(top, rows), (1 + g) * LANES : (2 + g) * LANES], xbuf[...]))

        def emit(q, pair, tile, lane, high, low):
            step = high.shape[0]
            row = pl.multiple_of(q * 3 * kgroup + pair * step, step)
            rbuf[tile, pl.ds(row, step), lane : lane + LANES] = high
            rbuf[tile, pl.ds(row + kgroup, step), lane : lane + LANES] = low
            rbuf[tile, pl.ds(row + 2 * kgroup, step), lane : lane + LANES] = high

        recipes = (((1, 1), (0, 1), (0, 1)), ((0, 1), (0, 1), (0, 2)))
        second_stage(
            ubuf, lbuf, tbuf, second_high, second_low, group, per, breadth, (1, 2), (0, 1), recipes, emit
        )
        for tile in range(count * breadth // 2):
            for q in range(3):
                wide = product(third[group, 1 if q == 1 else 0], rbuf[tile, q * 3 * kgroup : (q + 1) * 3 * kgroup])
                total = pick_diagonal(wide, breadth)
                for d in range(2):
                    row = (tile * 2 + d) * stride
                    old = jnp.where(group == 0, 0.0, obuf[q, row : row + breadth])
                    obuf[q, row : row + breadth] = old + total[:, d * LANES : (d + 1) * LANES]
        return carry

    lax.fori_loop(0, third.shape[0], group_body, 0)
    for n in range(count):
        for q in range(3):

            def store(a, lane, value):
                block[a : a + 8, lane : lane + LANES] = value

            turn_block(obuf.at[q], n * breadth * stride, breadth, store)
            slot = where[n, q]

            @pl.when((slot >= 0) & (slot < half_slots))
            def _(slot=slot):
                keep[slot] = keep[slot] + block[...]

            @pl.when(slot >= half_slots)
            def _(slot=slot):
                send[slot - half_slots] = send[slot - half_slots] + block[...]


def stage_scratch(volumes, spots, recipes, count, breadth, per):
    hi_count = breadth * breadth // LANES
    return [
        pltpu.VMEM((volumes, count, hi_count, per * breadth + PAD, LANES), F32),
        pltpu.VMEM((2, count * breadth * hi_count, volumes * 2 * LANES), BF16),
        pltpu.VMEM((2, spots[0] * 2 * LANES, spots[1] * 2 * LANES), BF16),
        pltpu.VMEM((count * breadth // 2, recipes * 3 * per * hi_count, 2 * LANES), BF16),
    ]


def cost(count, breadth, per, units):
    return pl.CostEstimate(flops=units * per * 2 * count * breadth**4 * 200, transcendentals=0, bytes_accessed=1 << 22)


def stage_call(kernel, name, where, own, extra, weights, third, groups, out_shapes, scratch, units):
    first, second_high, second_low = weights
    breadth = own.shape[1]
    terms = second_high.shape[0]
    per = terms // groups
    return pl.pallas_call(
        kernel,
        out_shape=out_shapes,
        in_specs=[pl.BlockSpec(memory_space=pltpu.SMEM), pl.BlockSpec(memory_space=pltpu.VMEM)]
        + [pl.BlockSpec(memory_space=pl.ANY)] * len(extra)
        + [pl.BlockSpec(memory_space=pltpu.VMEM)] * 4,
        out_specs=[pl.BlockSpec(memory_space=pltpu.VMEM)] * len(out_shapes),
        scratch_shapes=scratch,
        compiler_params=pltpu.CompilerParams(vmem_limit_bytes=36 << 20),
        cost_estimate=cost(own.shape[0], breadth, terms, units),
        name=name,
    )(where, own, *extra, first, second_high, second_low, third)


def merge_call(where, own, parts, weights, third, groups):
    count, breadth, width = own.shape
    per = weights[1].shape[0] // groups
    scratch = stage_scratch(3, (2, 1), 2, count, breadth, per)
    scratch = (
        [pltpu.VMEM((count * 3, breadth, width), F32), pltpu.VMEM((2 * LANES, width), BF16)]
        + scratch
        + [pltpu.VMEM((count * breadth * (breadth + PAD), LANES), F32), pltpu.SemaphoreType.DMA((count * 3,))]
    )
    return stage_call(
        functools.partial(merge_kernel, parts=len(parts)),
        "merge",
        where,
        own,
        list(parts),
        weights,
        third,
        groups,
        [jax.ShapeDtypeStruct(own.shape, F32)],
        scratch,
        9,
    )[0]


def spread_call(where, own, slots, weights, third, groups):
    count, breadth, width = own.shape
    per = weights[1].shape[0] // groups
    scratch = stage_scratch(2, (1, 2), 3, count, breadth, per)
    scratch = (
        [pltpu.VMEM((LANES, width), BF16)]
        + scratch
        + [pltpu.VMEM((3, count * breadth * (breadth + PAD), LANES), F32), pltpu.VMEM((breadth, width), F32)]
    )
    shape = jax.ShapeDtypeStruct((slots // 2, breadth, width), F32)
    return stage_call(
        spread_kernel,
        "spread",
        where,
        own,
        [],
        weights,
        third,
        groups,
        [shape, shape],
        scratch,
        8,
    )


def to_row(column):
    size = column.shape[0]
    diagonal = iota((size, size), 0) == iota((size, size), 1)
    return jnp.sum(jnp.where(diagonal, column, 0.0), axis=0, keepdims=True)


def to_column(row):
    size = row.shape[1]
    diagonal = iota((size, size), 0) == iota((size, size), 1)
    return jnp.sum(jnp.where(diagonal, row, 0.0), axis=1, keepdims=True)


def place_row(slot_row, row, runs, run_size, capacity):
    held = slot_row.shape[1]
    run_row = jnp.zeros(slot_row.shape, F32)
    for r in range(1, runs):
        run_row = run_row + jnp.where(slot_row >= r * run_size, 1.0, 0.0)
    same = to_column(run_row) == run_row
    earlier = iota((held, held), 0) < iota((held, held), 1)
    before = jnp.sum(jnp.where(same & earlier, 1.0, 0.0), axis=0, keepdims=True)
    far_row = run_row - row.astype(F32)
    far_row = jnp.where(far_row < 0.0, far_row + runs, far_row)
    return far_row * capacity + before


def pack_kernel(row, slot_row, fine, *refs, run_size):
    outs, stack = refs[:-1], refs[-1]
    held, volume = fine.shape
    runs = len(outs)
    capacity = outs[0].shape[0]
    places = runs * capacity
    slots = slot_row[...]
    place = place_row(slots, row[0], runs, run_size, capacity)
    hit = iota((places, held), 0).astype(F32) == place
    ids = jnp.sum(jnp.where(hit, slots.astype(F32) + 1.0, 0.0), axis=1, keepdims=True)
    ids = jnp.broadcast_to(ids, (places, LANES))
    one = jnp.where(hit, 1.0, 0.0).astype(BF16)
    rest = fine[...]
    for part in range(3):
        head = rest.astype(BF16)
        stack[part * held : (part + 1) * held] = head
        rest = rest - head.astype(F32)
    packed = product(jnp.concatenate([one] * 3, axis=1), stack[...])
    for k in range(runs):
        outs[k][:, :volume] = packed[k * capacity : (k + 1) * capacity]
        outs[k][:, volume:] = ids[k * capacity : (k + 1) * capacity]


def unpack_kernel(row, slot_row, *refs, run_size):
    backs = refs[:-2]
    out, stack = refs[-2:]
    held, volume = out.shape
    runs = len(backs)
    capacity = backs[0].shape[0]
    places = runs * capacity
    place = to_column(place_row(slot_row[...], row[0], runs, run_size, capacity))
    hit = iota((held, places), 1).astype(F32) == place
    one = jnp.where(hit, 1.0, 0.0).astype(BF16)
    rest = jnp.concatenate([back[...] for back in backs], axis=0)
    for part in range(3):
        head = rest.astype(BF16)
        stack[part * places : (part + 1) * places] = head
        rest = rest - head.astype(F32)
    out[...] = product(jnp.concatenate([one] * 3, axis=1), stack[...])


def child_code(ids, held):
    at = ids - 1.0
    return jnp.where(at < 0.0, -1.0, at - held * jnp.floor(at / held))


def row_code(index, count):
    inner = index & 7
    code = (inner >> 1) * 8 + (inner & 1) * 4 + (index >> 3)
    return jnp.where(inner < 2 * count, code.astype(F32), -2.0)


def child_rows(filter_matrix, count):
    breadth = filter_matrix.shape[0]
    half = breadth // 2
    lane = iota((breadth, half * 8), 1)
    inner = lane & 7
    hot = iota((breadth, half * 8), 0) == (inner & 1) * half + (lane >> 3)
    spread = exact_expand(filter_matrix, hot)
    return jnp.concatenate([jnp.where(inner >> 1 == n, spread, 0.0) for n in range(count)], axis=0)


def triple_lanes(x):
    high, low = split(x)
    return jnp.concatenate([high, high, low], axis=1)


def filter_kernel(filter_ref, *refs, count):
    got = refs[:-6]
    out, ids, stack, lines, cross, weave = refs[-6:]
    runs = len(got)
    capacity, volume = got[0].shape
    volume = volume - LANES
    places = runs * capacity
    breadth = filter_ref.shape[0]
    half = breadth // 2
    width = out.shape[2]
    face = width // 4
    span = volume // face
    lo_count = LANES // breadth
    hi_count = breadth // lo_count
    matrix = filter_ref[...]
    turned = matrix.T
    lane = iota((breadth, width), 1)
    outer = lane // breadth
    across_z = exact_expand(turned, iota((breadth, width), 0) == lane % breadth)
    across_y = exact_expand(turned, iota((breadth, width), 0) == (outer % lo_count) * hi_count + outer // lo_count)
    for g in range(4):
        zs = across_z[(g & 1) * half : (g & 1) * half + half]
        for j in range(half):
            row = (g >> 1) * half + j
            high, low = split(zs * across_y[row : row + 1])
            at = (g * half + j) * half
            cross[0, at : at + half] = high
            cross[1, at : at + half] = low
    joined = jnp.concatenate([piece[...] for piece in got], axis=0)
    ids[...] = jnp.concatenate([got[(runs - k) % runs][:, volume:] for k in range(runs)], axis=0)
    code = to_row(child_code(joined[:, volume : volume + 1], 8 * count))
    hit = row_code(iota((32, places), 0), count) == code
    one = jnp.where(hit, 1.0, 0.0).astype(BF16)
    high, low = split(joined[:, :volume])
    stack[:places] = high
    stack[places:] = low
    boxes = product(jnp.concatenate([one, one], axis=1), stack[...])
    for g in range(4):
        for i in range(0, span, 2):
            both = jnp.concatenate(
                [boxes[g * 8 : g * 8 + 8, (i + d) * face : (i + d + 1) * face] for d in range(2)], axis=0
            )
            high, low = split(both)
            lines[0, i * 8 : i * 8 + 16, g * face : (g + 1) * face] = high
            lines[1, i * 8 : i * 8 + 16, g * face : (g + 1) * face] = low
    total = product(lines[0], cross[0]) + product(lines[1], cross[0]) + product(lines[0], cross[1])
    high, low = split(total)
    size = total.shape[0]
    weave[:size] = high
    weave[size : 2 * size] = low
    weave[2 * size :] = high
    result = product(triple_lanes(child_rows(matrix, count)), weave[...])
    for n in range(count):
        out[n] = result[n * breadth : (n + 1) * breadth]


def unfilter_kernel(filter_ref, ids, *refs, count, runs):
    outs = refs[-3 - runs : -3]
    applied = refs[: -3 - runs]
    weave, cross, stack = refs[-3:]
    capacity, volume = outs[0].shape
    places = runs * capacity
    breadth = filter_ref.shape[0]
    half = breadth // 2
    width = applied[0].shape[2]
    face = width // 4
    size = count * breadth
    matrix = filter_ref[...]
    lane = iota((breadth, width), 1)
    octant = lane // face
    across_c = exact_expand(matrix, iota((breadth, width), 0) == octant % 2 * half + lane % half)
    across_b = exact_expand(matrix, iota((breadth, width), 0) == octant // 2 * half + lane // half % half)
    for b in range(breadth):
        high, low = split(across_c * across_b[b : b + 1])
        cross[0, b * breadth : (b + 1) * breadth] = high
        cross[1, b * breadth : (b + 1) * breadth] = low
    for n in range(count):
        total = applied[0][n]
        for piece in applied[1:]:
            total = total + piece[n]
        high, low = split(total)
        at = n * breadth
        weave[at : at + breadth] = high
        weave[size + at : size + at + breadth] = low
        weave[2 * size + at : 2 * size + at + breadth] = high
    lines = product(triple_lanes(child_rows(matrix, count).T), weave[...])
    high, low = split(lines)
    total = product(high, cross[0]) + product(low, cross[0]) + product(high, cross[1])
    for g in range(0, 4, 2):
        for i in range(total.shape[0] // 8):
            both = jnp.concatenate(
                [total[i * 8 : i * 8 + 8, (g + d) * face : (g + d + 1) * face] for d in range(2)], axis=0
            )
            high, low = split(both)
            stack[g * 8 : g * 8 + 16, i * face : (i + 1) * face] = high
            stack[32 + g * 8 : 32 + g * 8 + 16, i * face : (i + 1) * face] = low
    code = child_code(ids[:, :1], 8 * count)
    hit = row_code(iota((places, 32), 1), count) == code
    one = jnp.where(hit, 1.0, 0.0).astype(BF16)
    packed = product(jnp.concatenate([one, one], axis=1), stack[...])
    for k in range(runs):
        outs[k][...] = packed[k * capacity : (k + 1) * capacity]


def vmem_call(kernel, out_shape, scratch, name, in_specs=None, room=14, outputs=1, **settings):
    extra = {} if in_specs is None else dict(in_specs=in_specs)
    if isinstance(out_shape, list):
        shapes = [jax.ShapeDtypeStruct(shape, F32) for shape in out_shape]
    else:
        shapes = jax.ShapeDtypeStruct(out_shape, F32)
    if outputs > 1:
        shapes = [shapes] * outputs
    return pl.pallas_call(
        functools.partial(kernel, **settings),
        out_shape=shapes,
        scratch_shapes=[pltpu.VMEM(shape, dtype) for shape, dtype in scratch],
        compiler_params=pltpu.CompilerParams(vmem_limit_bytes=room << 20),
        name=name,
        **extra,
    )


def moved(array, row_step, bit):
    rows = lax.axis_size("row")
    cols = lax.axis_size("col")
    pairs = [
        (r * cols + c, (r + row_step) % rows * cols + (c ^ bit)) for r in range(rows) for c in range(cols)
    ]
    return lax.ppermute(array, ("row", "col"), pairs)


def local(fine_coeffs, fine_slot, neighbours, filter_matrix, kernel_ops):
    breadth = filter_matrix.shape[0]
    terms = kernel_ops.shape[0]
    runs = lax.axis_size("row")
    cols = lax.axis_size("col")
    held, volume = fine_coeffs.shape
    par_row = neighbours.shape[0]
    count = held // 8
    capacity = 2 * (held // runs)
    places = runs * capacity
    width = breadth * breadth
    hi_count = width // LANES
    groups = 2
    per = terms // groups
    uppers = range(0, cols, 2)

    slot_row = fine_slot.reshape(1, held)
    routing = dict(run_size=8 * par_row)
    row = jnp.full((1,), lax.axis_index("row"), jnp.int32)
    scalar = pl.BlockSpec(memory_space=pltpu.SMEM)
    plain = pl.BlockSpec(memory_space=pltpu.VMEM)
    sent = vmem_call(
        pack_kernel,
        (capacity, volume + LANES),
        [((3 * held, volume), BF16)],
        "pack",
        in_specs=[scalar, plain, plain],
        room=ROOM,
        outputs=runs,
        **routing,
    )(row, slot_row, fine_coeffs)
    got = [sent[0]] + [moved(sent[k], k, 0) for k in range(1, runs)]

    first, second_high, second_low, merge_third, spread_third = pl.pallas_call(
        functools.partial(prepare_kernel, groups=groups),
        out_shape=[
            jax.ShapeDtypeStruct((terms * breadth, 3 * LANES), BF16),
            jax.ShapeDtypeStruct((terms, 3, breadth, LANES), BF16),
            jax.ShapeDtypeStruct((terms, 3, breadth, LANES), BF16),
            jax.ShapeDtypeStruct((groups, LANES, 6 * per * hi_count), BF16),
            jax.ShapeDtypeStruct((groups, 2, LANES, 3 * per * hi_count), BF16),
        ],
        scratch_shapes=[pltpu.VMEM((9 * terms * (breadth + PAD), LANES), F32)],
        compiler_params=pltpu.CompilerParams(vmem_limit_bytes=PREP << 20),
        name="prepare",
    )(jnp.transpose(kernel_ops, (1, 2, 0, 3)))
    weights = (first, second_high, second_low)

    col_index = lax.axis_index("col")
    mine = lax.dynamic_slice_in_dim(neighbours, col_index * count, count, 0)[:, ::2]
    within = mine % par_row
    relation = (within // count) ^ col_index
    spot = (relation % 2) * (len(uppers) * count) + relation // 2 * count + within % count
    where = jnp.where(mine >= 0, spot, -1)

    filtered, ids = vmem_call(
        filter_kernel,
        [(count, breadth, width), (places, LANES)],
        [
            ((2 * places, volume), BF16),
            ((2, breadth * 4, width), BF16),
            ((2, width, width), BF16),
            ((12 * breadth, width), BF16),
        ],
        "filter",
        count=count,
    )(filter_matrix, *got)

    parts = [moved(filtered, -1, u) for u in uppers]
    keep, send = spread_call(where, filtered, par_row, weights, spread_third, groups)
    parts, keep, send = lax.optimization_barrier((parts, keep, send))
    parts = parts + [moved(part, 0, 1) for part in parts]
    came = moved(send, 0, 1)

    terms_out = []
    for u in uppers:
        at = u // 2 * count
        terms_out.append(moved(keep[at : at + count] + came[at : at + count], 1, u))
    pieces = [merge_call(where, filtered, parts, weights, merge_third, groups)] + terms_out
    results = vmem_call(
        unfilter_kernel,
        (capacity, volume),
        [
            ((3 * count * breadth, width), BF16),
            ((2, width, width), BF16),
            ((64, volume), BF16),
        ],
        "unfilter",
        in_specs=[plain] * (2 + len(pieces)),
        outputs=runs,
        count=count,
        runs=runs,
    )(filter_matrix, ids, *pieces)
    backs = [results[0]] + [moved(results[runs - j], -j, 0) for j in range(1, runs)]
    return vmem_call(
        unpack_kernel,
        (held, volume),
        [((3 * places, volume), BF16)],
        "unpack",
        in_specs=[scalar, plain] + [plain] * runs,
        **routing,
    )(row, slot_row, *backs)


def solution(mesh):
    in_specs = (P(("row", "col"), None), P(("row", "col")), P("row", None), P(), P())
    out_specs = P(("row", "col"), None)
    return jax.shard_map(local, mesh=mesh, in_specs=in_specs, out_specs=out_specs, check_vma=False)
```

```python
import functools

import jax
import jax.numpy as jnp
import numpy as np
from jax import lax
from jax.experimental import pallas as pl
from jax.experimental.pallas import tpu as pltpu
from jax.sharding import PartitionSpec as P

F32, BF16 = jnp.float32, jnp.bfloat16
LANES = 128
PAD = 8
UNROLL = True
ROOM = 60
PREP = 14


def iota(shape, axis):
    return lax.broadcasted_iota(jnp.int32, shape, axis)


def split(x):
    high = x.astype(BF16)
    return high, (x - high.astype(F32)).astype(BF16)


def product(a, b):
    return jnp.dot(a, b, preferred_element_type=F32)


def exact_expand(x, hot):
    one = jnp.where(hot, 1.0, 0.0).astype(BF16)
    total = None
    for part in range(3):
        head = x.astype(BF16)
        piece = product(head, one)
        total = piece if total is None else total + piece
        x = x - head.astype(F32)
    return total


def prepare_kernel(packed, first, second_high, second_low, merge, spread, ops, *, groups):
    terms = second_high.shape[0]
    breadth = second_high.shape[2]
    lo_count = LANES // breadth
    hi_count = breadth // lo_count
    per = terms // groups
    stride = breadth + PAD
    for axis in range(3):
        for k in range(3):
            for high in range(hi_count):
                block = packed[axis, k, :, high * LANES : (high + 1) * LANES]
                for low in range(lo_count):
                    turned = block if low == 0 else pltpu.roll(block, LANES - low * breadth, 1)
                    at = (axis * 3 + k) * terms * stride + high * lo_count + low
                    ops[pl.ds(at, terms, stride=stride), :] = turned

    def factor(term, axis, k):
        at = ((axis * 3 + k) * terms + term) * stride
        return ops[at : at + breadth, :breadth]

    blank = jnp.zeros((breadth, LANES - 3 * breadth), F32)
    for term in range(terms):
        for k in range(3):
            value = factor(term, 0, k)
            high = value.astype(BF16).astype(F32)
            line = jnp.concatenate([high, high, value - high, blank], axis=1)
            first[term * breadth : (term + 1) * breadth, k * LANES : (k + 1) * LANES] = line.astype(BF16)
        turned = jnp.concatenate([factor(term, 2, k) for k in range(3)], axis=0).T
        for k in range(3):
            high, low = split(jnp.concatenate([turned[:, k * breadth : (k + 1) * breadth]] * lo_count, axis=1))
            second_high[term, k] = high
            second_low[term, k] = low
    for g in range(groups):
        for inner in range(lo_count):
            strip = [
                jnp.concatenate(
                    [factor(g * per + t, 1, k)[:, inner * hi_count : (inner + 1) * hi_count] for t in range(per)], axis=1
                )
                for k in range(3)
            ]
            value = jnp.concatenate([strip[1], strip[0]], axis=1)
            high = value.astype(BF16).astype(F32)
            line = jnp.concatenate([high, high, value - high], axis=1)
            merge[g, inner * breadth : (inner + 1) * breadth] = line.astype(BF16)
            for s, k in enumerate((1, 2)):
                high = strip[k].astype(BF16).astype(F32)
                line = jnp.concatenate([high, high, strip[k] - high], axis=1)
                spread[g, s, inner * breadth : (inner + 1) * breadth] = line.astype(BF16)


def fill(xbuf, slot, block):
    breadth = block.shape[0]
    high, low = split(block)
    base = slot * LANES
    xbuf[base : base + breadth] = high
    xbuf[base + breadth : base + 2 * breadth] = low
    xbuf[base + 2 * breadth : base + 3 * breadth] = high


def place(ubuf, g, n, result):
    rows = result.shape[0]
    for h in range(result.shape[1] // LANES):
        ubuf[g, n, h, :rows] = result[:, h * LANES : (h + 1) * LANES]


def second_stage(ubuf, lbuf, tbuf, second_high, second_low, group, per, breadth, offsets, sides, recipes, emit):
    volumes, count, hi_count, stride = ubuf.shape[:4]
    lo_count = LANES // breadth
    wide = 2 * LANES
    flat = ubuf.reshape(volumes * count * hi_count * stride, LANES)
    block_mask = iota((LANES, LANES), 0) // breadth == iota((LANES, LANES), 1) // breadth
    zero_block = jnp.zeros((LANES, LANES), BF16)

    def pair_body(pair, carry):
        for spot, k in enumerate(offsets):
            row = spot * sides[0] * wide
            lane = spot * sides[1] * wide
            for half in range(2):
                term = group * per + pair * 2 + half
                high = jnp.concatenate([second_high[term, k]] * lo_count, axis=0)
                low = jnp.concatenate([second_low[term, k]] * lo_count, axis=0)
                high = jnp.where(block_mask, high, zero_block)
                low = jnp.where(block_mask, low, zero_block)
                tbuf[half, row : row + LANES, lane : lane + LANES] = high
                tbuf[half, row + LANES : row + wide, lane : lane + LANES] = high
                tbuf[half, row : row + LANES, lane + LANES : lane + wide] = low
        for half in range(2):
            term = pair * 2 + half
            for n in range(count):
                for g in range(volumes):
                    base = (g * count + n) * hi_count * stride + term * breadth
                    for a in range(0, breadth, 2):
                        pieces = [flat[pl.ds(base + a + d, hi_count, stride=stride), :] for d in range(2)]
                        high, low = split(jnp.concatenate(pieces, axis=0))
                        at = (n * breadth + a) * hi_count
                        lane = g * wide
                        lbuf[half, at : at + 2 * hi_count, lane : lane + LANES] = high
                        lbuf[half, at : at + 2 * hi_count, lane + LANES : lane + wide] = low
        results = []
        for half in range(2):
            line = []
            for (start, size), (row, rows), (lane, lanes) in recipes:
                full = product(
                    lbuf[half, :, start * wide : (start + size) * wide],
                    tbuf[half, row * wide : (row + rows) * wide, lane * wide : (lane + lanes) * wide],
                )
                for out in range(lanes):
                    line.append(full[:, out * wide : out * wide + LANES] + full[:, out * wide + LANES : (out + 1) * wide])
            results.append(line)
        for q in range(len(results[0])):
            for at in range(count * breadth):
                both = jnp.concatenate(
                    [results[half][q][at * hi_count : (at + 1) * hi_count] for half in range(2)], axis=0
                )
                high, low = split(both)
                emit(q, pair, at // 2, (at % 2) * LANES, high, low)
        return carry

    lax.fori_loop(0, per // 2, pair_body, 0, unroll=UNROLL)


def pick_diagonal(wide, breadth):
    lane_block = iota((breadth, wide.shape[1]), 1) % LANES // breadth
    total = wide[:breadth]
    for low in range(1, LANES // breadth):
        total = jnp.where(lane_block == low, wide[low * breadth : (low + 1) * breadth], total)
    return total


def turn_block(obuf, base, breadth, store):
    stride = breadth + PAD
    lo_count = LANES // breadth
    lane_of = iota((8, LANES), 1) // breadth
    for a in range(0, breadth, 8):
        for high in range(breadth // lo_count):
            level = [
                obuf[pl.ds(base + a * stride + high * lo_count + low, 8, stride=stride), :] for low in range(lo_count)
            ]
            step = 1
            while step < lo_count:
                own_side = (lane_of // step) % 2 == 0
                level = [
                    jnp.where(own_side, p, q) + pltpu.roll(jnp.where(own_side, q, p), step * breadth, 1)
                    for p, q in zip(level[::2], level[1::2])
                ]
                step *= 2
            store(a, high * LANES, level[0])


def merge_kernel(where, own, *refs, parts):
    sources = refs[:parts]
    first, second_high, second_low, third, out = refs[parts : parts + 5]
    vols, xbuf, ubuf, lbuf, tbuf, rbuf, obuf, sems = refs[parts + 5 :]
    count, breadth, width = own.shape
    rows = first.shape[0] // third.shape[0]
    per = rows // breadth
    kgroup = per * breadth * breadth // LANES

    def copies(action):
        for n in range(count):
            for axis in range(3):
                slot = n * 3 + axis
                at = where[n, axis]
                start = 0
                for source in sources:
                    size = source.shape[0]

                    @pl.when((at >= start) & (at < start + size))
                    def _(source=source, start=start, slot=slot, at=at):
                        action(pltpu.make_async_copy(source.at[at - start], vols.at[slot], sems.at[slot]))

                    start += size

    copies(lambda c: c.start())
    for n in range(count):
        for axis in range(3):

            @pl.when(where[n, axis] < 0)
            def _(slot=n * 3 + axis):
                vols[slot] = jnp.zeros((breadth, width), F32)

    tbuf[...] = jnp.zeros(tbuf.shape, BF16)
    xbuf[...] = jnp.zeros(xbuf.shape, BF16)
    copies(lambda c: c.wait())
    stride = breadth + PAD

    def group_body(group, carry):
        top = pl.multiple_of(group * rows, 8)
        for n in range(count):
            fill(xbuf, 0, vols[n * 3])
            fill(xbuf, 1, own[n])
            place(ubuf, 0, n, product(first[pl.ds(top, rows), : 2 * LANES], xbuf[...]))
            for g, axis in ((1, 2), (2, 1)):
                fill(xbuf, 0, vols[n * 3 + axis])
                place(ubuf, g, n, product(first[pl.ds(top, rows), LANES : 2 * LANES], xbuf[:LANES]))

        def emit(q, pair, tile, lane, high, low):
            step = high.shape[0]
            row = pl.multiple_of(q * kgroup + pair * step, step)
            rbuf[tile, pl.ds(row, step), lane : lane + LANES] = high
            rbuf[tile, pl.ds(row + 2 * kgroup, step), lane : lane + LANES] = low
            rbuf[tile, pl.ds(row + 4 * kgroup, step), lane : lane + LANES] = high

        recipes = (((0, 2), (0, 2), (0, 1)), ((2, 1), (0, 1), (0, 1)))
        second_stage(
            ubuf, lbuf, tbuf, second_high, second_low, group, per, breadth, (1, 0), (1, 0), recipes, emit
        )
        for tile in range(count * breadth // 2):
            total = pick_diagonal(product(third[group], rbuf[tile]), breadth)
            for d in range(2):
                row = (tile * 2 + d) * stride
                old = jnp.where(group == 0, 0.0, obuf[row : row + breadth])
                obuf[row : row + breadth] = old + total[:, d * LANES : (d + 1) * LANES]
        return carry

    lax.fori_loop(0, third.shape[0], group_body, 0)
    for n in range(count):

        def store(a, lane, value, n=n):
            out[n, a : a + 8, lane : lane + LANES] = value

        turn_block(obuf, n * breadth * stride, breadth, store)


def spread_kernel(where, own, *refs):
    first, second_high, second_low, third, keep, send = refs[:6]
    xbuf, ubuf, lbuf, tbuf, rbuf, obuf, block = refs[6:]
    count, breadth, width = own.shape
    rows = first.shape[0] // third.shape[0]
    per = rows // breadth
    kgroup = per * breadth * breadth // LANES
    half_slots = keep.shape[0]
    keep[...] = jnp.zeros(keep.shape, F32)
    send[...] = jnp.zeros(send.shape, F32)
    tbuf[...] = jnp.zeros(tbuf.shape, BF16)
    xbuf[...] = jnp.zeros(xbuf.shape, BF16)
    stride = breadth + PAD

    def group_body(group, carry):
        top = pl.multiple_of(group * rows, 8)
        for n in range(count):
            fill(xbuf, 0, own[n])
            for g in range(2):
                place(ubuf, g, n, product(first[pl.ds(top, rows), (1 + g) * LANES : (2 + g) * LANES], xbuf[...]))

        def emit(q, pair, tile, lane, high, low):
            step = high.shape[0]
            row = pl.multiple_of(q * 3 * kgroup + pair * step, step)
            rbuf[tile, pl.ds(row, step), lane : lane + LANES] = high
            rbuf[tile, pl.ds(row + kgroup, step), lane : lane + LANES] = low
            rbuf[tile, pl.ds(row + 2 * kgroup, step), lane : lane + LANES] = high

        recipes = (((1, 1), (0, 1), (0, 1)), ((0, 1), (0, 1), (0, 2)))
        second_stage(
            ubuf, lbuf, tbuf, second_high, second_low, group, per, breadth, (1, 2), (0, 1), recipes, emit
        )
        for tile in range(count * breadth // 2):
            for q in range(3):
                wide = product(third[group, 1 if q == 1 else 0], rbuf[tile, q * 3 * kgroup : (q + 1) * 3 * kgroup])
                total = pick_diagonal(wide, breadth)
                for d in range(2):
                    row = (tile * 2 + d) * stride
                    old = jnp.where(group == 0, 0.0, obuf[q, row : row + breadth])
                    obuf[q, row : row + breadth] = old + total[:, d * LANES : (d + 1) * LANES]
        return carry

    lax.fori_loop(0, third.shape[0], group_body, 0)
    for n in range(count):
        for q in range(3):

            def store(a, lane, value):
                block[a : a + 8, lane : lane + LANES] = value

            turn_block(obuf.at[q], n * breadth * stride, breadth, store)
            slot = where[n, q]

            @pl.when((slot >= 0) & (slot < half_slots))
            def _(slot=slot):
                keep[slot] = keep[slot] + block[...]

            @pl.when(slot >= half_slots)
            def _(slot=slot):
                send[slot - half_slots] = send[slot - half_slots] + block[...]


def stage_scratch(volumes, spots, recipes, count, breadth, per):
    hi_count = breadth * breadth // LANES
    return [
        pltpu.VMEM((volumes, count, hi_count, per * breadth + PAD, LANES), F32),
        pltpu.VMEM((2, count * breadth * hi_count, volumes * 2 * LANES), BF16),
        pltpu.VMEM((2, spots[0] * 2 * LANES, spots[1] * 2 * LANES), BF16),
        pltpu.VMEM((count * breadth // 2, recipes * 3 * per * hi_count, 2 * LANES), BF16),
    ]


def cost(count, breadth, per, units):
    return pl.CostEstimate(flops=units * per * 2 * count * breadth**4 * 200, transcendentals=0, bytes_accessed=1 << 22)


def stage_call(kernel, name, where, own, extra, weights, third, groups, out_shapes, scratch, units):
    first, second_high, second_low = weights
    breadth = own.shape[1]
    terms = second_high.shape[0]
    per = terms // groups
    return pl.pallas_call(
        kernel,
        out_shape=out_shapes,
        in_specs=[pl.BlockSpec(memory_space=pltpu.SMEM), pl.BlockSpec(memory_space=pltpu.VMEM)]
        + [pl.BlockSpec(memory_space=pl.ANY)] * len(extra)
        + [pl.BlockSpec(memory_space=pltpu.VMEM)] * 4,
        out_specs=[pl.BlockSpec(memory_space=pltpu.VMEM)] * len(out_shapes),
        scratch_shapes=scratch,
        compiler_params=pltpu.CompilerParams(vmem_limit_bytes=36 << 20),
        cost_estimate=cost(own.shape[0], breadth, terms, units),
        name=name,
    )(where, own, *extra, first, second_high, second_low, third)


def merge_call(where, own, parts, weights, third, groups):
    count, breadth, width = own.shape
    per = weights[1].shape[0] // groups
    scratch = stage_scratch(3, (2, 1), 2, count, breadth, per)
    scratch = (
        [pltpu.VMEM((count * 3, breadth, width), F32), pltpu.VMEM((2 * LANES, width), BF16)]
        + scratch
        + [pltpu.VMEM((count * breadth * (breadth + PAD), LANES), F32), pltpu.SemaphoreType.DMA((count * 3,))]
    )
    return stage_call(
        functools.partial(merge_kernel, parts=len(parts)),
        "merge",
        where,
        own,
        list(parts),
        weights,
        third,
        groups,
        [jax.ShapeDtypeStruct(own.shape, F32)],
        scratch,
        9,
    )[0]


def spread_call(where, own, slots, weights, third, groups):
    count, breadth, width = own.shape
    per = weights[1].shape[0] // groups
    scratch = stage_scratch(2, (1, 2), 3, count, breadth, per)
    scratch = (
        [pltpu.VMEM((LANES, width), BF16)]
        + scratch
        + [pltpu.VMEM((3, count * breadth * (breadth + PAD), LANES), F32), pltpu.VMEM((breadth, width), F32)]
    )
    shape = jax.ShapeDtypeStruct((slots // 2, breadth, width), F32)
    return stage_call(
        spread_kernel,
        "spread",
        where,
        own,
        [],
        weights,
        third,
        groups,
        [shape, shape],
        scratch,
        8,
    )


def to_row(column):
    size = column.shape[0]
    diagonal = iota((size, size), 0) == iota((size, size), 1)
    return jnp.sum(jnp.where(diagonal, column, 0.0), axis=0, keepdims=True)


def to_column(row):
    size = row.shape[1]
    diagonal = iota((size, size), 0) == iota((size, size), 1)
    return jnp.sum(jnp.where(diagonal, row, 0.0), axis=1, keepdims=True)


def place_row(slot_row, row, runs, run_size, capacity):
    held = slot_row.shape[1]
    run_row = jnp.zeros(slot_row.shape, F32)
    for r in range(1, runs):
        run_row = run_row + jnp.where(slot_row >= r * run_size, 1.0, 0.0)
    same = to_column(run_row) == run_row
    earlier = iota((held, held), 0) < iota((held, held), 1)
    before = jnp.sum(jnp.where(same & earlier, 1.0, 0.0), axis=0, keepdims=True)
    far_row = run_row - row.astype(F32)
    far_row = jnp.where(far_row < 0.0, far_row + runs, far_row)
    return far_row * capacity + before


def pack_kernel(row, slot_row, fine, *refs, run_size):
    outs, stack = refs[:-1], refs[-1]
    held, volume = fine.shape
    runs = len(outs)
    capacity = outs[0].shape[0]
    places = runs * capacity
    slots = slot_row[...]
    place = place_row(slots, row[0], runs, run_size, capacity)
    hit = iota((places, held), 0).astype(F32) == place
    ids = jnp.sum(jnp.where(hit, slots.astype(F32) + 1.0, 0.0), axis=1, keepdims=True)
    ids = jnp.broadcast_to(ids, (places, LANES))
    one = jnp.where(hit, 1.0, 0.0).astype(BF16)
    rest = fine[...]
    for part in range(3):
        head = rest.astype(BF16)
        stack[part * held : (part + 1) * held] = head
        rest = rest - head.astype(F32)
    packed = product(jnp.concatenate([one] * 3, axis=1), stack[...])
    for k in range(runs):
        outs[k][:, :volume] = packed[k * capacity : (k + 1) * capacity]
        outs[k][:, volume:] = ids[k * capacity : (k + 1) * capacity]


def unpack_kernel(row, slot_row, *refs, run_size):
    backs = refs[:-2]
    out, stack = refs[-2:]
    held, volume = out.shape
    runs = len(backs)
    capacity = backs[0].shape[0]
    places = runs * capacity
    place = to_column(place_row(slot_row[...], row[0], runs, run_size, capacity))
    hit = iota((held, places), 1).astype(F32) == place
    one = jnp.where(hit, 1.0, 0.0).astype(BF16)
    rest = jnp.concatenate([back[...] for back in backs], axis=0)
    for part in range(3):
        head = rest.astype(BF16)
        stack[part * places : (part + 1) * places] = head
        rest = rest - head.astype(F32)
    out[...] = product(jnp.concatenate([one] * 3, axis=1), stack[...])


def child_code(ids, held):
    at = ids - 1.0
    return jnp.where(at < 0.0, -1.0, at - held * jnp.floor(at / held))


def row_code(index, count):
    inner = index & 7
    code = (inner >> 1) * 8 + (inner & 1) * 4 + (index >> 3)
    return jnp.where(inner < 2 * count, code.astype(F32), -2.0)


def child_rows(filter_matrix, count):
    breadth = filter_matrix.shape[0]
    half = breadth // 2
    lane = iota((breadth, half * 8), 1)
    inner = lane & 7
    hot = iota((breadth, half * 8), 0) == (inner & 1) * half + (lane >> 3)
    spread = exact_expand(filter_matrix, hot)
    return jnp.concatenate([jnp.where(inner >> 1 == n, spread, 0.0) for n in range(count)], axis=0)


def triple_lanes(x):
    high, low = split(x)
    return jnp.concatenate([high, high, low], axis=1)


def filter_kernel(filter_ref, *refs, count):
    got = refs[:-6]
    out, ids, stack, lines, cross, weave = refs[-6:]
    runs = len(got)
    capacity, volume = got[0].shape
    volume = volume - LANES
    places = runs * capacity
    breadth = filter_ref.shape[0]
    half = breadth // 2
    width = out.shape[2]
    face = width // 4
    span = volume // face
    lo_count = LANES // breadth
    hi_count = breadth // lo_count
    matrix = filter_ref[...]
    turned = matrix.T
    lane = iota((breadth, width), 1)
    outer = lane // breadth
    across_z = exact_expand(turned, iota((breadth, width), 0) == lane % breadth)
    across_y = exact_expand(turned, iota((breadth, width), 0) == (outer % lo_count) * hi_count + outer // lo_count)
    for g in range(4):
        zs = across_z[(g & 1) * half : (g & 1) * half + half]
        for j in range(half):
            row = (g >> 1) * half + j
            high, low = split(zs * across_y[row : row + 1])
            at = (g * half + j) * half
            cross[0, at : at + half] = high
            cross[1, at : at + half] = low
    joined = jnp.concatenate([piece[...] for piece in got], axis=0)
    ids[...] = jnp.concatenate([got[(runs - k) % runs][:, volume:] for k in range(runs)], axis=0)
    code = to_row(child_code(joined[:, volume : volume + 1], 8 * count))
    hit = row_code(iota((32, places), 0), count) == code
    one = jnp.where(hit, 1.0, 0.0).astype(BF16)
    high, low = split(joined[:, :volume])
    stack[:places] = high
    stack[places:] = low
    boxes = product(jnp.concatenate([one, one], axis=1), stack[...])
    for g in range(4):
        for i in range(0, span, 2):
            both = jnp.concatenate(
                [boxes[g * 8 : g * 8 + 8, (i + d) * face : (i + d + 1) * face] for d in range(2)], axis=0
            )
            high, low = split(both)
            lines[0, i * 8 : i * 8 + 16, g * face : (g + 1) * face] = high
            lines[1, i * 8 : i * 8 + 16, g * face : (g + 1) * face] = low
    total = product(lines[0], cross[0]) + product(lines[1], cross[0]) + product(lines[0], cross[1])
    high, low = split(total)
    size = total.shape[0]
    weave[:size] = high
    weave[size : 2 * size] = low
    weave[2 * size :] = high
    result = product(triple_lanes(child_rows(matrix, count)), weave[...])
    for n in range(count):
        out[n] = result[n * breadth : (n + 1) * breadth]


def unfilter_kernel(filter_ref, ids, *refs, count, runs):
    outs = refs[-3 - runs : -3]
    applied = refs[: -3 - runs]
    weave, cross, stack = refs[-3:]
    capacity, volume = outs[0].shape
    places = runs * capacity
    breadth = filter_ref.shape[0]
    half = breadth // 2
    width = applied[0].shape[2]
    face = width // 4
    size = count * breadth
    matrix = filter_ref[...]
    lane = iota((breadth, width), 1)
    octant = lane // face
    across_c = exact_expand(matrix, iota((breadth, width), 0) == octant % 2 * half + lane % half)
    across_b = exact_expand(matrix, iota((breadth, width), 0) == octant // 2 * half + lane // half % half)
    for b in range(breadth):
        high, low = split(across_c * across_b[b : b + 1])
        cross[0, b * breadth : (b + 1) * breadth] = high
        cross[1, b * breadth : (b + 1) * breadth] = low
    for n in range(count):
        total = applied[0][n]
        for piece in applied[1:]:
            total = total + piece[n]
        high, low = split(total)
        at = n * breadth
        weave[at : at + breadth] = high
        weave[size + at : size + at + breadth] = low
        weave[2 * size + at : 2 * size + at + breadth] = high
    lines = product(triple_lanes(child_rows(matrix, count).T), weave[...])
    high, low = split(lines)
    total = product(high, cross[0]) + product(low, cross[0]) + product(high, cross[1])
    for g in range(0, 4, 2):
        for i in range(total.shape[0] // 8):
            both = jnp.concatenate(
                [total[i * 8 : i * 8 + 8, (g + d) * face : (g + d + 1) * face] for d in range(2)], axis=0
            )
            high, low = split(both)
            stack[g * 8 : g * 8 + 16, i * face : (i + 1) * face] = high
            stack[32 + g * 8 : 32 + g * 8 + 16, i * face : (i + 1) * face] = low
    code = child_code(ids[:, :1], 8 * count)
    hit = row_code(iota((places, 32), 1), count) == code
    one = jnp.where(hit, 1.0, 0.0).astype(BF16)
    packed = product(jnp.concatenate([one, one], axis=1), stack[...])
    for k in range(runs):
        outs[k][...] = packed[k * capacity : (k + 1) * capacity]


def add_kernel(keep, came, *outs):
    count = outs[0].shape[0]
    for i, out in enumerate(outs):
        out[...] = keep[i * count : (i + 1) * count] + came[i * count : (i + 1) * count]


def vmem_call(kernel, out_shape, scratch, name, in_specs=None, room=14, outputs=1, **settings):
    extra = {} if in_specs is None else dict(in_specs=in_specs)
    if isinstance(out_shape, list):
        shapes = [jax.ShapeDtypeStruct(shape, F32) for shape in out_shape]
    else:
        shapes = jax.ShapeDtypeStruct(out_shape, F32)
    if outputs > 1:
        shapes = [shapes] * outputs
    return pl.pallas_call(
        functools.partial(kernel, **settings),
        out_shape=shapes,
        scratch_shapes=[pltpu.VMEM(shape, dtype) for shape, dtype in scratch],
        compiler_params=pltpu.CompilerParams(vmem_limit_bytes=room << 20),
        name=name,
        **extra,
    )


def moved(array, row_step, bit):
    rows = lax.axis_size("row")
    cols = lax.axis_size("col")
    pairs = [
        (r * cols + c, (r + row_step) % rows * cols + (c ^ bit)) for r in range(rows) for c in range(cols)
    ]
    return lax.ppermute(array, ("row", "col"), pairs)


def local(fine_coeffs, fine_slot, neighbours, filter_matrix, kernel_ops):
    breadth = filter_matrix.shape[0]
    terms = kernel_ops.shape[0]
    runs = lax.axis_size("row")
    cols = lax.axis_size("col")
    held, volume = fine_coeffs.shape
    par_row = neighbours.shape[0]
    count = held // 8
    capacity = 2 * (held // runs)
    places = runs * capacity
    width = breadth * breadth
    hi_count = width // LANES
    groups = 2
    per = terms // groups
    uppers = range(0, cols, 2)

    slot_row = fine_slot.reshape(1, held)
    routing = dict(run_size=8 * par_row)
    row = jnp.full((1,), lax.axis_index("row"), jnp.int32)
    scalar = pl.BlockSpec(memory_space=pltpu.SMEM)
    plain = pl.BlockSpec(memory_space=pltpu.VMEM)
    sent = vmem_call(
        pack_kernel,
        (capacity, volume + LANES),
        [((3 * held, volume), BF16)],
        "pack",
        in_specs=[scalar, plain, plain],
        room=ROOM,
        outputs=runs,
        **routing,
    )(row, slot_row, fine_coeffs)
    got = [sent[0]] + [moved(sent[k], k, 0) for k in range(1, runs)]

    first, second_high, second_low, merge_third, spread_third = pl.pallas_call(
        functools.partial(prepare_kernel, groups=groups),
        out_shape=[
            jax.ShapeDtypeStruct((terms * breadth, 3 * LANES), BF16),
            jax.ShapeDtypeStruct((terms, 3, breadth, LANES), BF16),
            jax.ShapeDtypeStruct((terms, 3, breadth, LANES), BF16),
            jax.ShapeDtypeStruct((groups, LANES, 6 * per * hi_count), BF16),
            jax.ShapeDtypeStruct((groups, 2, LANES, 3 * per * hi_count), BF16),
        ],
        scratch_shapes=[pltpu.VMEM((9 * terms * (breadth + PAD), LANES), F32)],
        compiler_params=pltpu.CompilerParams(vmem_limit_bytes=PREP << 20),
        name="prepare",
    )(jnp.transpose(kernel_ops, (1, 2, 0, 3)))
    weights = (first, second_high, second_low)

    col_index = lax.axis_index("col")
    mine = lax.dynamic_slice_in_dim(neighbours, col_index * count, count, 0)[:, ::2]
    within = mine % par_row
    relation = (within // count) ^ col_index
    spot = (relation % 2) * (len(uppers) * count) + relation // 2 * count + within % count
    where = jnp.where(mine >= 0, spot, -1)

    filtered, ids = vmem_call(
        filter_kernel,
        [(count, breadth, width), (places, LANES)],
        [
            ((2 * places, volume), BF16),
            ((2, breadth * 4, width), BF16),
            ((2, width, width), BF16),
            ((12 * breadth, width), BF16),
        ],
        "filter",
        count=count,
    )(filter_matrix, *got)

    parts = [moved(filtered, -1, u) for u in reversed(uppers)][::-1]
    keep, send = spread_call(where, filtered, par_row, weights, spread_third, groups)
    parts, keep, send = lax.optimization_barrier((parts, keep, send))
    parts = parts + [moved(part, 0, 1) for part in parts]
    came = moved(send, 0, 1)

    sums = vmem_call(
        add_kernel, [(count, breadth, width)] * len(uppers), [], "add", in_specs=[plain] * 2, room=8
    )(keep, came)
    terms_out = [moved(sums[u // 2], 1, u) for u in reversed(uppers)]
    pieces = [merge_call(where, filtered, parts, weights, merge_third, groups)] + terms_out
    results = vmem_call(
        unfilter_kernel,
        (capacity, volume),
        [
            ((3 * count * breadth, width), BF16),
            ((2, width, width), BF16),
            ((64, volume), BF16),
        ],
        "unfilter",
        in_specs=[plain] * (2 + len(pieces)),
        outputs=runs,
        count=count,
        runs=runs,
    )(filter_matrix, ids, *pieces)
    backs = [results[0]] + [moved(results[runs - j], -j, 0) for j in range(1, runs)]
    return vmem_call(
        unpack_kernel,
        (held, volume),
        [((3 * places, volume), BF16)],
        "unpack",
        in_specs=[scalar, plain] + [plain] * runs,
        **routing,
    )(row, slot_row, *backs)


def solution(mesh):
    in_specs = (P(("row", "col"), None), P(("row", "col")), P("row", None), P(), P())
    out_specs = P(("row", "col"), None)
    return jax.shard_map(local, mesh=mesh, in_specs=in_specs, out_specs=out_specs, check_vma=False)
```

```python
import functools

import jax
import jax.numpy as jnp
import numpy as np
from jax import lax
from jax.experimental import pallas as pl
from jax.experimental.pallas import tpu as pltpu
from jax.sharding import PartitionSpec as P

F32, BF16 = jnp.float32, jnp.bfloat16
LANES = 128
PAD = 8
UNROLL = True
ROOM = 60
PREP = 14


def iota(shape, axis):
    return lax.broadcasted_iota(jnp.int32, shape, axis)


def split(x):
    high = x.astype(BF16)
    return high, (x - high.astype(F32)).astype(BF16)


def product(a, b):
    return jnp.dot(a, b, preferred_element_type=F32)


def exact_expand(x, hot):
    one = jnp.where(hot, 1.0, 0.0).astype(BF16)
    total = None
    for part in range(3):
        head = x.astype(BF16)
        piece = product(head, one)
        total = piece if total is None else total + piece
        x = x - head.astype(F32)
    return total


def prepare_kernel(packed, first, second_high, second_low, merge, spread, ops, *, groups):
    terms = second_high.shape[0]
    breadth = second_high.shape[2]
    lo_count = LANES // breadth
    hi_count = breadth // lo_count
    per = terms // groups
    stride = breadth + PAD
    for axis in range(3):
        for k in range(3):
            for high in range(hi_count):
                block = packed[axis, k, :, high * LANES : (high + 1) * LANES]
                for low in range(lo_count):
                    turned = block if low == 0 else pltpu.roll(block, LANES - low * breadth, 1)
                    at = (axis * 3 + k) * terms * stride + high * lo_count + low
                    ops[pl.ds(at, terms, stride=stride), :] = turned

    def factor(term, axis, k):
        at = ((axis * 3 + k) * terms + term) * stride
        return ops[at : at + breadth, :breadth]

    blank = jnp.zeros((breadth, LANES - 3 * breadth), F32)
    for term in range(terms):
        for k in range(3):
            value = factor(term, 0, k)
            high = value.astype(BF16).astype(F32)
            line = jnp.concatenate([high, high, value - high, blank], axis=1)
            first[term * breadth : (term + 1) * breadth, k * LANES : (k + 1) * LANES] = line.astype(BF16)
        turned = jnp.concatenate([factor(term, 2, k) for k in range(3)], axis=0).T
        for k in range(3):
            high, low = split(jnp.concatenate([turned[:, k * breadth : (k + 1) * breadth]] * lo_count, axis=1))
            second_high[term, k] = high
            second_low[term, k] = low
    for g in range(groups):
        for inner in range(lo_count):
            strip = [
                jnp.concatenate(
                    [factor(g * per + t, 1, k)[:, inner * hi_count : (inner + 1) * hi_count] for t in range(per)], axis=1
                )
                for k in range(3)
            ]
            value = jnp.concatenate([strip[1], strip[0]], axis=1)
            high = value.astype(BF16).astype(F32)
            line = jnp.concatenate([high, high, value - high], axis=1)
            merge[g, inner * breadth : (inner + 1) * breadth] = line.astype(BF16)
            for s, k in enumerate((1, 2)):
                high = strip[k].astype(BF16).astype(F32)
                line = jnp.concatenate([high, high, strip[k] - high], axis=1)
                spread[g, s, inner * breadth : (inner + 1) * breadth] = line.astype(BF16)


def fill(xbuf, slot, block):
    breadth = block.shape[0]
    high, low = split(block)
    base = slot * LANES
    xbuf[base : base + breadth] = high
    xbuf[base + breadth : base + 2 * breadth] = low
    xbuf[base + 2 * breadth : base + 3 * breadth] = high


def place(ubuf, g, n, result):
    rows = result.shape[0]
    for h in range(result.shape[1] // LANES):
        ubuf[g, n, h, :rows] = result[:, h * LANES : (h + 1) * LANES]


def second_stage(ubuf, lbuf, tbuf, second_high, second_low, group, per, breadth, offsets, sides, recipes, emit):
    volumes, count, hi_count, stride = ubuf.shape[:4]
    lo_count = LANES // breadth
    wide = 2 * LANES
    flat = ubuf.reshape(volumes * count * hi_count * stride, LANES)
    block_mask = iota((LANES, LANES), 0) // breadth == iota((LANES, LANES), 1) // breadth
    zero_block = jnp.zeros((LANES, LANES), BF16)

    def pair_body(pair, carry):
        for spot, k in enumerate(offsets):
            row = spot * sides[0] * wide
            lane = spot * sides[1] * wide
            for half in range(2):
                term = group * per + pair * 2 + half
                high = jnp.concatenate([second_high[term, k]] * lo_count, axis=0)
                low = jnp.concatenate([second_low[term, k]] * lo_count, axis=0)
                high = jnp.where(block_mask, high, zero_block)
                low = jnp.where(block_mask, low, zero_block)
                tbuf[half, row : row + LANES, lane : lane + LANES] = high
                tbuf[half, row + LANES : row + wide, lane : lane + LANES] = high
                tbuf[half, row : row + LANES, lane + LANES : lane + wide] = low
        for half in range(2):
            term = pair * 2 + half
            for n in range(count):
                for g in range(volumes):
                    base = (g * count + n) * hi_count * stride + term * breadth
                    for a in range(0, breadth, 2):
                        pieces = [flat[pl.ds(base + a + d, hi_count, stride=stride), :] for d in range(2)]
                        high, low = split(jnp.concatenate(pieces, axis=0))
                        at = (n * breadth + a) * hi_count
                        lane = g * wide
                        lbuf[half, at : at + 2 * hi_count, lane : lane + LANES] = high
                        lbuf[half, at : at + 2 * hi_count, lane + LANES : lane + wide] = low
        results = []
        for half in range(2):
            line = []
            for (start, size), (row, rows), (lane, lanes) in recipes:
                full = product(
                    lbuf[half, :, start * wide : (start + size) * wide],
                    tbuf[half, row * wide : (row + rows) * wide, lane * wide : (lane + lanes) * wide],
                )
                for out in range(lanes):
                    line.append(full[:, out * wide : out * wide + LANES] + full[:, out * wide + LANES : (out + 1) * wide])
            results.append(line)
        for q in range(len(results[0])):
            for at in range(count * breadth):
                both = jnp.concatenate(
                    [results[half][q][at * hi_count : (at + 1) * hi_count] for half in range(2)], axis=0
                )
                high, low = split(both)
                emit(q, pair, at // 2, (at % 2) * LANES, high, low)
        return carry

    lax.fori_loop(0, per // 2, pair_body, 0, unroll=UNROLL)


def pick_diagonal(wide, breadth):
    lane_block = iota((breadth, wide.shape[1]), 1) % LANES // breadth
    total = wide[:breadth]
    for low in range(1, LANES // breadth):
        total = jnp.where(lane_block == low, wide[low * breadth : (low + 1) * breadth], total)
    return total


def turn_block(obuf, base, breadth, store):
    stride = breadth + PAD
    lo_count = LANES // breadth
    lane_of = iota((8, LANES), 1) // breadth
    for a in range(0, breadth, 8):
        for high in range(breadth // lo_count):
            level = [
                obuf[pl.ds(base + a * stride + high * lo_count + low, 8, stride=stride), :] for low in range(lo_count)
            ]
            step = 1
            while step < lo_count:
                own_side = (lane_of // step) % 2 == 0
                level = [
                    jnp.where(own_side, p, q) + pltpu.roll(jnp.where(own_side, q, p), step * breadth, 1)
                    for p, q in zip(level[::2], level[1::2])
                ]
                step *= 2
            store(a, high * LANES, level[0])


def merge_kernel(where, own, *refs, parts):
    sources = refs[:parts]
    first, second_high, second_low, third, out = refs[parts : parts + 5]
    vols, xbuf, ubuf, lbuf, tbuf, rbuf, obuf, sems = refs[parts + 5 :]
    count, breadth, width = own.shape
    rows = first.shape[0] // third.shape[0]
    per = rows // breadth
    kgroup = per * breadth * breadth // LANES

    def copies(action):
        for n in range(count):
            for axis in range(3):
                slot = n * 3 + axis
                at = where[n, axis]
                start = 0
                for source in sources:
                    size = source.shape[0]

                    @pl.when((at >= start) & (at < start + size))
                    def _(source=source, start=start, slot=slot, at=at):
                        action(pltpu.make_async_copy(source.at[at - start], vols.at[slot], sems.at[slot]))

                    start += size

    copies(lambda c: c.start())
    for n in range(count):
        for axis in range(3):

            @pl.when(where[n, axis] < 0)
            def _(slot=n * 3 + axis):
                vols[slot] = jnp.zeros((breadth, width), F32)

    tbuf[...] = jnp.zeros(tbuf.shape, BF16)
    xbuf[...] = jnp.zeros(xbuf.shape, BF16)
    copies(lambda c: c.wait())
    stride = breadth + PAD

    def group_body(group, carry):
        top = pl.multiple_of(group * rows, 8)
        for n in range(count):
            fill(xbuf, 0, vols[n * 3])
            fill(xbuf, 1, own[n])
            place(ubuf, 0, n, product(first[pl.ds(top, rows), : 2 * LANES], xbuf[...]))
            for g, axis in ((1, 2), (2, 1)):
                fill(xbuf, 0, vols[n * 3 + axis])
                place(ubuf, g, n, product(first[pl.ds(top, rows), LANES : 2 * LANES], xbuf[:LANES]))

        def emit(q, pair, tile, lane, high, low):
            step = high.shape[0]
            row = pl.multiple_of(q * kgroup + pair * step, step)
            rbuf[tile, pl.ds(row, step), lane : lane + LANES] = high
            rbuf[tile, pl.ds(row + 2 * kgroup, step), lane : lane + LANES] = low
            rbuf[tile, pl.ds(row + 4 * kgroup, step), lane : lane + LANES] = high

        recipes = (((0, 2), (0, 2), (0, 1)), ((2, 1), (0, 1), (0, 1)))
        second_stage(
            ubuf, lbuf, tbuf, second_high, second_low, group, per, breadth, (1, 0), (1, 0), recipes, emit
        )
        for tile in range(count * breadth // 2):
            total = pick_diagonal(product(third[group], rbuf[tile]), breadth)
            for d in range(2):
                row = (tile * 2 + d) * stride
                old = jnp.where(group == 0, 0.0, obuf[row : row + breadth])
                obuf[row : row + breadth] = old + total[:, d * LANES : (d + 1) * LANES]
        return carry

    lax.fori_loop(0, third.shape[0], group_body, 0)
    for n in range(count):

        def store(a, lane, value, n=n):
            out[n, a : a + 8, lane : lane + LANES] = value

        turn_block(obuf, n * breadth * stride, breadth, store)


def spread_kernel(where, own, *refs):
    first, second_high, second_low, third, keep, send = refs[:6]
    xbuf, ubuf, lbuf, tbuf, rbuf, obuf, block = refs[6:]
    count, breadth, width = own.shape
    rows = first.shape[0] // third.shape[0]
    per = rows // breadth
    kgroup = per * breadth * breadth // LANES
    half_slots = keep.shape[0]
    keep[...] = jnp.zeros(keep.shape, F32)
    send[...] = jnp.zeros(send.shape, F32)
    tbuf[...] = jnp.zeros(tbuf.shape, BF16)
    xbuf[...] = jnp.zeros(xbuf.shape, BF16)
    stride = breadth + PAD

    def group_body(group, carry):
        top = pl.multiple_of(group * rows, 8)
        for n in range(count):
            fill(xbuf, 0, own[n])
            for g in range(2):
                place(ubuf, g, n, product(first[pl.ds(top, rows), (1 + g) * LANES : (2 + g) * LANES], xbuf[...]))

        def emit(q, pair, tile, lane, high, low):
            step = high.shape[0]
            row = pl.multiple_of(q * 3 * kgroup + pair * step, step)
            rbuf[tile, pl.ds(row, step), lane : lane + LANES] = high
            rbuf[tile, pl.ds(row + kgroup, step), lane : lane + LANES] = low
            rbuf[tile, pl.ds(row + 2 * kgroup, step), lane : lane + LANES] = high

        recipes = (((1, 1), (0, 1), (0, 1)), ((0, 1), (0, 1), (0, 2)))
        second_stage(
            ubuf, lbuf, tbuf, second_high, second_low, group, per, breadth, (1, 2), (0, 1), recipes, emit
        )
        for tile in range(count * breadth // 2):
            for q in range(3):
                wide = product(third[group, 1 if q == 1 else 0], rbuf[tile, q * 3 * kgroup : (q + 1) * 3 * kgroup])
                total = pick_diagonal(wide, breadth)
                for d in range(2):
                    row = (tile * 2 + d) * stride
                    old = jnp.where(group == 0, 0.0, obuf[q, row : row + breadth])
                    obuf[q, row : row + breadth] = old + total[:, d * LANES : (d + 1) * LANES]
        return carry

    lax.fori_loop(0, third.shape[0], group_body, 0)
    for n in range(count):
        for q in range(3):

            def store(a, lane, value):
                block[a : a + 8, lane : lane + LANES] = value

            turn_block(obuf.at[q], n * breadth * stride, breadth, store)
            slot = where[n, q]

            @pl.when((slot >= 0) & (slot < half_slots))
            def _(slot=slot):
                keep[slot] = keep[slot] + block[...]

            @pl.when(slot >= half_slots)
            def _(slot=slot):
                send[slot - half_slots] = send[slot - half_slots] + block[...]


def stage_scratch(volumes, spots, recipes, count, breadth, per):
    hi_count = breadth * breadth // LANES
    return [
        pltpu.VMEM((volumes, count, hi_count, per * breadth + PAD, LANES), F32),
        pltpu.VMEM((2, count * breadth * hi_count, volumes * 2 * LANES), BF16),
        pltpu.VMEM((2, spots[0] * 2 * LANES, spots[1] * 2 * LANES), BF16),
        pltpu.VMEM((count * breadth // 2, recipes * 3 * per * hi_count, 2 * LANES), BF16),
    ]


def cost(count, breadth, per, units):
    return pl.CostEstimate(flops=units * per * 2 * count * breadth**4 * 200, transcendentals=0, bytes_accessed=1 << 22)


def stage_call(kernel, name, where, own, extra, weights, third, groups, out_shapes, scratch, units):
    first, second_high, second_low = weights
    breadth = own.shape[1]
    terms = second_high.shape[0]
    per = terms // groups
    return pl.pallas_call(
        kernel,
        out_shape=out_shapes,
        in_specs=[pl.BlockSpec(memory_space=pltpu.SMEM), pl.BlockSpec(memory_space=pltpu.VMEM)]
        + [pl.BlockSpec(memory_space=pl.ANY)] * len(extra)
        + [pl.BlockSpec(memory_space=pltpu.VMEM)] * 4,
        out_specs=[pl.BlockSpec(memory_space=pltpu.VMEM)] * len(out_shapes),
        scratch_shapes=scratch,
        compiler_params=pltpu.CompilerParams(vmem_limit_bytes=36 << 20),
        cost_estimate=cost(own.shape[0], breadth, terms, units),
        name=name,
    )(where, own, *extra, first, second_high, second_low, third)


def merge_call(where, own, parts, weights, third, groups):
    count, breadth, width = own.shape
    per = weights[1].shape[0] // groups
    scratch = stage_scratch(3, (2, 1), 2, count, breadth, per)
    scratch = (
        [pltpu.VMEM((count * 3, breadth, width), F32), pltpu.VMEM((2 * LANES, width), BF16)]
        + scratch
        + [pltpu.VMEM((count * breadth * (breadth + PAD), LANES), F32), pltpu.SemaphoreType.DMA((count * 3,))]
    )
    return stage_call(
        functools.partial(merge_kernel, parts=len(parts)),
        "merge",
        where,
        own,
        list(parts),
        weights,
        third,
        groups,
        [jax.ShapeDtypeStruct(own.shape, F32)],
        scratch,
        9,
    )[0]


def spread_call(where, own, slots, weights, third, groups):
    count, breadth, width = own.shape
    per = weights[1].shape[0] // groups
    scratch = stage_scratch(2, (1, 2), 3, count, breadth, per)
    scratch = (
        [pltpu.VMEM((LANES, width), BF16)]
        + scratch
        + [pltpu.VMEM((3, count * breadth * (breadth + PAD), LANES), F32), pltpu.VMEM((breadth, width), F32)]
    )
    shape = jax.ShapeDtypeStruct((slots // 2, breadth, width), F32)
    return stage_call(
        spread_kernel,
        "spread",
        where,
        own,
        [],
        weights,
        third,
        groups,
        [shape, shape],
        scratch,
        8,
    )


def to_row(column):
    size = column.shape[0]
    diagonal = iota((size, size), 0) == iota((size, size), 1)
    return jnp.sum(jnp.where(diagonal, column, 0.0), axis=0, keepdims=True)


def to_column(row):
    size = row.shape[1]
    diagonal = iota((size, size), 0) == iota((size, size), 1)
    return jnp.sum(jnp.where(diagonal, row, 0.0), axis=1, keepdims=True)


def place_row(slot_row, row, runs, run_size, capacity):
    held = slot_row.shape[1]
    run_row = jnp.zeros(slot_row.shape, F32)
    for r in range(1, runs):
        run_row = run_row + jnp.where(slot_row >= r * run_size, 1.0, 0.0)
    same = to_column(run_row) == run_row
    earlier = iota((held, held), 0) < iota((held, held), 1)
    before = jnp.sum(jnp.where(same & earlier, 1.0, 0.0), axis=0, keepdims=True)
    far_row = run_row - row.astype(F32)
    far_row = jnp.where(far_row < 0.0, far_row + runs, far_row)
    return far_row * capacity + before


def pack_kernel(row, slot_row, fine, *refs, run_size):
    outs, stack = refs[:-1], refs[-1]
    held, volume = fine.shape
    runs = len(outs)
    capacity = outs[0].shape[0]
    places = runs * capacity
    slots = slot_row[...]
    place = place_row(slots, row[0], runs, run_size, capacity)
    hit = iota((places, held), 0).astype(F32) == place
    ids = jnp.sum(jnp.where(hit, slots.astype(F32) + 1.0, 0.0), axis=1, keepdims=True)
    ids = jnp.broadcast_to(ids, (places, LANES))
    one = jnp.where(hit, 1.0, 0.0).astype(BF16)
    rest = fine[...]
    for part in range(2):
        head = rest.astype(BF16)
        stack[part * held : (part + 1) * held] = head
        rest = rest - head.astype(F32)
    packed = product(jnp.concatenate([one] * 2, axis=1), stack[...])
    for k in range(runs):
        outs[k][:, :volume] = packed[k * capacity : (k + 1) * capacity]
        outs[k][:, volume:] = ids[k * capacity : (k + 1) * capacity]


def unpack_kernel(row, slot_row, *refs, run_size):
    backs = refs[:-2]
    out, stack = refs[-2:]
    held, volume = out.shape
    runs = len(backs)
    capacity = backs[0].shape[0]
    places = runs * capacity
    place = to_column(place_row(slot_row[...], row[0], runs, run_size, capacity))
    hit = iota((held, places), 1).astype(F32) == place
    one = jnp.where(hit, 1.0, 0.0).astype(BF16)
    rest = jnp.concatenate([back[...] for back in backs], axis=0)
    for part in range(2):
        head = rest.astype(BF16)
        stack[part * places : (part + 1) * places] = head
        rest = rest - head.astype(F32)
    out[...] = product(jnp.concatenate([one] * 2, axis=1), stack[...])


def child_code(ids, held):
    at = ids - 1.0
    return jnp.where(at < 0.0, -1.0, at - held * jnp.floor(at / held))


def row_code(index, count):
    inner = index & 7
    code = (inner >> 1) * 8 + (inner & 1) * 4 + (index >> 3)
    return jnp.where(inner < 2 * count, code.astype(F32), -2.0)


def child_rows(filter_matrix, count):
    breadth = filter_matrix.shape[0]
    half = breadth // 2
    lane = iota((breadth, half * 8), 1)
    inner = lane & 7
    hot = iota((breadth, half * 8), 0) == (inner & 1) * half + (lane >> 3)
    spread = exact_expand(filter_matrix, hot)
    return jnp.concatenate([jnp.where(inner >> 1 == n, spread, 0.0) for n in range(count)], axis=0)


def triple_lanes(x):
    high, low = split(x)
    return jnp.concatenate([high, high, low], axis=1)


def filter_kernel(filter_ref, *refs, count):
    got = refs[:-6]
    out, ids, stack, lines, cross, weave = refs[-6:]
    runs = len(got)
    capacity, volume = got[0].shape
    volume = volume - LANES
    places = runs * capacity
    breadth = filter_ref.shape[0]
    half = breadth // 2
    width = out.shape[2]
    face = width // 4
    span = volume // face
    lo_count = LANES // breadth
    hi_count = breadth // lo_count
    matrix = filter_ref[...]
    turned = matrix.T
    lane = iota((breadth, width), 1)
    outer = lane // breadth
    across_z = exact_expand(turned, iota((breadth, width), 0) == lane % breadth)
    across_y = exact_expand(turned, iota((breadth, width), 0) == (outer % lo_count) * hi_count + outer // lo_count)
    for g in range(4):
        zs = across_z[(g & 1) * half : (g & 1) * half + half]
        for j in range(half):
            row = (g >> 1) * half + j
            high, low = split(zs * across_y[row : row + 1])
            at = (g * half + j) * half
            cross[0, at : at + half] = high
            cross[1, at : at + half] = low
    joined = jnp.concatenate([piece[...] for piece in got], axis=0)
    ids[...] = jnp.concatenate([got[(runs - k) % runs][:, volume:] for k in range(runs)], axis=0)
    code = to_row(child_code(joined[:, volume : volume + 1], 8 * count))
    hit = row_code(iota((32, places), 0), count) == code
    one = jnp.where(hit, 1.0, 0.0).astype(BF16)
    high, low = split(joined[:, :volume])
    stack[:places] = high
    stack[places:] = low
    boxes = product(jnp.concatenate([one, one], axis=1), stack[...])
    for g in range(4):
        for i in range(0, span, 2):
            both = jnp.concatenate(
                [boxes[g * 8 : g * 8 + 8, (i + d) * face : (i + d + 1) * face] for d in range(2)], axis=0
            )
            high, low = split(both)
            lines[0, i * 8 : i * 8 + 16, g * face : (g + 1) * face] = high
            lines[1, i * 8 : i * 8 + 16, g * face : (g + 1) * face] = low
    total = product(lines[0], cross[0]) + product(lines[1], cross[0]) + product(lines[0], cross[1])
    high, low = split(total)
    size = total.shape[0]
    weave[:size] = high
    weave[size : 2 * size] = low
    weave[2 * size :] = high
    result = product(triple_lanes(child_rows(matrix, count)), weave[...])
    for n in range(count):
        out[n] = result[n * breadth : (n + 1) * breadth]


def unfilter_kernel(filter_ref, ids, *refs, count, runs):
    outs = refs[-3 - runs : -3]
    applied = refs[: -3 - runs]
    weave, cross, stack = refs[-3:]
    capacity, volume = outs[0].shape
    places = runs * capacity
    breadth = filter_ref.shape[0]
    half = breadth // 2
    width = applied[0].shape[2]
    face = width // 4
    size = count * breadth
    matrix = filter_ref[...]
    lane = iota((breadth, width), 1)
    octant = lane // face
    across_c = exact_expand(matrix, iota((breadth, width), 0) == octant % 2 * half + lane % half)
    across_b = exact_expand(matrix, iota((breadth, width), 0) == octant // 2 * half + lane // half % half)
    for b in range(breadth):
        high, low = split(across_c * across_b[b : b + 1])
        cross[0, b * breadth : (b + 1) * breadth] = high
        cross[1, b * breadth : (b + 1) * breadth] = low
    for n in range(count):
        total = applied[0][n]
        for piece in applied[1:]:
            total = total + piece[n]
        high, low = split(total)
        at = n * breadth
        weave[at : at + breadth] = high
        weave[size + at : size + at + breadth] = low
        weave[2 * size + at : 2 * size + at + breadth] = high
    lines = product(triple_lanes(child_rows(matrix, count).T), weave[...])
    high, low = split(lines)
    total = product(high, cross[0]) + product(low, cross[0]) + product(high, cross[1])
    for g in range(0, 4, 2):
        for i in range(total.shape[0] // 8):
            both = jnp.concatenate(
                [total[i * 8 : i * 8 + 8, (g + d) * face : (g + d + 1) * face] for d in range(2)], axis=0
            )
            high, low = split(both)
            stack[g * 8 : g * 8 + 16, i * face : (i + 1) * face] = high
            stack[32 + g * 8 : 32 + g * 8 + 16, i * face : (i + 1) * face] = low
    code = child_code(ids[:, :1], 8 * count)
    hit = row_code(iota((places, 32), 1), count) == code
    one = jnp.where(hit, 1.0, 0.0).astype(BF16)
    packed = product(jnp.concatenate([one, one], axis=1), stack[...])
    for k in range(runs):
        outs[k][...] = packed[k * capacity : (k + 1) * capacity]


def add_kernel(keep, came, *outs):
    count = outs[0].shape[0]
    for i, out in enumerate(outs):
        out[...] = keep[i * count : (i + 1) * count] + came[i * count : (i + 1) * count]


def vmem_call(kernel, out_shape, scratch, name, in_specs=None, room=14, outputs=1, **settings):
    extra = {} if in_specs is None else dict(in_specs=in_specs)
    if isinstance(out_shape, list):
        shapes = [jax.ShapeDtypeStruct(shape, F32) for shape in out_shape]
    else:
        shapes = jax.ShapeDtypeStruct(out_shape, F32)
    if outputs > 1:
        shapes = [shapes] * outputs
    return pl.pallas_call(
        functools.partial(kernel, **settings),
        out_shape=shapes,
        scratch_shapes=[pltpu.VMEM(shape, dtype) for shape, dtype in scratch],
        compiler_params=pltpu.CompilerParams(vmem_limit_bytes=room << 20),
        name=name,
        **extra,
    )


def moved(array, row_step, bit):
    rows = lax.axis_size("row")
    cols = lax.axis_size("col")
    pairs = [
        (r * cols + c, (r + row_step) % rows * cols + (c ^ bit)) for r in range(rows) for c in range(cols)
    ]
    return lax.ppermute(array, ("row", "col"), pairs)


def local(fine_coeffs, fine_slot, neighbours, filter_matrix, kernel_ops):
    breadth = filter_matrix.shape[0]
    terms = kernel_ops.shape[0]
    runs = lax.axis_size("row")
    cols = lax.axis_size("col")
    held, volume = fine_coeffs.shape
    par_row = neighbours.shape[0]
    count = held // 8
    capacity = 2 * (held // runs)
    places = runs * capacity
    width = breadth * breadth
    hi_count = width // LANES
    groups = 2
    per = terms // groups
    uppers = range(0, cols, 2)

    slot_row = fine_slot.reshape(1, held)
    routing = dict(run_size=8 * par_row)
    row = jnp.full((1,), lax.axis_index("row"), jnp.int32)
    scalar = pl.BlockSpec(memory_space=pltpu.SMEM)
    plain = pl.BlockSpec(memory_space=pltpu.VMEM)
    sent = vmem_call(
        pack_kernel,
        (capacity, volume + LANES),
        [((2 * held, volume), BF16)],
        "pack",
        in_specs=[scalar, plain, plain],
        room=ROOM,
        outputs=runs,
        **routing,
    )(row, slot_row, fine_coeffs)
    got = [sent[0]] + [moved(sent[k], k, 0) for k in range(1, runs)]

    first, second_high, second_low, merge_third, spread_third = pl.pallas_call(
        functools.partial(prepare_kernel, groups=groups),
        out_shape=[
            jax.ShapeDtypeStruct((terms * breadth, 3 * LANES), BF16),
            jax.ShapeDtypeStruct((terms, 3, breadth, LANES), BF16),
            jax.ShapeDtypeStruct((terms, 3, breadth, LANES), BF16),
            jax.ShapeDtypeStruct((groups, LANES, 6 * per * hi_count), BF16),
            jax.ShapeDtypeStruct((groups, 2, LANES, 3 * per * hi_count), BF16),
        ],
        scratch_shapes=[pltpu.VMEM(((9 * terms + 8) * (breadth + PAD), LANES), F32)],
        compiler_params=pltpu.CompilerParams(vmem_limit_bytes=PREP << 20),
        name="prepare",
    )(jnp.transpose(kernel_ops, (1, 2, 0, 3)))
    weights = (first, second_high, second_low)

    col_index = lax.axis_index("col")
    mine = lax.dynamic_slice_in_dim(neighbours, col_index * count, count, 0)[:, ::2]
    within = mine % par_row
    relation = (within // count) ^ col_index
    spot = (relation % 2) * (len(uppers) * count) + relation // 2 * count + within % count
    where = jnp.where(mine >= 0, spot, -1)

    filtered, ids = vmem_call(
        filter_kernel,
        [(count, breadth, width), (places, LANES)],
        [
            ((2 * places, volume), BF16),
            ((2, breadth * 4, width), BF16),
            ((2, width, width), BF16),
            ((12 * breadth, width), BF16),
        ],
        "filter",
        count=count,
    )(filter_matrix, *got)

    parts = [moved(filtered, -1, u) for u in reversed(uppers)][::-1]
    keep, send = spread_call(where, filtered, par_row, weights, spread_third, groups)
    parts, keep, send = lax.optimization_barrier((parts, keep, send))
    parts = parts + [moved(part, 0, 1) for part in parts]
    came = moved(send, 0, 1)

    sums = vmem_call(
        add_kernel, [(count, breadth, width)] * len(uppers), [], "add", in_specs=[plain] * 2, room=8
    )(keep, came)
    terms_out = [moved(sums[u // 2], 1, u) for u in reversed(uppers)]
    pieces = [merge_call(where, filtered, parts, weights, merge_third, groups)] + terms_out
    results = vmem_call(
        unfilter_kernel,
        (capacity, volume),
        [
            ((3 * count * breadth, width), BF16),
            ((2, width, width), BF16),
            ((64, volume), BF16),
        ],
        "unfilter",
        in_specs=[plain] * (2 + len(pieces)),
        outputs=runs,
        count=count,
        runs=runs,
    )(filter_matrix, ids, *pieces)
    backs = [results[0]] + [moved(results[runs - j], -j, 0) for j in range(1, runs)]
    return vmem_call(
        unpack_kernel,
        (held, volume),
        [((2 * places, volume), BF16)],
        "unpack",
        in_specs=[scalar, plain] + [plain] * runs,
        **routing,
    )(row, slot_row, *backs)


def solution(mesh):
    in_specs = (P(("row", "col"), None), P(("row", "col")), P("row", None), P(), P())
    out_specs = P(("row", "col"), None)
    return jax.shard_map(local, mesh=mesh, in_specs=in_specs, out_specs=out_specs, check_vma=False)
```
